32 devices in a mesh: prow: 8 (over y, x, core), pcol: 4 (over z).
Axes of the slice: x: 2, y: 2, z: 4, core: 2. Of those that a mesh axis runs over, the one named last changes fastest.
Arguments:
- panel: float32 [32768, 512], P('prow', 'pcol'), may hold values from -0.08 to 0.08
- slab: float32 [32768, 2048], P('prow', 'pcol'), may hold values from -6 to 6
- pivots: int32 [512], replicated, may hold values from 512 to 32767, as said below
- diag_inverse: float32 [512, 512], replicated, as said below
Outputs:
- updated: float32 [32768, 2048], P('prow', 'pcol')
The draws below stay inside these ranges and needn't reach their ends.
Inputs may be any that keep to these rules, and one draw needn't show every extreme that they name: `pivots`: 512 distinct row indices, each below the diagonal block; their owners along prow are uneven. `diag_inverse`: unit lower triangular.
All inputs are finite; a program needn't handle non-finite values.
Results may differ from the reference program's by a relative error of at most 0.000053.
Values sent between devices are 32-bit elements; how exact they have to be, the bound alone decides.
No kernel may reach another device: no remote copies, remote signals or barrier semaphores. Data moves between devices by JAX's collectives and lax.ppermute only.
A program may use at most 128 MiB of HBM per device.

```python
import jax
import jax.numpy as jnp
from jax import lax

NB = 512
SLAB = 2048
ROWS_DEV = 4096
ROWS = 32768


def draw_pivots(key, part):
    first_key, second_key = jax.random.split(jax.random.fold_in(key, 11))
    owners = ROWS // ROWS_DEV
    levels = jax.random.randint(first_key, (owners,), 0, 4)
    candidate = jnp.arange(NB, ROWS, dtype=jnp.int32)
    owner_of = candidate // ROWS_DEV
    raw_score = jax.random.randint(second_key, (ROWS - NB,), 0, 1024) + levels[owner_of] * 1024
    score = raw_score * ROWS + (ROWS - 1 - candidate)
    forced = (candidate == NB) | (candidate == ROWS - 1) | (candidate == ROWS_DEV) | (candidate == owners // 2 * ROWS_DEV)
    score = jnp.where(forced, 2 ** 30, score)
    top_values, positions = lax.top_k(score, NB)
    return candidate[positions].astype(jnp.int32)


def draw_diag_inverse(key, part):
    row_index = jnp.arange(NB)[:, None]
    col_index = jnp.arange(NB)[None, :]
    values = jax.random.normal(jax.random.fold_in(key, 5), (NB, NB), jnp.float32)
    lower = jnp.where(row_index > col_index, values * NB ** (-0.5), 0.0)
    return (lower + jnp.where(row_index == col_index, 1.0, 0.0)).astype(jnp.float32)


def steps_of(key, extent, cuts, smallest, high):
    gain, own = 1.0, jax.random.fold_in(key, 6)
    for position, blocks in cuts:
        heights = jnp.exp(jax.random.uniform(jax.random.fold_in(own, position), (blocks,), jnp.float32, smallest / len(cuts), high / len(cuts)))
        gain = gain * jnp.repeat(heights, extent[position] // blocks).reshape([-1 if axis == position else 1 for axis in range(len(extent))])
    return gain


def centred(stream_key, dims, deviation, most, shards=(), kind=jnp.bfloat16):
    entries = jax.random.normal(stream_key, dims, jnp.float32) * deviation
    if len(shards) > 0:
        entries = steps_of(stream_key, dims, shards, -0.22, 0.18) * entries
    return jnp.clip(entries, min=-most, max=most).astype(kind)


def setup_inputs(seed: int = 0) -> dict:
    arg_keys = jax.random.split(jax.random.key(seed), 5)
    panel = jnp.clip(jax.random.uniform(arg_keys[0], (ROWS, NB), jnp.float32, -0.08, 0.08) * steps_of(arg_keys[0], (ROWS, NB), ((0, 8), (1, 4)), -0.4, 0.0), -0.08, 0.08)
    slab = centred(arg_keys[1], (ROWS, SLAB), 1.0, 6.0, ((0, 8), (1, 4)), jnp.float32)
    pivots = draw_pivots(jax.random.fold_in(arg_keys[4], 71), 0)
    diag_inverse = draw_diag_inverse(jax.random.fold_in(arg_keys[4], 71), 0)
    return dict(panel=panel, slab=slab, pivots=pivots, diag_inverse=diag_inverse)


def reference(panel, slab, pivots, diag_inverse):
    picked = slab[pivots]
    swapped = slab.at[pivots].set(slab[:NB])
    upper = jnp.dot(diag_inverse, picked, precision=lax.Precision.HIGHEST, preferred_element_type=jnp.float32)
    product = jnp.dot(panel, upper, precision=lax.Precision.HIGHEST, preferred_element_type=jnp.float32)
    updated = swapped - product
    return updated.at[:NB].set(upper)
```

```python
import jax
import jax.numpy as jnp
from jax import lax
from jax.experimental import pallas as pl
from jax.experimental.pallas import tpu as pltpu
from jax.sharding import PartitionSpec as P

SWAP = [(0, 1), (1, 0), (2, 3), (3, 2)]
ACROSS = [(0, 2), (1, 3), (2, 0), (3, 1)]
MIDDLE = [(1, 2), (2, 1)]
ENDS = [(2, 3), (1, 0)]
PIECES = (12, 4)
TILE = 512
VMEM_LIMIT = 60 << 20
SMALL = pl.CostEstimate(flops=0, bytes_accessed=0, transcendentals=0)


def split(x):
    high = x.astype(jnp.bfloat16)
    low = (x - high.astype(jnp.float32)).astype(jnp.bfloat16)
    return high, low


def product(left, right):
    left_high, left_low = split(left)
    right_high, right_low = split(right)

    def dot(a, b):
        return jnp.dot(a, b, preferred_element_type=jnp.float32)

    return dot(left_high, right_high) + (dot(left_high, right_low) + dot(left_low, right_high))


def pick_kernel(info, pivots, slab, send, keep, rows, sem):
    copy = pltpu.make_async_copy(slab, rows, sem)
    copy.start()
    place = info[1]
    count = rows.shape[0]
    block = send.shape[0]
    first = place * count
    send[...] = jnp.zeros_like(send)
    keep[...] = jnp.zeros_like(keep)
    copy.wait()

    def fill(picked, top):
        @pl.when(place == 0)
        def _():
            top[...] = rows[:block, :]

        @pl.loop(0, block)
        def _(k):
            row = pivots[k] - first

            @pl.when((row >= 0) & (row < count))
            def _():
                picked[pl.ds(k, 1), :] = rows[pl.ds(row, 1), :]

    @pl.when(place % 2 == 0)
    def _():
        fill(keep, send)

    @pl.when(place % 2 == 1)
    def _():
        fill(send, keep)


def pick(info, pivots, slab, block):
    columns = slab.shape[1]
    shape = jax.ShapeDtypeStruct((block, columns), slab.dtype)
    return pl.pallas_call(
        pick_kernel,
        out_shape=(shape, shape),
        grid_spec=pltpu.PrefetchScalarGridSpec(
            num_scalar_prefetch=2,
            grid=(),
            in_specs=[pl.BlockSpec(memory_space=pl.ANY)],
            out_specs=[pl.BlockSpec(memory_space=pltpu.VMEM)] * 2,
            scratch_shapes=[pltpu.VMEM(slab.shape, slab.dtype), pltpu.SemaphoreType.DMA],
        ),
        compiler_params=pltpu.CompilerParams(vmem_limit_bytes=VMEM_LIMIT),
        cost_estimate=SMALL,
        name="pick",
    )(info, pivots, slab)


def swap_kernel(tile, info, pivots, slab, total, other, own, inverse, out, upper, rows, in_sem, out_sem):
    copy = pltpu.make_async_copy(slab, rows, in_sem)
    copy.start()
    column, place = info[0], info[1]
    count, width = own.shape
    block = upper.shape[0]
    first = place * count

    def fill(picked, old_top):
        upper[...] = product(inverse[...], picked[...])
        copy.wait()

        @pl.loop(0, block)
        def _(k):
            row = pivots[k] - first

            @pl.when((row >= 0) & (row < count))
            def _():
                rows[pl.ds(row, 1), :] = old_top[pl.ds(k, 1), :]

    @pl.when(place % 2 == 0)
    def _():
        fill(total, other)

    @pl.when(place % 2 == 1)
    def _():
        fill(other, total)

    mine = upper[pl.ds(pl.multiple_of(column * width, width), width), :]

    @pl.loop(0, count // tile)
    def _(t):
        part = pl.ds(pl.multiple_of(t * tile, tile), tile)
        rows[part, :] = rows[part, :] - product(own[part, :], mine)

        @pl.when((place == 0) & (t < block // tile))
        def _():
            rows[part, :] = upper[pl.ds(pl.multiple_of(jnp.minimum(t * tile, block - tile), tile), tile), :]

        pltpu.make_async_copy(rows.at[part, :], out.at[part, :], out_sem).start()

    pltpu.make_async_copy(rows, out, out_sem).wait()


def swap(info, pivots, slab, total, other, own, inverse):
    block = inverse.shape[0]
    return pl.pallas_call(
        lambda *refs: swap_kernel(min(TILE, block), *refs),
        out_shape=(
            jax.ShapeDtypeStruct(slab.shape, slab.dtype),
            jax.ShapeDtypeStruct((block, slab.shape[1]), slab.dtype),
        ),
        grid_spec=pltpu.PrefetchScalarGridSpec(
            num_scalar_prefetch=2,
            grid=(),
            in_specs=[pl.BlockSpec(memory_space=pl.ANY)] + [pl.BlockSpec(memory_space=pltpu.VMEM)] * 4,
            out_specs=(pl.BlockSpec(memory_space=pl.ANY), pl.BlockSpec(memory_space=pltpu.VMEM)),
            scratch_shapes=[
                pltpu.VMEM(slab.shape, slab.dtype),
                pltpu.SemaphoreType.DMA,
                pltpu.SemaphoreType.DMA,
            ],
        ),
        compiler_params=pltpu.CompilerParams(vmem_limit_bytes=VMEM_LIMIT),
        cost_estimate=SMALL,
        name="swap",
    )(info, pivots, slab, total, other, own, inverse)


def update_kernel(first_row, block, shards, info, base, *refs):
    *blocks, out = refs
    panels, uppers = blocks[: len(blocks) - len(shards)], blocks[len(blocks) - len(shards) :]
    tile = base.shape[0]
    panels = [panel[...] for panel in panels]
    if len(panels) > len(uppers):
        panels = [panels[0] + panels[1]]
    delta = product(panels[0], uppers[0][...])
    for panel, upper in zip(panels[1:], uppers[1:]):
        delta += product(panel, upper[...])
    if first_row < block:
        start = first_row + pl.program_id(0) * tile
        delta = jnp.where((info[1] == 0) & (start < block), 0.0, delta)
    out[...] = base[...] - delta


def update(info, base, panels, shards, upper, first_row, count):
    columns = base.shape[1]
    width = panels[0].shape[1]
    block = upper.shape[0]
    tile = min(TILE, count)
    shift = first_row // tile
    here = lambda i, info: (i + shift, 0)
    plain = lambda i, info: (i, 0)
    return pl.pallas_call(
        lambda *refs: update_kernel(first_row, block, shards, *refs),
        out_shape=jax.ShapeDtypeStruct(base.shape, base.dtype),
        grid_spec=pltpu.PrefetchScalarGridSpec(
            num_scalar_prefetch=1,
            grid=(count // tile,),
            in_specs=[pl.BlockSpec((tile, columns), here)]
            + [pl.BlockSpec((tile, width), here if p.shape[0] != count else plain) for p in panels]
            + [pl.BlockSpec((width, columns), lambda i, info, s=s: (info[0] ^ s, 0)) for s in shards],
            out_specs=pl.BlockSpec((tile, columns), here),
        ),
        input_output_aliases={1: 0},
        compiler_params=pltpu.CompilerParams(vmem_limit_bytes=VMEM_LIMIT),
        cost_estimate=SMALL,
        name="update",
    )(info, base, *panels, *([upper] * len(shards)))


def exchange(value, bit, count):
    return lax.ppermute(value, "prow", [(i, i ^ (1 << bit)) for i in range(count)])


def solution(mesh):
    row_parts, column_parts = mesh.shape["prow"], mesh.shape["pcol"]
    bits = row_parts.bit_length() - 1
    if column_parts != 4 or row_parts != 1 << bits or bits < 1:
        raise ValueError("unsupported mesh")

    def shards(panel, slab, pivots, diag_inverse):
        rows_here = slab.shape[0]
        block = diag_inverse.shape[0]
        place = lax.axis_index("prow")
        column = lax.axis_index("pcol")
        info = jnp.stack([column, place]).astype(jnp.int32)

        starts, pieces, at = [], [], 0
        for part in PIECES:
            size = rows_here * part // sum(PIECES)
            starts.append(at)
            pieces.append(panel[at : at + size])
            at += size
        near = lax.ppermute(panel, "pcol", SWAP)
        across = [lax.ppermute(piece, "pcol", ACROSS) for piece in pieces]

        def gather_rows(slab, pivots):
            send, keep = pick(info, pivots, slab, block)
            total = keep + exchange(send, 0, row_parts)
            for bit in range(1, bits):
                total = total + exchange(total, bit, row_parts)
            other = exchange(total, 0, row_parts)
            return total, other

        def no_rows(slab, pivots):
            return slab[:block], slab[:block]

        total, other = lax.cond(pivots[0] >= 0, gather_rows, no_rows, slab, pivots)
        across, _ = lax.optimization_barrier((across, total))
        result, upper = swap(info, pivots, slab, total, other, panel, diag_inverse)

        ends = [lax.ppermute(piece, "pcol", ENDS) for piece in across]
        later, near = lax.optimization_barrier((pieces, near))
        middle = [lax.ppermute(piece, "pcol", MIDDLE) for piece in later]
        for start, piece in zip(starts, across):
            result = update(info, result, [near, piece], (1, 2), upper, start, piece.shape[0])
        for start, end, mid in zip(starts, ends, middle):
            result = update(info, result, [end, mid], (3,), upper, start, end.shape[0])
        return result

    in_specs = (P("prow", "pcol"), P("prow", "pcol"), P(), P())
    return jax.shard_map(
        shards, mesh=mesh, in_specs=in_specs, out_specs=P("prow", "pcol"), check_vma=False
    )
```

```python
import jax
import jax.numpy as jnp
from jax import lax
from jax.experimental import pallas as pl
from jax.experimental.pallas import tpu as pltpu
from jax.sharding import PartitionSpec as P

SWAP = [(0, 1), (1, 0), (2, 3), (3, 2)]
ACROSS = [(0, 2), (1, 3), (2, 0), (3, 1)]
MIDDLE = [(1, 2), (2, 1)]
ENDS = [(2, 3), (1, 0)]
PIECES = (14, 2)
TILE = 512
LAST_TILE = 128
SMALL = pl.CostEstimate(flops=0, bytes_accessed=0, transcendentals=0)
HBM = pl.BlockSpec(memory_space=pl.ANY)
VMEM = pl.BlockSpec(memory_space=pltpu.VMEM)


def split(x):
    high = x.astype(jnp.bfloat16)
    low = (x - high.astype(jnp.float32)).astype(jnp.bfloat16)
    return high, low


def left_terms(x):
    high, low = split(x)
    return jnp.concatenate([high, high, low], axis=1)


def right_terms(x):
    high, low = split(x)
    return jnp.concatenate([high, low, high], axis=0)


def dot(a, b):
    return jnp.dot(a, b, preferred_element_type=jnp.float32)


def aligned(start, size):
    return pl.ds(pl.multiple_of(start, size), size)


def pick_kernel(info, pivots, slab, send, keep, rows, sem, top_sem):
    copy = pltpu.make_async_copy(slab, rows, sem)
    copy.start()
    place = info[1]
    count = rows.shape[0]
    block = send.shape[0]
    first = place * count

    def fill(picked, top):
        load = pltpu.make_async_copy(slab.at[pl.ds(0, block), :], top, top_sem)

        @pl.when(place == 0)
        def _():
            load.start()

        @pl.when(place != 0)
        def _():
            top[...] = jnp.zeros_like(top)

        copy.wait()

        @pl.loop(0, block // 8)
        def _(group):
            base = pl.multiple_of(group * 8, 8)
            for j in range(8):
                row = pivots[base + j] - first
                owned = (row >= 0) & (row < count)
                value = rows[pl.ds(jnp.where(owned, row, 0), 1), :]
                picked[pl.ds(base + j, 1), :] = jnp.where(owned, value, 0.0)

        @pl.when(place == 0)
        def _():
            load.wait()

    @pl.when(place % 2 == 0)
    def _():
        fill(keep, send)

    @pl.when(place % 2 == 1)
    def _():
        fill(send, keep)


def pick(info, pivots, slab, block):
    columns = slab.shape[1]
    shape = jax.ShapeDtypeStruct((block, columns), slab.dtype)
    return pl.pallas_call(
        pick_kernel,
        out_shape=(shape, shape),
        grid_spec=pltpu.PrefetchScalarGridSpec(
            num_scalar_prefetch=2,
            grid=(),
            in_specs=[HBM],
            out_specs=(VMEM, VMEM),
            scratch_shapes=[
                pltpu.VMEM(slab.shape, slab.dtype),
                pltpu.SemaphoreType.DMA,
                pltpu.SemaphoreType.DMA,
            ],
        ),
        compiler_params=pltpu.CompilerParams(vmem_limit_bytes=16 << 20),
        cost_estimate=SMALL,
        name="pick",
    )(info, pivots, slab)


def upper_kernel(width, info, total, other, inverse, upper, terms):
    block = upper.shape[0]

    def fill(picked):
        upper[...] = dot(left_terms(inverse[...]), right_terms(picked[...]))

    @pl.when(info[1] % 2 == 0)
    def _():
        fill(total)

    @pl.when(info[1] % 2 == 1)
    def _():
        fill(other)

    for shard in range(block // width):
        terms[pl.ds(shard * 3 * width, 3 * width), :] = right_terms(upper[pl.ds(shard * width, width), :])


def make_upper(info, total, other, inverse, width):
    block, columns = total.shape
    return pl.pallas_call(
        lambda *refs: upper_kernel(width, *refs),
        out_shape=(
            jax.ShapeDtypeStruct((block, columns), total.dtype),
            jax.ShapeDtypeStruct((3 * block, columns), jnp.bfloat16),
        ),
        grid_spec=pltpu.PrefetchScalarGridSpec(
            num_scalar_prefetch=1,
            grid=(),
            in_specs=[VMEM] * 3,
            out_specs=(VMEM, VMEM),
        ),
        compiler_params=pltpu.CompilerParams(vmem_limit_bytes=24 << 20),
        cost_estimate=SMALL,
        name="upper",
    )(info, total, other, inverse)


def main_kernel(tile, info, pivots, slab, total, other, own, near, *refs):
    *across, upper, terms, out, own_rows, near_rows, across_rows, sem, panel_sem = refs
    copy = pltpu.make_async_copy(slab, out, sem)
    copy.start()
    loads = [(own, own_rows), (near, near_rows)]
    at = 0
    for piece in across:
        loads.append((piece, across_rows.at[pl.ds(at, piece.shape[0]), :]))
        at += piece.shape[0]
    loads = [pltpu.make_async_copy(a, b, panel_sem.at[i]) for i, (a, b) in enumerate(loads)]
    for load in loads:
        load.start()
    column, place = info[0], info[1]
    count, width = own_rows.shape
    block = upper.shape[0]
    first = place * count
    copy.wait()

    def fill(old_top):
        @pl.loop(0, block // 8)
        def _(group):
            base = pl.multiple_of(group * 8, 8)
            for j in range(8):
                row = pivots[base + j] - first
                owned = (row >= 0) & (row < count)
                place_at = pl.ds(jnp.where(owned, row, 0), 1)
                out[place_at, :] = jnp.where(owned, old_top[pl.ds(base + j, 1), :], out[place_at, :])

    @pl.when(place % 2 == 0)
    def _():
        fill(other)

    @pl.when(place % 2 == 1)
    def _():
        fill(total)

    for load in loads:
        load.wait()

    @pl.loop(0, count // tile)
    def _(t):
        part = aligned(t * tile, tile)
        left = [left_terms(panel[part, :]) for panel in (own_rows, near_rows, across_rows)]
        right = [terms[aligned((column ^ shard) * 3 * width, 3 * width), :] for shard in range(3)]
        out[part, :] = out[part, :] - dot(jnp.concatenate(left, axis=1), jnp.concatenate(right, axis=0))

        @pl.when((place == 0) & (t < block // tile))
        def _():
            out[part, :] = upper[aligned(jnp.minimum(t * tile, block - tile), tile), :]


def main_update(info, pivots, slab, total, other, own, near, across, upper, terms):
    block = upper.shape[0]
    return pl.pallas_call(
        lambda *refs: main_kernel(min(TILE, block), *refs),
        out_shape=jax.ShapeDtypeStruct(slab.shape, slab.dtype),
        grid_spec=pltpu.PrefetchScalarGridSpec(
            num_scalar_prefetch=2,
            grid=(),
            in_specs=[HBM, VMEM, VMEM, HBM, HBM] + [HBM] * len(across) + [VMEM, VMEM],
            out_specs=VMEM,
            scratch_shapes=[pltpu.VMEM(own.shape, own.dtype)] * 3
            + [pltpu.SemaphoreType.DMA, pltpu.SemaphoreType.DMA((2 + len(across),))],
        ),
        compiler_params=pltpu.CompilerParams(vmem_limit_bytes=32 << 20),
        cost_estimate=SMALL,
        name="main_update",
    )(info, pivots, slab, total, other, own, near, *across, upper, terms)


def last_kernel(first_row, block, tile, info, base, ends, middle, terms, *refs):
    out = refs[-1]
    step = pl.program_id(0)
    part = aligned(step * tile, tile)
    delta = dot(left_terms(ends[part, :] + middle[part, :]), terms[...])
    if first_row < block:
        keep = (info[1] == 0) & (first_row + step * tile < block)
        delta = jnp.where(keep, 0.0, delta)
    out[...] = base[aligned(first_row + step * tile, tile), :] - delta


def last_update(info, base, ends, middle, terms, block, first_row, tile, done):
    columns = base.shape[1]
    count, width = ends.shape
    shift = first_row // tile
    return pl.pallas_call(
        lambda *refs: last_kernel(first_row, block, tile, *refs),
        out_shape=jax.ShapeDtypeStruct(base.shape, base.dtype),
        grid_spec=pltpu.PrefetchScalarGridSpec(
            num_scalar_prefetch=1,
            grid=(count // tile,),
            in_specs=[VMEM] * 3
            + [pl.BlockSpec((3 * width, columns), lambda i, info: (info[0] ^ 3, 0))]
            + [HBM] * len(done),
            out_specs=pl.BlockSpec((tile, columns), lambda i, info: (i + shift, 0)),
        ),
        input_output_aliases={5: 0} if done else {},
        compiler_params=pltpu.CompilerParams(vmem_limit_bytes=24 << 20),
        cost_estimate=SMALL,
        name="last_update",
    )(info, base, ends, middle, terms, *done)


def exchange(value, bit, count):
    return lax.ppermute(value, "prow", [(i, i ^ (1 << bit)) for i in range(count)])


def solution(mesh):
    row_parts, column_parts = mesh.shape["prow"], mesh.shape["pcol"]
    bits = row_parts.bit_length() - 1
    if column_parts != 4 or row_parts != 1 << bits or bits < 1:
        raise ValueError("unsupported mesh")

    def shards(panel, slab, pivots, diag_inverse):
        rows_here = slab.shape[0]
        width = panel.shape[1]
        block = diag_inverse.shape[0]
        place = lax.axis_index("prow")
        column = lax.axis_index("pcol")
        info = jnp.stack([column, place]).astype(jnp.int32)

        starts, pieces, at = [], [], 0
        for part in PIECES:
            size = rows_here * part // sum(PIECES)
            starts.append(at)
            pieces.append(panel[at : at + size])
            at += size
        near = lax.ppermute(panel, "pcol", SWAP)
        across = [lax.ppermute(piece, "pcol", ACROSS) for piece in pieces]

        def gather_rows(slab, pivots):
            send, keep = pick(info, pivots, slab, block)
            total = keep + exchange(send, 0, row_parts)
            for bit in range(1, bits):
                total = total + exchange(total, bit, row_parts)
            return total, exchange(total, 0, row_parts)

        def no_rows(slab, pivots):
            return slab[:block], slab[:block]

        total, other = lax.cond(pivots[0] >= 0, gather_rows, no_rows, slab, pivots)
        upper, terms = make_upper(info, total, other, diag_inverse, width)
        across, _ = lax.optimization_barrier((across, upper))
        ends = [lax.ppermute(piece, "pcol", ENDS) for piece in across]
        later, near = lax.optimization_barrier((pieces, near))
        middle = [lax.ppermute(piece, "pcol", MIDDLE) for piece in later]
        base = main_update(info, pivots, slab, total, other, panel, near, across, upper, terms)
        done = []
        for start, end, mid in zip(starts, ends, middle):
            tile = LAST_TILE if done else TILE
            done = [last_update(info, base, end, mid, terms, block, start, min(tile, block), done)]
        return done[0]

    in_specs = (P("prow", "pcol"), P("prow", "pcol"), P(), P())
    return jax.shard_map(
        shards, mesh=mesh, in_specs=in_specs, out_specs=P("prow", "pcol"), check_vma=False
    )
```

```python
import jax
import jax.numpy as jnp
from jax import lax
from jax.experimental import pallas as pl
from jax.experimental.pallas import tpu as pltpu
from jax.sharding import PartitionSpec as P

SWAP = [(0, 1), (1, 0), (2, 3), (3, 2)]
ACROSS = [(0, 2), (1, 3), (2, 0), (3, 1)]
MIDDLE = [(1, 2), (2, 1)]
ENDS = [(2, 3), (1, 0)]
PIECES = (7, 6, 3)
TILE = 512
LAST_TILE = 256
SMALL = pl.CostEstimate(flops=0, bytes_accessed=0, transcendentals=0)
HBM = pl.BlockSpec(memory_space=pl.ANY)
VMEM = pl.BlockSpec(memory_space=pltpu.VMEM)


def split(x):
    high = x.astype(jnp.bfloat16)
    low = (x - high.astype(jnp.float32)).astype(jnp.bfloat16)
    return high, low


def left_terms(x):
    high, low = split(x)
    return jnp.concatenate([high, high, low], axis=1)


def right_terms(x):
    high, low = split(x)
    return jnp.concatenate([high, low, high], axis=0)


def dot(a, b):
    return jnp.dot(a, b, preferred_element_type=jnp.float32)


def aligned(start, size):
    return pl.ds(pl.multiple_of(start, size), size)


def cut_kernel(spans, panel, *refs):
    outs, sem = refs[:-1], refs[-1]
    copies = [
        pltpu.make_async_copy(panel.at[pl.ds(start, size), :], out, sem.at[i])
        for i, ((start, size), out) in enumerate(zip(spans, outs))
    ]
    for copy in copies:
        copy.start()
    for copy in copies:
        copy.wait()


def cut(panel, spans):
    return pl.pallas_call(
        lambda *refs: cut_kernel(spans, *refs),
        out_shape=tuple(jax.ShapeDtypeStruct((size, panel.shape[1]), panel.dtype) for _, size in spans),
        in_specs=[HBM],
        out_specs=tuple([VMEM] * len(spans)),
        scratch_shapes=[pltpu.SemaphoreType.DMA((len(spans),))],
        compiler_params=pltpu.CompilerParams(vmem_limit_bytes=8 << 20),
        cost_estimate=SMALL,
        name="cut",
    )(panel)


def pick_kernel(info, pivots, slab, send, keep, rows, sem, top_sem):
    copy = pltpu.make_async_copy(slab, rows, sem)
    copy.start()
    place = info[1]
    count = rows.shape[0]
    block = send.shape[0]
    first = place * count

    def fill(picked, top):
        load = pltpu.make_async_copy(slab.at[pl.ds(0, block), :], top, top_sem)

        @pl.when(place == 0)
        def _():
            load.start()

        @pl.when(place != 0)
        def _():
            top[...] = jnp.zeros_like(top)

        copy.wait()

        @pl.loop(0, block // 8)
        def _(group):
            base = pl.multiple_of(group * 8, 8)
            for j in range(8):
                row = pivots[base + j] - first
                owned = (row >= 0) & (row < count)
                value = rows[pl.ds(jnp.where(owned, row, 0), 1), :]
                picked[pl.ds(base + j, 1), :] = jnp.where(owned, value, 0.0)

        @pl.when(place == 0)
        def _():
            load.wait()

    @pl.when(place % 2 == 0)
    def _():
        fill(keep, send)

    @pl.when(place % 2 == 1)
    def _():
        fill(send, keep)


def pick(info, pivots, slab, block):
    columns = slab.shape[1]
    shape = jax.ShapeDtypeStruct((block, columns), slab.dtype)
    return pl.pallas_call(
        pick_kernel,
        out_shape=(shape, shape),
        grid_spec=pltpu.PrefetchScalarGridSpec(
            num_scalar_prefetch=2,
            grid=(),
            in_specs=[HBM],
            out_specs=(VMEM, VMEM),
            scratch_shapes=[
                pltpu.VMEM(slab.shape, slab.dtype),
                pltpu.SemaphoreType.DMA,
                pltpu.SemaphoreType.DMA,
            ],
        ),
        compiler_params=pltpu.CompilerParams(vmem_limit_bytes=16 << 20),
        cost_estimate=SMALL,
        name="pick",
    )(info, pivots, slab)


def upper_kernel(width, info, total, other, inverse, upper, terms):
    block = upper.shape[0]

    def fill(picked):
        upper[...] = dot(left_terms(inverse[...]), right_terms(picked[...]))

    @pl.when(info[1] % 2 == 0)
    def _():
        fill(total)

    @pl.when(info[1] % 2 == 1)
    def _():
        fill(other)

    for shard in range(block // width):
        terms[pl.ds(shard * 3 * width, 3 * width), :] = right_terms(upper[pl.ds(shard * width, width), :])


def make_upper(info, total, other, inverse, width):
    block, columns = total.shape
    return pl.pallas_call(
        lambda *refs: upper_kernel(width, *refs),
        out_shape=(
            jax.ShapeDtypeStruct((block, columns), total.dtype),
            jax.ShapeDtypeStruct((3 * block, columns), jnp.bfloat16),
        ),
        grid_spec=pltpu.PrefetchScalarGridSpec(
            num_scalar_prefetch=1,
            grid=(),
            in_specs=[VMEM] * 3,
            out_specs=(VMEM, VMEM),
        ),
        compiler_params=pltpu.CompilerParams(vmem_limit_bytes=24 << 20),
        cost_estimate=SMALL,
        name="upper",
    )(info, total, other, inverse)


def main_kernel(tile, info, pivots, slab, total, other, own, near, *refs):
    *across, upper, terms, out, own_rows, near_rows, across_rows, sem, panel_sem = refs
    copy = pltpu.make_async_copy(slab, out, sem)
    copy.start()
    loads = [(own, own_rows), (near, near_rows)]
    at = 0
    for piece in across:
        loads.append((piece, across_rows.at[pl.ds(at, piece.shape[0]), :]))
        at += piece.shape[0]
    loads = [pltpu.make_async_copy(a, b, panel_sem.at[i]) for i, (a, b) in enumerate(loads)]
    for load in loads:
        load.start()
    column, place = info[0], info[1]
    count, width = own_rows.shape
    block = upper.shape[0]
    first = place * count
    copy.wait()

    def fill(old_top):
        @pl.loop(0, block // 8)
        def _(group):
            base = pl.multiple_of(group * 8, 8)
            for j in range(8):
                row = pivots[base + j] - first
                owned = (row >= 0) & (row < count)
                place_at = pl.ds(jnp.where(owned, row, 0), 1)
                out[place_at, :] = jnp.where(owned, old_top[pl.ds(base + j, 1), :], out[place_at, :])

    @pl.when(place % 2 == 0)
    def _():
        fill(other)

    @pl.when(place % 2 == 1)
    def _():
        fill(total)

    for load in loads:
        load.wait()

    @pl.loop(0, count // tile)
    def _(t):
        part = aligned(t * tile, tile)
        left = [left_terms(panel[part, :]) for panel in (own_rows, near_rows, across_rows)]
        right = [terms[aligned((column ^ shard) * 3 * width, 3 * width), :] for shard in range(3)]
        out[part, :] = out[part, :] - dot(jnp.concatenate(left, axis=1), jnp.concatenate(right, axis=0))

        @pl.when((place == 0) & (t < block // tile))
        def _():
            out[part, :] = upper[aligned(jnp.minimum(t * tile, block - tile), tile), :]


def main_update(info, pivots, slab, total, other, own, near, across, upper, terms):
    block = upper.shape[0]
    return pl.pallas_call(
        lambda *refs: main_kernel(min(TILE, block), *refs),
        out_shape=jax.ShapeDtypeStruct(slab.shape, slab.dtype),
        grid_spec=pltpu.PrefetchScalarGridSpec(
            num_scalar_prefetch=2,
            grid=(),
            in_specs=[HBM, VMEM, VMEM, HBM, HBM] + [HBM] * len(across) + [VMEM, VMEM],
            out_specs=VMEM,
            scratch_shapes=[pltpu.VMEM(own.shape, own.dtype)] * 3
            + [pltpu.SemaphoreType.DMA, pltpu.SemaphoreType.DMA((2 + len(across),))],
        ),
        compiler_params=pltpu.CompilerParams(vmem_limit_bytes=32 << 20),
        cost_estimate=SMALL,
        name="main_update",
    )(info, pivots, slab, total, other, own, near, *across, upper, terms)


def last_kernel(first_row, block, tile, parts, info, base, terms, *refs):
    ends, middle = refs[:parts], refs[parts]
    out, result, sem = refs[-3:]
    count, width = middle.shape
    right = terms[aligned((info[0] ^ 3) * 3 * width, 3 * width), :]
    copies = []
    at = 0
    for end in ends:
        for inner in range(0, end.shape[0], tile):
            part = pl.ds(at, tile)
            delta = dot(left_terms(end[pl.ds(inner, tile), :] + middle[part, :]), right)
            row = first_row + at
            if row < block:
                delta = jnp.where(info[1] == 0, 0.0, delta)
            result[part, :] = base[pl.ds(row, tile), :] - delta
            copies.append(pltpu.make_async_copy(result.at[part, :], out.at[pl.ds(row, tile), :], sem))
            copies[-1].start()
            at += tile
    pltpu.make_async_copy(result, out.at[pl.ds(first_row, count), :], sem).wait()


def last_update(info, base, terms, ends, middle, block, first_row, tile, done):
    columns = base.shape[1]
    count = middle.shape[0]
    return pl.pallas_call(
        lambda *refs: last_kernel(first_row, block, tile, len(ends), *refs),
        out_shape=jax.ShapeDtypeStruct(base.shape, base.dtype),
        grid_spec=pltpu.PrefetchScalarGridSpec(
            num_scalar_prefetch=1,
            grid=(),
            in_specs=[VMEM] * (3 + len(ends)) + [HBM] * len(done),
            out_specs=HBM,
            scratch_shapes=[pltpu.VMEM((count, columns), base.dtype), pltpu.SemaphoreType.DMA],
        ),
        input_output_aliases={4 + len(ends): 0} if done else {},
        compiler_params=pltpu.CompilerParams(vmem_limit_bytes=24 << 20),
        cost_estimate=SMALL,
        name="last_update",
    )(info, base, terms, *ends, middle, *done)


def exchange(value, bit, count):
    return lax.ppermute(value, "prow", [(i, i ^ (1 << bit)) for i in range(count)])


def solution(mesh):
    row_parts, column_parts = mesh.shape["prow"], mesh.shape["pcol"]
    bits = row_parts.bit_length() - 1
    if column_parts != 4 or row_parts != 1 << bits or bits < 1:
        raise ValueError("unsupported mesh")

    def shards(panel, slab, pivots, diag_inverse):
        rows_here = slab.shape[0]
        width = panel.shape[1]
        block = diag_inverse.shape[0]
        place = lax.axis_index("prow")
        column = lax.axis_index("pcol")
        info = jnp.stack([column, place]).astype(jnp.int32)

        first, second, last = (rows_here * part // sum(PIECES) for part in PIECES)
        early = first + second
        pieces = cut(panel, [(0, first), (first, second + last)])
        across = [lax.ppermute(piece, "pcol", ACROSS) for piece in pieces]
        panel, _ = lax.optimization_barrier((panel, pieces))
        near = lax.ppermute(panel, "pcol", SWAP)

        def gather_rows(slab, pivots):
            send, keep = pick(info, pivots, slab, block)
            total = keep + exchange(send, 0, row_parts)
            for bit in range(1, bits):
                total = total + exchange(total, bit, row_parts)
            return total, exchange(total, 0, row_parts)

        def no_rows(slab, pivots):
            return slab[:block], slab[:block]

        total, other = lax.cond(pivots[0] >= 0, gather_rows, no_rows, slab, pivots)
        upper, terms = make_upper(info, total, other, diag_inverse, width)
        head, later, upper = lax.optimization_barrier((across[0], panel, upper))
        most, tail = cut(later, [(0, early), (early, last)])
        ends = [lax.ppermute(piece, "pcol", ENDS) for piece in (head, across[1][:second], across[1][second:])]
        middle = lax.ppermute(most, "pcol", MIDDLE)
        tail, near = lax.optimization_barrier((tail, near))
        middle_tail = lax.ppermute(tail, "pcol", MIDDLE)
        base = main_update(info, pivots, slab, total, other, panel, near, across, upper, terms)
        result = last_update(info, base, terms, ends[:2], middle, block, 0, LAST_TILE, [])
        return last_update(info, base, terms, ends[2:], middle_tail, block, early, LAST_TILE, [result])

    in_specs = (P("prow", "pcol"), P("prow", "pcol"), P(), P())
    return jax.shard_map(
        shards, mesh=mesh, in_specs=in_specs, out_specs=P("prow", "pcol"), check_vma=False
    )
```

```python
import jax
import jax.numpy as jnp
from jax import lax
from jax.experimental import pallas as pl
from jax.experimental.pallas import tpu as pltpu
from jax.sharding import PartitionSpec as P

SWAP = [(0, 1), (1, 0), (2, 3), (3, 2)]
ACROSS = [(0, 2), (1, 3), (2, 0), (3, 1)]
MIDDLE = [(1, 2), (2, 1)]
ENDS = [(2, 3), (1, 0)]
PIECES = (15, 13, 4)
TILE = 512
LAST_TILE = 256
SMALL = pl.CostEstimate(flops=0, bytes_accessed=0, transcendentals=0)
HBM = pl.BlockSpec(memory_space=pl.ANY)
VMEM = pl.BlockSpec(memory_space=pltpu.VMEM)


def split(x):
    high = x.astype(jnp.bfloat16)
    low = (x - high.astype(jnp.float32)).astype(jnp.bfloat16)
    return high, low


def left_terms(x):
    high, low = split(x)
    return jnp.concatenate([high, high, low], axis=1)


def right_terms(x):
    high, low = split(x)
    return jnp.concatenate([high, low, high], axis=0)


def dot(a, b):
    return jnp.dot(a, b, preferred_element_type=jnp.float32)


def aligned(start, size):
    return pl.ds(pl.multiple_of(start, size), size)


def cut_kernel(spans, panel, *refs):
    outs, sem = refs[:-1], refs[-1]
    for i, ((start, size), out) in enumerate(zip(spans, outs)):
        for at in range(0, size, TILE):
            step = min(TILE, size - at)
            pltpu.make_async_copy(
                panel.at[pl.ds(start + at, step), :], out.at[pl.ds(at, step), :], sem.at[i]
            ).start()
    for i, ((start, size), out) in enumerate(zip(spans, outs)):
        pltpu.make_async_copy(panel.at[pl.ds(start, size), :], out, sem.at[i]).wait()


def cut(panel, spans):
    return pl.pallas_call(
        lambda *refs: cut_kernel(spans, *refs),
        out_shape=tuple(jax.ShapeDtypeStruct((size, panel.shape[1]), panel.dtype) for _, size in spans),
        in_specs=[pl.BlockSpec(memory_space=pltpu.HBM)],
        out_specs=tuple([HBM] * len(spans)),
        scratch_shapes=[pltpu.SemaphoreType.DMA((len(spans),))],
        compiler_params=pltpu.CompilerParams(vmem_limit_bytes=8 << 20),
        cost_estimate=SMALL,
        name="cut",
    )(pltpu.with_memory_space_constraint(panel, pltpu.HBM))


def pick_kernel(info, pivots, slab, send, keep, rows, sem, top_sem):
    copy = pltpu.make_async_copy(slab, rows, sem)
    copy.start()
    place = info[1]
    count = rows.shape[0]
    block = send.shape[0]
    first = place * count

    def fill(picked, top):
        load = pltpu.make_async_copy(slab.at[pl.ds(0, block), :], top, top_sem)

        @pl.when(place == 0)
        def _():
            load.start()

        @pl.when(place != 0)
        def _():
            top[...] = jnp.zeros_like(top)

        copy.wait()

        @pl.loop(0, block // 8)
        def _(group):
            base = pl.multiple_of(group * 8, 8)
            for j in range(8):
                row = pivots[base + j] - first
                owned = (row >= 0) & (row < count)
                value = rows[pl.ds(jnp.where(owned, row, 0), 1), :]
                picked[pl.ds(base + j, 1), :] = jnp.where(owned, value, 0.0)

        @pl.when(place == 0)
        def _():
            load.wait()

    @pl.when(place % 2 == 0)
    def _():
        fill(keep, send)

    @pl.when(place % 2 == 1)
    def _():
        fill(send, keep)


def pick(info, pivots, slab, block):
    columns = slab.shape[1]
    shape = jax.ShapeDtypeStruct((block, columns), slab.dtype)
    return pl.pallas_call(
        pick_kernel,
        out_shape=(shape, shape),
        grid_spec=pltpu.PrefetchScalarGridSpec(
            num_scalar_prefetch=2,
            grid=(),
            in_specs=[HBM],
            out_specs=(VMEM, VMEM),
            scratch_shapes=[
                pltpu.VMEM(slab.shape, slab.dtype),
                pltpu.SemaphoreType.DMA,
                pltpu.SemaphoreType.DMA,
            ],
        ),
        compiler_params=pltpu.CompilerParams(vmem_limit_bytes=16 << 20),
        cost_estimate=SMALL,
        name="pick",
    )(info, pivots, slab)


def upper_kernel(width, info, total, other, inverse, upper, terms, last_terms):
    block = upper.shape[0]

    def fill(picked):
        upper[...] = dot(left_terms(inverse[...]), right_terms(picked[...]))

    @pl.when(info[1] % 2 == 0)
    def _():
        fill(total)

    @pl.when(info[1] % 2 == 1)
    def _():
        fill(other)

    for shard in range(4):
        value = right_terms(upper[aligned((info[0] ^ shard) * width, width), :])
        if shard < 3:
            terms[pl.ds(shard * 3 * width, 3 * width), :] = value
        else:
            last_terms[...] = value


def make_upper(info, total, other, inverse, width):
    block, columns = total.shape
    return pl.pallas_call(
        lambda *refs: upper_kernel(width, *refs),
        out_shape=(
            jax.ShapeDtypeStruct((block, columns), total.dtype),
            jax.ShapeDtypeStruct((9 * width, columns), jnp.bfloat16),
            jax.ShapeDtypeStruct((3 * width, columns), jnp.bfloat16),
        ),
        grid_spec=pltpu.PrefetchScalarGridSpec(
            num_scalar_prefetch=1,
            grid=(),
            in_specs=[VMEM] * 3,
            out_specs=(VMEM, VMEM, VMEM),
        ),
        compiler_params=pltpu.CompilerParams(vmem_limit_bytes=24 << 20),
        cost_estimate=SMALL,
        name="upper",
    )(info, total, other, inverse)


def main_kernel(tile, info, pivots, slab, total, other, own, near, *refs):
    *across, upper, terms, out, own_rows, near_rows, across_rows, sem, panel_sem = refs
    copy = pltpu.make_async_copy(slab, out, sem)
    copy.start()
    loads = [(own, own_rows), (near, near_rows)]
    at = 0
    for piece in across:
        loads.append((piece, across_rows.at[pl.ds(at, piece.shape[0]), :]))
        at += piece.shape[0]
    loads = [pltpu.make_async_copy(a, b, panel_sem.at[i]) for i, (a, b) in enumerate(loads)]
    for load in loads:
        load.start()
    place = info[1]
    count = own_rows.shape[0]
    block = upper.shape[0]
    first = place * count
    copy.wait()

    def fill(old_top):
        @pl.loop(0, block // 8)
        def _(group):
            base = pl.multiple_of(group * 8, 8)
            for j in range(8):
                row = pivots[base + j] - first
                owned = (row >= 0) & (row < count)
                place_at = pl.ds(jnp.where(owned, row, 0), 1)
                out[place_at, :] = jnp.where(owned, old_top[pl.ds(base + j, 1), :], out[place_at, :])

    @pl.when(place % 2 == 0)
    def _():
        fill(other)

    @pl.when(place % 2 == 1)
    def _():
        fill(total)

    for load in loads:
        load.wait()

    @pl.loop(0, count // tile)
    def _(t):
        part = aligned(t * tile, tile)
        left = [left_terms(panel[part, :]) for panel in (own_rows, near_rows, across_rows)]
        out[part, :] = out[part, :] - dot(jnp.concatenate(left, axis=1), terms[...])

        @pl.when((place == 0) & (t < block // tile))
        def _():
            out[part, :] = upper[aligned(jnp.minimum(t * tile, block - tile), tile), :]


def main_update(info, pivots, slab, total, other, own, near, across, upper, terms):
    block = upper.shape[0]
    return pl.pallas_call(
        lambda *refs: main_kernel(min(TILE, block), *refs),
        out_shape=jax.ShapeDtypeStruct(slab.shape, slab.dtype),
        grid_spec=pltpu.PrefetchScalarGridSpec(
            num_scalar_prefetch=2,
            grid=(),
            in_specs=[HBM, VMEM, VMEM, HBM, HBM] + [HBM] * len(across) + [VMEM, VMEM],
            out_specs=VMEM,
            scratch_shapes=[pltpu.VMEM(own.shape, own.dtype)] * 3
            + [pltpu.SemaphoreType.DMA, pltpu.SemaphoreType.DMA((2 + len(across),))],
        ),
        compiler_params=pltpu.CompilerParams(vmem_limit_bytes=32 << 20),
        cost_estimate=SMALL,
        name="main_update",
    )(info, pivots, slab, total, other, own, near, *across, upper, terms)


def last_kernel(first_row, block, tile, parts, base, terms, *refs):
    ends, middle = refs[:parts], refs[parts]
    out, result, sem = refs[-3:]
    at = 0
    for end in ends:
        inner = 0
        while inner < end.shape[0]:
            size = min(tile, end.shape[0] - inner)
            part = pl.ds(at, size)
            row = first_row + at
            delta = dot(left_terms(end[pl.ds(inner, size), :] + middle[part, :]), terms[...])
            if row < block:
                delta = jnp.where(lax.axis_index("prow") == 0, 0.0, delta)
            result[part, :] = base[pl.ds(row, size), :] - delta
            pltpu.make_async_copy(result.at[part, :], out.at[pl.ds(row, size), :], sem).start()
            inner += size
            at += size
    pltpu.make_async_copy(result, out.at[pl.ds(first_row, at), :], sem).wait()


def last_update(base, terms, ends, middle, block, first_row, done):
    columns = base.shape[1]
    count = middle.shape[0]
    return pl.pallas_call(
        lambda *refs: last_kernel(first_row, block, min(LAST_TILE, block), len(ends), *refs),
        out_shape=jax.ShapeDtypeStruct(base.shape, base.dtype),
        in_specs=[VMEM] * (3 + len(ends)) + [HBM] * len(done),
        out_specs=HBM,
        scratch_shapes=[pltpu.VMEM((count, columns), base.dtype), pltpu.SemaphoreType.DMA],
        input_output_aliases={3 + len(ends): 0} if done else {},
        compiler_params=pltpu.CompilerParams(vmem_limit_bytes=24 << 20),
        cost_estimate=SMALL,
        name="last_update",
    )(base, terms, *ends, middle, *done)


def exchange(value, bit, count):
    return lax.ppermute(value, "prow", [(i, i ^ (1 << bit)) for i in range(count)])


def solution(mesh):
    row_parts, column_parts = mesh.shape["prow"], mesh.shape["pcol"]
    bits = row_parts.bit_length() - 1
    if column_parts != 4 or row_parts != 1 << bits or bits < 1:
        raise ValueError("unsupported mesh")

    def shards(panel, slab, pivots, diag_inverse):
        rows_here = slab.shape[0]
        width = panel.shape[1]
        block = diag_inverse.shape[0]
        place = lax.axis_index("prow")
        column = lax.axis_index("pcol")
        info = jnp.stack([column, place]).astype(jnp.int32)

        first, second, last = (rows_here * part // sum(PIECES) for part in PIECES)
        early = first + second
        near = lax.ppermute(panel, "pcol", SWAP)
        pieces = cut(panel, [(0, first), (first, second + last)])
        across = [lax.ppermute(piece, "pcol", ACROSS) for piece in pieces]

        def gather_rows(slab, pivots):
            send, keep = pick(info, pivots, slab, block)
            total = keep + exchange(send, 0, row_parts)
            for bit in range(1, bits):
                total = total + exchange(total, bit, row_parts)
            return total, exchange(total, 0, row_parts)

        def no_rows(slab, pivots):
            return slab[:block], slab[:block]

        total, other = lax.cond(pivots[0] >= 0, gather_rows, no_rows, slab, pivots)
        upper, terms, last_terms = make_upper(info, total, other, diag_inverse, width)
        head, later, upper = lax.optimization_barrier((across[0], panel, upper))
        most, tail = cut(later, [(0, early), (early, last)])
        rest, near = lax.optimization_barrier((across[1], near))
        ends = [lax.ppermute(piece, "pcol", ENDS) for piece in (head, rest[:second], rest[second:])]
        middle = lax.ppermute(most, "pcol", MIDDLE)
        tail, rest = lax.optimization_barrier((tail, rest))
        middle_tail = lax.ppermute(tail, "pcol", MIDDLE)
        base = main_update(info, pivots, slab, total, other, panel, near, across, upper, terms)
        result = last_update(base, last_terms, ends[:2], middle, block, 0, [])
        return last_update(base, last_terms, ends[2:], middle_tail, block, early, [result])

    in_specs = (P("prow", "pcol"), P("prow", "pcol"), P(), P())
    return jax.shard_map(
        shards, mesh=mesh, in_specs=in_specs, out_specs=P("prow", "pcol"), check_vma=False
    )
```

```python
import jax
import jax.numpy as jnp
from jax import lax
from jax.experimental import pallas as pl
from jax.experimental.pallas import tpu as pltpu
from jax.sharding import PartitionSpec as P

SWAP = [(0, 1), (1, 0), (2, 3), (3, 2)]
ACROSS = [(0, 2), (1, 3), (2, 0), (3, 1)]
MIDDLE = [(1, 2), (2, 1)]
ENDS = [(2, 3), (1, 0)]
PIECES = (15, 13, 4)
TILE = 512
LAST_TILE = 256
SMALL = pl.CostEstimate(flops=0, bytes_accessed=0, transcendentals=0)
HBM = pl.BlockSpec(memory_space=pl.ANY)
VMEM = pl.BlockSpec(memory_space=pltpu.VMEM)


def split(x):
    high = x.astype(jnp.bfloat16)
    low = (x - high.astype(jnp.float32)).astype(jnp.bfloat16)
    return high, low


def left_terms(x):
    high, low = split(x)
    return jnp.concatenate([high, high, low], axis=1)


def right_terms(x):
    high, low = split(x)
    return jnp.concatenate([high, low, high], axis=0)


def dot(a, b):
    return jnp.dot(a, b, preferred_element_type=jnp.float32)


def aligned(start, size):
    return pl.ds(pl.multiple_of(start, size), size)


def load_kernel(spans, panel, *refs):
    outs, sem = refs[:-1], refs[-1]
    copies = [
        pltpu.make_async_copy(panel.at[pl.ds(start, size), :], out, sem.at[i])
        for i, ((start, size), out) in enumerate(zip(spans, outs))
    ]
    for copy in copies:
        copy.start()
    for copy in copies:
        copy.wait()


def load_pieces(panel, spans):
    return pl.pallas_call(
        lambda *refs: load_kernel(spans, *refs),
        out_shape=tuple(jax.ShapeDtypeStruct((size, panel.shape[1]), panel.dtype) for _, size in spans),
        in_specs=[pl.BlockSpec(memory_space=pltpu.HBM)],
        out_specs=tuple([VMEM] * len(spans)),
        scratch_shapes=[pltpu.SemaphoreType.DMA((len(spans),))],
        compiler_params=pltpu.CompilerParams(vmem_limit_bytes=8 << 20),
        cost_estimate=SMALL,
        name="load_pieces",
    )(pltpu.with_memory_space_constraint(panel, pltpu.HBM))


def cut_kernel(spans, panel, *refs):
    outs, (rows, sem, out_sem) = refs[:-3], refs[-3:]
    steps = []
    for i, (start, size) in enumerate(spans):
        for at in range(0, size, TILE):
            steps.append((i, start + at, at, min(TILE, size - at)))

    def load(number):
        _, row, _, size = steps[number]
        part = pl.ds(row, size)
        return pltpu.make_async_copy(panel.at[part, :], rows.at[part, :], sem.at[number])

    for number in range(len(steps)):
        load(number).start()
    for number, (i, row, at, size) in enumerate(steps):
        load(number).wait()
        pltpu.make_async_copy(rows.at[pl.ds(row, size), :], outs[i].at[pl.ds(at, size), :], out_sem.at[i]).start()
    for i, (start, size) in enumerate(spans):
        pltpu.make_async_copy(rows.at[pl.ds(start, size), :], outs[i], out_sem.at[i]).wait()


def cut(panel, spans):
    count = sum(-(-size // TILE) for _, size in spans)
    return pl.pallas_call(
        lambda *refs: cut_kernel(spans, *refs),
        out_shape=tuple(jax.ShapeDtypeStruct((size, panel.shape[1]), panel.dtype) for _, size in spans),
        in_specs=[pl.BlockSpec(memory_space=pltpu.HBM)],
        out_specs=tuple([HBM] * len(spans)),
        scratch_shapes=[
            pltpu.VMEM(panel.shape, panel.dtype),
            pltpu.SemaphoreType.DMA((count,)),
            pltpu.SemaphoreType.DMA((len(spans),)),
        ],
        compiler_params=pltpu.CompilerParams(vmem_limit_bytes=8 << 20),
        cost_estimate=SMALL,
        name="cut",
    )(pltpu.with_memory_space_constraint(panel, pltpu.HBM))


def pick_kernel(info, pivots, slab, send, keep, rows, sem, top_sem):
    copy = pltpu.make_async_copy(slab, rows, sem)
    copy.start()
    place = info[1]
    count = rows.shape[0]
    block = send.shape[0]
    first = place * count

    def fill(picked, top):
        load = pltpu.make_async_copy(slab.at[pl.ds(0, block), :], top, top_sem)

        @pl.when(place == 0)
        def _():
            load.start()

        @pl.when(place != 0)
        def _():
            top[...] = jnp.zeros_like(top)

        copy.wait()

        @pl.loop(0, block // 8)
        def _(group):
            base = pl.multiple_of(group * 8, 8)
            for j in range(8):
                row = pivots[base + j] - first
                owned = (row >= 0) & (row < count)
                value = rows[pl.ds(jnp.where(owned, row, 0), 1), :]
                picked[pl.ds(base + j, 1), :] = jnp.where(owned, value, 0.0)

        @pl.when(place == 0)
        def _():
            load.wait()

    @pl.when(place % 2 == 0)
    def _():
        fill(keep, send)

    @pl.when(place % 2 == 1)
    def _():
        fill(send, keep)


def pick(info, pivots, slab, block):
    columns = slab.shape[1]
    shape = jax.ShapeDtypeStruct((block, columns), slab.dtype)
    return pl.pallas_call(
        pick_kernel,
        out_shape=(shape, shape),
        grid_spec=pltpu.PrefetchScalarGridSpec(
            num_scalar_prefetch=2,
            grid=(),
            in_specs=[HBM],
            out_specs=(VMEM, VMEM),
            scratch_shapes=[
                pltpu.VMEM(slab.shape, slab.dtype),
                pltpu.SemaphoreType.DMA,
                pltpu.SemaphoreType.DMA,
            ],
        ),
        compiler_params=pltpu.CompilerParams(vmem_limit_bytes=16 << 20),
        cost_estimate=SMALL,
        name="pick",
    )(info, pivots, slab)


def upper_kernel(width, info, total, other, inverse, upper, terms, last_terms):
    block = upper.shape[0]

    def fill(picked):
        upper[...] = dot(left_terms(inverse[...]), right_terms(picked[...]))

    @pl.when(info[1] % 2 == 0)
    def _():
        fill(total)

    @pl.when(info[1] % 2 == 1)
    def _():
        fill(other)

    for shard in range(4):
        value = right_terms(upper[aligned((info[0] ^ shard) * width, width), :])
        if shard < 3:
            terms[pl.ds(shard * 3 * width, 3 * width), :] = value
        else:
            last_terms[...] = value


def make_upper(info, total, other, inverse, width):
    block, columns = total.shape
    return pl.pallas_call(
        lambda *refs: upper_kernel(width, *refs),
        out_shape=(
            jax.ShapeDtypeStruct((block, columns), total.dtype),
            jax.ShapeDtypeStruct((9 * width, columns), jnp.bfloat16),
            jax.ShapeDtypeStruct((3 * width, columns), jnp.bfloat16),
        ),
        grid_spec=pltpu.PrefetchScalarGridSpec(
            num_scalar_prefetch=1,
            grid=(),
            in_specs=[VMEM] * 3,
            out_specs=(VMEM, VMEM, VMEM),
        ),
        compiler_params=pltpu.CompilerParams(vmem_limit_bytes=24 << 20),
        cost_estimate=SMALL,
        name="upper",
    )(info, total, other, inverse)


def main_kernel(tile, info, pivots, slab, total, other, own, near, *refs):
    *across, upper, terms, out, own_rows, near_rows, across_rows, sem, panel_sem = refs
    copy = pltpu.make_async_copy(slab, out, sem)
    copy.start()
    loads = [(own, own_rows), (near, near_rows)]
    at = 0
    for piece in across:
        loads.append((piece, across_rows.at[pl.ds(at, piece.shape[0]), :]))
        at += piece.shape[0]
    loads = [pltpu.make_async_copy(a, b, panel_sem.at[i]) for i, (a, b) in enumerate(loads)]
    for load in loads:
        load.start()
    place = info[1]
    count = own_rows.shape[0]
    block = upper.shape[0]
    first = place * count
    copy.wait()

    def fill(old_top):
        @pl.loop(0, block // 8)
        def _(group):
            base = pl.multiple_of(group * 8, 8)
            for j in range(8):
                row = pivots[base + j] - first
                owned = (row >= 0) & (row < count)
                place_at = pl.ds(jnp.where(owned, row, 0), 1)
                out[place_at, :] = jnp.where(owned, old_top[pl.ds(base + j, 1), :], out[place_at, :])

    @pl.when(place % 2 == 0)
    def _():
        fill(other)

    @pl.when(place % 2 == 1)
    def _():
        fill(total)

    for load in loads:
        load.wait()

    @pl.loop(0, count // tile)
    def _(t):
        part = aligned(t * tile, tile)
        left = [left_terms(panel[part, :]) for panel in (own_rows, near_rows, across_rows)]
        out[part, :] = out[part, :] - dot(jnp.concatenate(left, axis=1), terms[...])

        @pl.when((place == 0) & (t < block // tile))
        def _():
            out[part, :] = upper[aligned(jnp.minimum(t * tile, block - tile), tile), :]


def main_update(info, pivots, slab, total, other, own, near, across, upper, terms):
    block = upper.shape[0]
    return pl.pallas_call(
        lambda *refs: main_kernel(min(TILE, block), *refs),
        out_shape=jax.ShapeDtypeStruct(slab.shape, slab.dtype),
        grid_spec=pltpu.PrefetchScalarGridSpec(
            num_scalar_prefetch=2,
            grid=(),
            in_specs=[HBM, VMEM, VMEM, HBM, HBM] + [HBM] * len(across) + [VMEM, VMEM],
            out_specs=VMEM,
            scratch_shapes=[pltpu.VMEM(own.shape, own.dtype)] * 3
            + [pltpu.SemaphoreType.DMA, pltpu.SemaphoreType.DMA((2 + len(across),))],
        ),
        compiler_params=pltpu.CompilerParams(vmem_limit_bytes=32 << 20),
        cost_estimate=SMALL,
        name="main_update",
    )(info, pivots, slab, total, other, own, near, *across, upper, terms)


def last_kernel(first_row, block, tile, parts, base, terms, *refs):
    ends, middle = refs[:parts], refs[parts]
    out, result, sem = refs[-3:]
    at = 0
    for end in ends:
        inner = 0
        while inner < end.shape[0]:
            size = min(tile, end.shape[0] - inner)
            part = pl.ds(at, size)
            row = first_row + at
            delta = dot(left_terms(end[pl.ds(inner, size), :] + middle[part, :]), terms[...])
            if row < block:
                delta = jnp.where(lax.axis_index("prow") == 0, 0.0, delta)
            result[part, :] = base[pl.ds(row, size), :] - delta
            pltpu.make_async_copy(result.at[part, :], out.at[pl.ds(row, size), :], sem).start()
            inner += size
            at += size
    pltpu.make_async_copy(result, out.at[pl.ds(first_row, at), :], sem).wait()


def last_update(base, terms, ends, middle, block, first_row, done):
    columns = base.shape[1]
    count = middle.shape[0]
    return pl.pallas_call(
        lambda *refs: last_kernel(first_row, block, min(LAST_TILE, block), len(ends), *refs),
        out_shape=jax.ShapeDtypeStruct(base.shape, base.dtype),
        in_specs=[VMEM] * (3 + len(ends)) + [HBM] * len(done),
        out_specs=HBM,
        scratch_shapes=[pltpu.VMEM((count, columns), base.dtype), pltpu.SemaphoreType.DMA],
        input_output_aliases={3 + len(ends): 0} if done else {},
        compiler_params=pltpu.CompilerParams(vmem_limit_bytes=24 << 20),
        cost_estimate=SMALL,
        name="last_update",
    )(base, terms, *ends, middle, *done)


def exchange(value, bit, count):
    return lax.ppermute(value, "prow", [(i, i ^ (1 << bit)) for i in range(count)])


def solution(mesh):
    row_parts, column_parts = mesh.shape["prow"], mesh.shape["pcol"]
    bits = row_parts.bit_length() - 1
    if column_parts != 4 or row_parts != 1 << bits or bits < 1:
        raise ValueError("unsupported mesh")

    def shards(panel, slab, pivots, diag_inverse):
        rows_here = slab.shape[0]
        width = panel.shape[1]
        block = diag_inverse.shape[0]
        place = lax.axis_index("prow")
        column = lax.axis_index("pcol")
        info = jnp.stack([column, place]).astype(jnp.int32)

        first, second, last = (rows_here * part // sum(PIECES) for part in PIECES)
        early = first + second
        near = lax.ppermute(panel, "pcol", SWAP)
        pieces = cut(panel, [(0, first), (first, second + last)])
        across = [lax.ppermute(piece, "pcol", ACROSS) for piece in pieces]

        def gather_rows(slab, pivots):
            send, keep = pick(info, pivots, slab, block)
            total = keep + exchange(send, 0, row_parts)
            for bit in range(1, bits):
                total = total + exchange(total, bit, row_parts)
            return total, exchange(total, 0, row_parts)

        def no_rows(slab, pivots):
            return slab[:block], slab[:block]

        total, other = lax.cond(pivots[0] >= 0, gather_rows, no_rows, slab, pivots)
        upper, terms, last_terms = make_upper(info, total, other, diag_inverse, width)
        head, later, upper = lax.optimization_barrier((across[0], panel, upper))
        most, tail = load_pieces(later, [(0, early), (early, last)])
        rest, near = lax.optimization_barrier((across[1], near))
        ends = [lax.ppermute(piece, "pcol", ENDS) for piece in (head, rest[:second], rest[second:])]
        middle = lax.ppermute(most, "pcol", MIDDLE)
        tail, rest = lax.optimization_barrier((tail, rest))
        middle_tail = lax.ppermute(tail, "pcol", MIDDLE)
        base = main_update(info, pivots, slab, total, other, panel, near, across, upper, terms)
        result = last_update(base, last_terms, ends[:2], middle, block, 0, [])
        return last_update(base, last_terms, ends[2:], middle_tail, block, early, [result])

    in_specs = (P("prow", "pcol"), P("prow", "pcol"), P(), P())
    return jax.shard_map(
        shards, mesh=mesh, in_specs=in_specs, out_specs=P("prow", "pcol"), check_vma=False
    )
```

```python
import jax
import jax.numpy as jnp
from jax import lax
from jax.experimental import pallas as pl
from jax.experimental.pallas import tpu as pltpu
from jax.sharding import PartitionSpec as P

SWAP = [(0, 1), (1, 0), (2, 3), (3, 2)]
ACROSS = [(0, 2), (1, 3), (2, 0), (3, 1)]
MIDDLE = [(1, 2), (2, 1)]
ENDS = [(2, 3), (1, 0)]
PIECES = (4, 12, 12, 4)
TILE = 512
LAST_TILE = 256
SMALL = pl.CostEstimate(flops=0, bytes_accessed=0, transcendentals=0)
HBM = pl.BlockSpec(memory_space=pl.ANY)
VMEM = pl.BlockSpec(memory_space=pltpu.VMEM)


def split(x):
    high = x.astype(jnp.bfloat16)
    low = (x - high.astype(jnp.float32)).astype(jnp.bfloat16)
    return high, low


def left_terms(x):
    high, low = split(x)
    return jnp.concatenate([high, high, low], axis=1)


def right_terms(x):
    high, low = split(x)
    return jnp.concatenate([high, low, high], axis=0)


def dot(a, b):
    return jnp.dot(a, b, preferred_element_type=jnp.float32)


def aligned(start, size):
    return pl.ds(pl.multiple_of(start, size), size)


def load_kernel(spans, panel, *refs):
    outs, sem = refs[:-1], refs[-1]
    copies = [
        pltpu.make_async_copy(panel.at[pl.ds(start, size), :], out, sem.at[i])
        for i, ((start, size), out) in enumerate(zip(spans, outs))
    ]
    for copy in copies:
        copy.start()
    for copy in copies:
        copy.wait()


def load_pieces(panel, spans):
    return pl.pallas_call(
        lambda *refs: load_kernel(spans, *refs),
        out_shape=tuple(jax.ShapeDtypeStruct((size, panel.shape[1]), panel.dtype) for _, size in spans),
        in_specs=[pl.BlockSpec(memory_space=pltpu.HBM)],
        out_specs=tuple([VMEM] * len(spans)),
        scratch_shapes=[pltpu.SemaphoreType.DMA((len(spans),))],
        compiler_params=pltpu.CompilerParams(vmem_limit_bytes=8 << 20),
        cost_estimate=SMALL,
        name="load_pieces",
    )(pltpu.with_memory_space_constraint(panel, pltpu.HBM))


def cut_kernel(spans, panel, *refs):
    outs, (rows, sem, out_sem) = refs[:-3], refs[-3:]
    steps = []
    for i, (start, size) in enumerate(spans):
        for at in range(0, size, TILE):
            steps.append((i, start + at, at, min(TILE, size - at)))

    def load(number):
        _, row, _, size = steps[number]
        part = pl.ds(row, size)
        return pltpu.make_async_copy(panel.at[part, :], rows.at[part, :], sem.at[number])

    for number in range(len(steps)):
        load(number).start()
    for number, (i, row, at, size) in enumerate(steps):
        load(number).wait()
        pltpu.make_async_copy(rows.at[pl.ds(row, size), :], outs[i].at[pl.ds(at, size), :], out_sem.at[i]).start()
    for i, (start, size) in enumerate(spans):
        pltpu.make_async_copy(rows.at[pl.ds(start, size), :], outs[i], out_sem.at[i]).wait()


def cut(panel, spans):
    count = sum(-(-size // TILE) for _, size in spans)
    return pl.pallas_call(
        lambda *refs: cut_kernel(spans, *refs),
        out_shape=tuple(jax.ShapeDtypeStruct((size, panel.shape[1]), panel.dtype) for _, size in spans),
        in_specs=[pl.BlockSpec(memory_space=pltpu.HBM)],
        out_specs=tuple([HBM] * len(spans)),
        scratch_shapes=[
            pltpu.VMEM(panel.shape, panel.dtype),
            pltpu.SemaphoreType.DMA((count,)),
            pltpu.SemaphoreType.DMA((len(spans),)),
        ],
        compiler_params=pltpu.CompilerParams(vmem_limit_bytes=8 << 20),
        cost_estimate=SMALL,
        name="cut",
    )(pltpu.with_memory_space_constraint(panel, pltpu.HBM))


def pick_kernel(info, pivots, slab, send, keep, rows, sem, top_sem):
    copy = pltpu.make_async_copy(slab, rows, sem)
    copy.start()
    place = info[1]
    count = rows.shape[0]
    block = send.shape[0]
    first = place * count

    def fill(picked, top):
        load = pltpu.make_async_copy(slab.at[pl.ds(0, block), :], top, top_sem)

        @pl.when(place == 0)
        def _():
            load.start()

        @pl.when(place != 0)
        def _():
            top[...] = jnp.zeros_like(top)

        copy.wait()

        @pl.loop(0, block // 8)
        def _(group):
            base = pl.multiple_of(group * 8, 8)
            for j in range(8):
                row = pivots[base + j] - first
                owned = (row >= 0) & (row < count)
                value = rows[pl.ds(jnp.where(owned, row, 0), 1), :]
                picked[pl.ds(base + j, 1), :] = jnp.where(owned, value, 0.0)

        @pl.when(place == 0)
        def _():
            load.wait()

    @pl.when(place % 2 == 0)
    def _():
        fill(keep, send)

    @pl.when(place % 2 == 1)
    def _():
        fill(send, keep)


def pick(info, pivots, slab, block):
    columns = slab.shape[1]
    shape = jax.ShapeDtypeStruct((block, columns), slab.dtype)
    return pl.pallas_call(
        pick_kernel,
        out_shape=(shape, shape),
        grid_spec=pltpu.PrefetchScalarGridSpec(
            num_scalar_prefetch=2,
            grid=(),
            in_specs=[HBM],
            out_specs=(VMEM, VMEM),
            scratch_shapes=[
                pltpu.VMEM(slab.shape, slab.dtype),
                pltpu.SemaphoreType.DMA,
                pltpu.SemaphoreType.DMA,
            ],
        ),
        compiler_params=pltpu.CompilerParams(vmem_limit_bytes=16 << 20),
        cost_estimate=SMALL,
        name="pick",
    )(info, pivots, slab)


def upper_kernel(width, info, total, other, inverse, upper, terms, last_terms):
    block = upper.shape[0]

    def fill(picked):
        upper[...] = dot(left_terms(inverse[...]), right_terms(picked[...]))

    @pl.when(info[1] % 2 == 0)
    def _():
        fill(total)

    @pl.when(info[1] % 2 == 1)
    def _():
        fill(other)

    for shard in range(4):
        value = right_terms(upper[aligned((info[0] ^ shard) * width, width), :])
        if shard < 3:
            terms[pl.ds(shard * 3 * width, 3 * width), :] = value
        else:
            last_terms[...] = value


def make_upper(info, total, other, inverse, width):
    block, columns = total.shape
    return pl.pallas_call(
        lambda *refs: upper_kernel(width, *refs),
        out_shape=(
            jax.ShapeDtypeStruct((block, columns), total.dtype),
            jax.ShapeDtypeStruct((9 * width, columns), jnp.bfloat16),
            jax.ShapeDtypeStruct((3 * width, columns), jnp.bfloat16),
        ),
        grid_spec=pltpu.PrefetchScalarGridSpec(
            num_scalar_prefetch=1,
            grid=(),
            in_specs=[VMEM] * 3,
            out_specs=(VMEM, VMEM, VMEM),
        ),
        compiler_params=pltpu.CompilerParams(vmem_limit_bytes=24 << 20),
        cost_estimate=SMALL,
        name="upper",
    )(info, total, other, inverse)


def main_kernel(tile, info, pivots, slab, total, other, own, near, *refs):
    *across, upper, terms, out, own_rows, near_rows, across_rows, sem, panel_sem = refs
    copy = pltpu.make_async_copy(slab, out, sem)
    copy.start()
    loads = [(own, own_rows), (near, near_rows)]
    at = 0
    for piece in across:
        loads.append((piece, across_rows.at[pl.ds(at, piece.shape[0]), :]))
        at += piece.shape[0]
    loads = [pltpu.make_async_copy(a, b, panel_sem.at[i]) for i, (a, b) in enumerate(loads)]
    for load in loads:
        load.start()
    place = info[1]
    count = own_rows.shape[0]
    block = upper.shape[0]
    first = place * count
    copy.wait()

    def fill(old_top):
        @pl.loop(0, block // 8)
        def _(group):
            base = pl.multiple_of(group * 8, 8)
            for j in range(8):
                row = pivots[base + j] - first
                owned = (row >= 0) & (row < count)
                place_at = pl.ds(jnp.where(owned, row, 0), 1)
                out[place_at, :] = jnp.where(owned, old_top[pl.ds(base + j, 1), :], out[place_at, :])

    @pl.when(place % 2 == 0)
    def _():
        fill(other)

    @pl.when(place % 2 == 1)
    def _():
        fill(total)

    for load in loads:
        load.wait()

    @pl.loop(0, count // tile)
    def _(t):
        part = aligned(t * tile, tile)
        left = [left_terms(panel[part, :]) for panel in (own_rows, near_rows, across_rows)]
        out[part, :] = out[part, :] - dot(jnp.concatenate(left, axis=1), terms[...])

        @pl.when((place == 0) & (t < block // tile))
        def _():
            out[part, :] = upper[aligned(jnp.minimum(t * tile, block - tile), tile), :]


def main_update(info, pivots, slab, total, other, own, near, across, upper, terms):
    block = upper.shape[0]
    return pl.pallas_call(
        lambda *refs: main_kernel(min(TILE, block), *refs),
        out_shape=jax.ShapeDtypeStruct(slab.shape, slab.dtype),
        grid_spec=pltpu.PrefetchScalarGridSpec(
            num_scalar_prefetch=2,
            grid=(),
            in_specs=[HBM, VMEM, VMEM, HBM, HBM] + [HBM] * len(across) + [VMEM, VMEM],
            out_specs=VMEM,
            scratch_shapes=[pltpu.VMEM(own.shape, own.dtype)] * 3
            + [pltpu.SemaphoreType.DMA, pltpu.SemaphoreType.DMA((2 + len(across),))],
        ),
        compiler_params=pltpu.CompilerParams(vmem_limit_bytes=32 << 20),
        cost_estimate=SMALL,
        name="main_update",
    )(info, pivots, slab, total, other, own, near, *across, upper, terms)


def last_kernel(first_row, block, tile, parts, base, terms, *refs):
    ends, middle = refs[:parts], refs[parts]
    out, result, sem = refs[-3:]
    at = 0
    for end in ends:
        inner = 0
        while inner < end.shape[0]:
            size = min(tile, end.shape[0] - inner)
            part = pl.ds(at, size)
            row = first_row + at
            delta = dot(left_terms(end[pl.ds(inner, size), :] + middle[part, :]), terms[...])
            if row < block:
                delta = jnp.where(lax.axis_index("prow") == 0, 0.0, delta)
            result[part, :] = base[pl.ds(row, size), :] - delta
            pltpu.make_async_copy(result.at[part, :], out.at[pl.ds(row, size), :], sem).start()
            inner += size
            at += size
    pltpu.make_async_copy(result, out.at[pl.ds(first_row, at), :], sem).wait()


def last_update(base, terms, ends, middle, block, first_row, done):
    columns = base.shape[1]
    count = middle.shape[0]
    return pl.pallas_call(
        lambda *refs: last_kernel(first_row, block, min(LAST_TILE, block), len(ends), *refs),
        out_shape=jax.ShapeDtypeStruct(base.shape, base.dtype),
        in_specs=[VMEM] * (3 + len(ends)) + [HBM] * len(done),
        out_specs=HBM,
        scratch_shapes=[pltpu.VMEM((count, columns), base.dtype), pltpu.SemaphoreType.DMA],
        input_output_aliases={3 + len(ends): 0} if done else {},
        compiler_params=pltpu.CompilerParams(vmem_limit_bytes=24 << 20),
        cost_estimate=SMALL,
        name="last_update",
    )(base, terms, *ends, middle, *done)


def exchange(value, bit, count):
    return lax.ppermute(value, "prow", [(i, i ^ (1 << bit)) for i in range(count)])


def solution(mesh):
    row_parts, column_parts = mesh.shape["prow"], mesh.shape["pcol"]
    bits = row_parts.bit_length() - 1
    if column_parts != 4 or row_parts != 1 << bits or bits < 1:
        raise ValueError("unsupported mesh")

    def shards(panel, slab, pivots, diag_inverse):
        rows_here = slab.shape[0]
        width = panel.shape[1]
        block = diag_inverse.shape[0]
        place = lax.axis_index("prow")
        column = lax.axis_index("pcol")
        info = jnp.stack([column, place]).astype(jnp.int32)

        small, first, second, last = (rows_here * part // sum(PIECES) for part in PIECES)
        early = small + first + second
        near = lax.ppermute(panel, "pcol", SWAP)
        start = panel[:small]
        begun = lax.ppermute(start, "pcol", ACROSS)
        later, _ = lax.optimization_barrier((panel, start))
        pieces = cut(later, [(small, first), (small + first, second + last)])
        across = [lax.ppermute(piece, "pcol", ACROSS) for piece in pieces]

        def gather_rows(slab, pivots):
            send, keep = pick(info, pivots, slab, block)
            total = keep + exchange(send, 0, row_parts)
            for bit in range(1, bits):
                total = total + exchange(total, bit, row_parts)
            return total, exchange(total, 0, row_parts)

        def no_rows(slab, pivots):
            return slab[:block], slab[:block]

        total, other = lax.cond(pivots[0] >= 0, gather_rows, no_rows, slab, pivots)
        upper, terms, last_terms = make_upper(info, total, other, diag_inverse, width)
        begun, later, upper = lax.optimization_barrier((begun, panel, upper))
        head, upper = lax.optimization_barrier((across[0], upper))
        head = jnp.concatenate([begun, head], axis=0)
        most, tail = load_pieces(later, [(0, early), (early, last)])
        rest, near = lax.optimization_barrier((across[1], near))
        ends = [lax.ppermute(piece, "pcol", ENDS) for piece in (head, rest[:second], rest[second:])]
        middle = lax.ppermute(most, "pcol", MIDDLE)
        tail, rest = lax.optimization_barrier((tail, rest))
        middle_tail = lax.ppermute(tail, "pcol", MIDDLE)
        base = main_update(info, pivots, slab, total, other, panel, near, [head, rest], upper, terms)
        result = last_update(base, last_terms, ends[:2], middle, block, 0, [])
        return last_update(base, last_terms, ends[2:], middle_tail, block, early, [result])

    in_specs = (P("prow", "pcol"), P("prow", "pcol"), P(), P())
    return jax.shard_map(
        shards, mesh=mesh, in_specs=in_specs, out_specs=P("prow", "pcol"), check_vma=False
    )
```

```python
import jax
import jax.numpy as jnp
from jax import lax
from jax.experimental import pallas as pl
from jax.experimental.pallas import tpu as pltpu
from jax.sharding import PartitionSpec as P

SWAP = [(0, 1), (1, 0), (2, 3), (3, 2)]
ACROSS = [(0, 2), (1, 3), (2, 0), (3, 1)]
MIDDLE = [(1, 2), (2, 1)]
ENDS = [(2, 3), (1, 0)]
FAR = [(0, 2), (3, 1)]
PIECES = (57, 53, 18)
TILE = 512
LAST_TILE = 256
SMALL = pl.CostEstimate(flops=0, bytes_accessed=0, transcendentals=0)
HBM = pl.BlockSpec(memory_space=pl.ANY)
VMEM = pl.BlockSpec(memory_space=pltpu.VMEM)


def split(x):
    high = x.astype(jnp.bfloat16)
    low = (x - high.astype(jnp.float32)).astype(jnp.bfloat16)
    return high, low


def left_terms(x):
    high, low = split(x)
    return jnp.concatenate([high, high, low], axis=1)


def right_terms(x):
    high, low = split(x)
    return jnp.concatenate([high, low, high], axis=0)


def dot(a, b):
    return jnp.dot(a, b, preferred_element_type=jnp.float32)


def aligned(start, size):
    return pl.ds(pl.multiple_of(start, size), size)


def load_kernel(spans, panel, *refs):
    outs, sem = refs[:-1], refs[-1]
    copies = [
        pltpu.make_async_copy(panel.at[pl.ds(start, size), :], out, sem.at[i])
        for i, ((start, size), out) in enumerate(zip(spans, outs))
    ]
    for copy in copies:
        copy.start()
    for copy in copies:
        copy.wait()


def load_pieces(panel, spans):
    return pl.pallas_call(
        lambda *refs: load_kernel(spans, *refs),
        out_shape=tuple(jax.ShapeDtypeStruct((size, panel.shape[1]), panel.dtype) for _, size in spans),
        in_specs=[pl.BlockSpec(memory_space=pltpu.HBM)],
        out_specs=tuple([VMEM] * len(spans)),
        scratch_shapes=[pltpu.SemaphoreType.DMA((len(spans),))],
        compiler_params=pltpu.CompilerParams(vmem_limit_bytes=8 << 20),
        cost_estimate=SMALL,
        name="load_pieces",
    )(pltpu.with_memory_space_constraint(panel, pltpu.HBM))


def cut_kernel(spans, panel, *refs):
    outs, (rows, sem, out_sem) = refs[:-3], refs[-3:]
    steps = []
    for i, (start, size) in enumerate(spans):
        for at in range(0, size, TILE):
            steps.append((i, start + at, at, min(TILE, size - at)))

    def load(number):
        _, row, _, size = steps[number]
        part = pl.ds(row, size)
        return pltpu.make_async_copy(panel.at[part, :], rows.at[part, :], sem.at[number])

    for number in range(len(steps)):
        load(number).start()
    for number, (i, row, at, size) in enumerate(steps):
        load(number).wait()
        pltpu.make_async_copy(rows.at[pl.ds(row, size), :], outs[i].at[pl.ds(at, size), :], out_sem.at[i]).start()
    for i, (start, size) in enumerate(spans):
        pltpu.make_async_copy(rows.at[pl.ds(start, size), :], outs[i], out_sem.at[i]).wait()


def cut(panel, spans):
    count = sum(-(-size // TILE) for _, size in spans)
    return pl.pallas_call(
        lambda *refs: cut_kernel(spans, *refs),
        out_shape=tuple(jax.ShapeDtypeStruct((size, panel.shape[1]), panel.dtype) for _, size in spans),
        in_specs=[pl.BlockSpec(memory_space=pltpu.HBM)],
        out_specs=tuple([HBM] * len(spans)),
        scratch_shapes=[
            pltpu.VMEM(panel.shape, panel.dtype),
            pltpu.SemaphoreType.DMA((count,)),
            pltpu.SemaphoreType.DMA((len(spans),)),
        ],
        compiler_params=pltpu.CompilerParams(vmem_limit_bytes=8 << 20),
        cost_estimate=SMALL,
        name="cut",
    )(pltpu.with_memory_space_constraint(panel, pltpu.HBM))


def pick_kernel(info, pivots, slab, send, keep, rows, sem, top_sem):
    copy = pltpu.make_async_copy(slab, rows, sem)
    copy.start()
    place = info[1]
    count = rows.shape[0]
    block = send.shape[0]
    first = place * count

    def fill(picked, top):
        load = pltpu.make_async_copy(slab.at[pl.ds(0, block), :], top, top_sem)

        @pl.when(place == 0)
        def _():
            load.start()

        @pl.when(place != 0)
        def _():
            top[...] = jnp.zeros_like(top)

        copy.wait()

        @pl.loop(0, block // 8)
        def _(group):
            base = pl.multiple_of(group * 8, 8)
            for j in range(8):
                row = pivots[base + j] - first
                owned = (row >= 0) & (row < count)
                value = rows[pl.ds(jnp.where(owned, row, 0), 1), :]
                picked[pl.ds(base + j, 1), :] = jnp.where(owned, value, 0.0)

        @pl.when(place == 0)
        def _():
            load.wait()

    @pl.when(place % 2 == 0)
    def _():
        fill(keep, send)

    @pl.when(place % 2 == 1)
    def _():
        fill(send, keep)


def pick(info, pivots, slab, block):
    columns = slab.shape[1]
    shape = jax.ShapeDtypeStruct((block, columns), slab.dtype)
    return pl.pallas_call(
        pick_kernel,
        out_shape=(shape, shape),
        grid_spec=pltpu.PrefetchScalarGridSpec(
            num_scalar_prefetch=2,
            grid=(),
            in_specs=[HBM],
            out_specs=(VMEM, VMEM),
            scratch_shapes=[
                pltpu.VMEM(slab.shape, slab.dtype),
                pltpu.SemaphoreType.DMA,
                pltpu.SemaphoreType.DMA,
            ],
        ),
        compiler_params=pltpu.CompilerParams(vmem_limit_bytes=16 << 20),
        cost_estimate=SMALL,
        name="pick",
    )(info, pivots, slab)


def upper_kernel(width, info, total, other, inverse, upper, terms, across_terms, last_terms):
    block = upper.shape[0]

    def fill(picked):
        upper[...] = dot(left_terms(inverse[...]), right_terms(picked[...]))

    @pl.when(info[1] % 2 == 0)
    def _():
        fill(total)

    @pl.when(info[1] % 2 == 1)
    def _():
        fill(other)

    for shard in range(4):
        value = right_terms(upper[aligned((info[0] ^ shard) * width, width), :])
        if shard == 2:
            across_terms[...] = value
        if shard < 3:
            terms[pl.ds(shard * 3 * width, 3 * width), :] = value
        else:
            last_terms[...] = value


def make_upper(info, total, other, inverse, width):
    block, columns = total.shape
    return pl.pallas_call(
        lambda *refs: upper_kernel(width, *refs),
        out_shape=(
            jax.ShapeDtypeStruct((block, columns), total.dtype),
            jax.ShapeDtypeStruct((9 * width, columns), jnp.bfloat16),
            jax.ShapeDtypeStruct((3 * width, columns), jnp.bfloat16),
            jax.ShapeDtypeStruct((3 * width, columns), jnp.bfloat16),
        ),
        grid_spec=pltpu.PrefetchScalarGridSpec(
            num_scalar_prefetch=1,
            grid=(),
            in_specs=[VMEM] * 3,
            out_specs=(VMEM, VMEM, VMEM, VMEM),
        ),
        compiler_params=pltpu.CompilerParams(vmem_limit_bytes=24 << 20),
        cost_estimate=SMALL,
        name="upper",
    )(info, total, other, inverse)


def main_kernel(tile, info, pivots, slab, total, other, own, near, *refs):
    *across, upper, terms, out, own_rows, near_rows, across_rows, sem, panel_sem = refs
    copy = pltpu.make_async_copy(slab, out, sem)
    copy.start()
    loads = [(own, own_rows), (near, near_rows)]
    at = 0
    for piece in across:
        loads.append((piece, across_rows.at[pl.ds(at, piece.shape[0]), :]))
        at += piece.shape[0]
    loads = [pltpu.make_async_copy(a, b, panel_sem.at[i]) for i, (a, b) in enumerate(loads)]
    for load in loads:
        load.start()
    place = info[1]
    count = own_rows.shape[0]
    block = upper.shape[0]
    first = place * count
    copy.wait()

    def fill(old_top):
        @pl.loop(0, block // 8)
        def _(group):
            base = pl.multiple_of(group * 8, 8)
            for j in range(8):
                row = pivots[base + j] - first
                owned = (row >= 0) & (row < count)
                place_at = pl.ds(jnp.where(owned, row, 0), 1)
                out[place_at, :] = jnp.where(owned, old_top[pl.ds(base + j, 1), :], out[place_at, :])

    @pl.when(place % 2 == 0)
    def _():
        fill(other)

    @pl.when(place % 2 == 1)
    def _():
        fill(total)

    for load in loads:
        load.wait()

    def subtract(part, panels):
        left = jnp.concatenate([left_terms(panel[part, :]) for panel in panels], axis=1)
        out[part, :] = out[part, :] - dot(left, terms[pl.ds(0, left.shape[1]), :])

    @pl.loop(0, at // tile)
    def _(t):
        part = aligned(t * tile, tile)
        subtract(part, (own_rows, near_rows, across_rows))

        @pl.when((place == 0) & (t < block // tile))
        def _():
            out[part, :] = upper[aligned(jnp.minimum(t * tile, block - tile), tile), :]

    if at % tile:
        subtract(pl.ds(at - at % tile, at % tile), (own_rows, near_rows, across_rows))
    subtract(pl.ds(at, count - at), (own_rows, near_rows))


def main_update(info, pivots, slab, total, other, own, near, across, upper, terms):
    block = upper.shape[0]
    return pl.pallas_call(
        lambda *refs: main_kernel(min(TILE, block), *refs),
        out_shape=jax.ShapeDtypeStruct(slab.shape, slab.dtype),
        grid_spec=pltpu.PrefetchScalarGridSpec(
            num_scalar_prefetch=2,
            grid=(),
            in_specs=[HBM, VMEM, VMEM, HBM, HBM] + [HBM] * len(across) + [VMEM, VMEM],
            out_specs=VMEM,
            scratch_shapes=[pltpu.VMEM(own.shape, own.dtype)] * 2
            + [pltpu.VMEM((sum(piece.shape[0] for piece in across), own.shape[1]), own.dtype)]
            + [pltpu.SemaphoreType.DMA, pltpu.SemaphoreType.DMA((2 + len(across),))],
        ),
        compiler_params=pltpu.CompilerParams(vmem_limit_bytes=32 << 20),
        cost_estimate=SMALL,
        name="main_update",
    )(info, pivots, slab, total, other, own, near, *across, upper, terms)


def last_kernel(first_row, block, tile, groups, base, *refs):
    out, result, sem = refs[-3:]
    count = result.shape[0]
    blocks = []
    at = 0
    for offsets in groups:
        blocks.append((refs[at], list(zip(refs[at + 1 : at + 1 + len(offsets)], offsets))))
        at += 1 + len(offsets)
    for at in range(0, count, tile):
        size = min(tile, count - at)
        part = pl.ds(at, size)
        row = first_row + at
        delta = None
        for terms, pieces in blocks:
            left = sum(piece[pl.ds(offset + at, size), :] for piece, offset in pieces)
            change = dot(left_terms(left), terms[...])
            delta = change if delta is None else delta + change
        if row < block:
            delta = jnp.where(lax.axis_index("prow") == 0, 0.0, delta)
        result[part, :] = base[pl.ds(row, size), :] - delta
        pltpu.make_async_copy(result.at[part, :], out.at[pl.ds(row, size), :], sem).start()
    pltpu.make_async_copy(result, out.at[pl.ds(first_row, count), :], sem).wait()


def last_update(base, groups, count, block, first_row, done):
    offsets = [[offset for _, offset in pieces] for _, pieces in groups]
    arrays = [array for terms, pieces in groups for array in (terms, *(piece for piece, _ in pieces))]
    return pl.pallas_call(
        lambda *refs: last_kernel(first_row, block, min(LAST_TILE, block), offsets, *refs),
        out_shape=jax.ShapeDtypeStruct(base.shape, base.dtype),
        in_specs=[VMEM] * (1 + len(arrays)) + [HBM] * len(done),
        out_specs=HBM,
        scratch_shapes=[pltpu.VMEM((count, base.shape[1]), base.dtype), pltpu.SemaphoreType.DMA],
        input_output_aliases={1 + len(arrays): 0} if done else {},
        compiler_params=pltpu.CompilerParams(vmem_limit_bytes=24 << 20),
        cost_estimate=SMALL,
        name="last_update",
    )(base, *arrays, *done)


def exchange(value, bit, count):
    return lax.ppermute(value, "prow", [(i, i ^ (1 << bit)) for i in range(count)])


def solution(mesh):
    row_parts, column_parts = mesh.shape["prow"], mesh.shape["pcol"]
    bits = row_parts.bit_length() - 1
    if column_parts != 4 or row_parts != 1 << bits or bits < 1:
        raise ValueError("unsupported mesh")

    def shards(panel, slab, pivots, diag_inverse):
        rows_here = slab.shape[0]
        width = panel.shape[1]
        block = diag_inverse.shape[0]
        place = lax.axis_index("prow")
        column = lax.axis_index("pcol")
        info = jnp.stack([column, place]).astype(jnp.int32)

        first, second, last = (rows_here * part // sum(PIECES) for part in PIECES)
        early = first + second
        spans = [(0, first), (first, second), (early, last)]
        near = lax.ppermute(panel, "pcol", SWAP)
        *pieces, tail = cut(panel, spans)
        across = [lax.ppermute(piece, "pcol", ACROSS) for piece in pieces]
        far = lax.ppermute(tail, "pcol", FAR)

        def gather_rows(slab, pivots):
            send, keep = pick(info, pivots, slab, block)
            total = keep + exchange(send, 0, row_parts)
            for bit in range(1, bits):
                total = total + exchange(total, bit, row_parts)
            return total, exchange(total, 0, row_parts)

        def no_rows(slab, pivots):
            return slab[:block], slab[:block]

        total, other = lax.cond(pivots[0] >= 0, gather_rows, no_rows, slab, pivots)
        upper, terms, across_terms, last_terms = make_upper(info, total, other, diag_inverse, width)
        far, later, upper = lax.optimization_barrier((far, panel, upper))
        head, upper = lax.optimization_barrier((across[0], upper))
        head_mid, rest_mid, tail_mid = load_pieces(later, spans)
        tail_mid = lax.ppermute(tail_mid, "pcol", MIDDLE)
        head_mid = lax.ppermute(head_mid, "pcol", MIDDLE)
        head_end = lax.ppermute(head, "pcol", ENDS)
        rest, rest_mid, near = lax.optimization_barrier((across[1], rest_mid, near))
        rest_end = lax.ppermute(rest, "pcol", ENDS)
        rest_mid = lax.ppermute(rest_mid, "pcol", MIDDLE)
        both, rest = lax.optimization_barrier((jnp.concatenate([far, tail_mid], axis=0), rest))
        both = lax.ppermute(both, "pcol", ENDS)

        base = main_update(info, pivots, slab, total, other, panel, near, [head, rest], upper, terms)
        result = last_update(base, [(last_terms, [(head_end, 0), (head_mid, 0)])], first, block, 0, [])
        result = last_update(base, [(last_terms, [(rest_end, 0), (rest_mid, 0)])], second, block, first, [result])
        groups = [(across_terms, [(far, 0), (both, last)]), (last_terms, [(tail_mid, 0), (both, 0)])]
        return last_update(base, groups, last, block, early, [result])

    in_specs = (P("prow", "pcol"), P("prow", "pcol"), P(), P())
    return jax.shard_map(
        shards, mesh=mesh, in_specs=in_specs, out_specs=P("prow", "pcol"), check_vma=False
    )
```

```python
import jax
import jax.numpy as jnp
from jax import lax
from jax.experimental import pallas as pl
from jax.experimental.pallas import tpu as pltpu
from jax.sharding import PartitionSpec as P

SWAP = [(0, 1), (1, 0), (2, 3), (3, 2)]
ACROSS = [(0, 2), (1, 3), (2, 0), (3, 1)]
MIDDLE = [(1, 2), (2, 1)]
ENDS = [(2, 3), (1, 0)]
FAR = [(0, 2), (3, 1)]
PIECES = (64, 46, 18)
MIDDLE_PIECES = (58, 52, 18)
TILE = 512
LAST_TILE = 256
SMALL = pl.CostEstimate(flops=0, bytes_accessed=0, transcendentals=0)
HBM = pl.BlockSpec(memory_space=pl.ANY)
VMEM = pl.BlockSpec(memory_space=pltpu.VMEM)


def split(x):
    high = x.astype(jnp.bfloat16)
    low = (x - high.astype(jnp.float32)).astype(jnp.bfloat16)
    return high, low


def left_terms(x):
    high, low = split(x)
    return jnp.concatenate([high, high, low], axis=1)


def right_terms(x):
    high, low = split(x)
    return jnp.concatenate([high, low, high], axis=0)


def dot(a, b):
    return jnp.dot(a, b, preferred_element_type=jnp.float32)


def aligned(start, size):
    return pl.ds(pl.multiple_of(start, size), size)


def load_kernel(spans, panel, *refs):
    outs, sem = refs[:-1], refs[-1]
    copies = [
        pltpu.make_async_copy(panel.at[pl.ds(start, size), :], out, sem.at[i])
        for i, ((start, size), out) in enumerate(zip(spans, outs))
    ]
    for copy in copies:
        copy.start()
    for copy in copies:
        copy.wait()


def load_pieces(panel, spans):
    return pl.pallas_call(
        lambda *refs: load_kernel(spans, *refs),
        out_shape=tuple(jax.ShapeDtypeStruct((size, panel.shape[1]), panel.dtype) for _, size in spans),
        in_specs=[pl.BlockSpec(memory_space=pltpu.HBM)],
        out_specs=tuple([VMEM] * len(spans)),
        scratch_shapes=[pltpu.SemaphoreType.DMA((len(spans),))],
        compiler_params=pltpu.CompilerParams(vmem_limit_bytes=8 << 20),
        cost_estimate=SMALL,
        name="load_pieces",
    )(pltpu.with_memory_space_constraint(panel, pltpu.HBM))


def cut_kernel(spans, panel, *refs):
    outs, (rows, sem, out_sem) = refs[:-3], refs[-3:]
    steps = []
    for i, (start, size) in enumerate(spans):
        for at in range(0, size, TILE):
            steps.append((i, start + at, at, min(TILE, size - at)))

    def load(number):
        _, row, _, size = steps[number]
        part = pl.ds(row, size)
        return pltpu.make_async_copy(panel.at[part, :], rows.at[part, :], sem.at[number])

    for number in range(len(steps)):
        load(number).start()
    for number, (i, row, at, size) in enumerate(steps):
        load(number).wait()
        pltpu.make_async_copy(rows.at[pl.ds(row, size), :], outs[i].at[pl.ds(at, size), :], out_sem.at[i]).start()
    for i, (start, size) in enumerate(spans):
        pltpu.make_async_copy(rows.at[pl.ds(start, size), :], outs[i], out_sem.at[i]).wait()


def cut(panel, spans):
    count = sum(-(-size // TILE) for _, size in spans)
    return pl.pallas_call(
        lambda *refs: cut_kernel(spans, *refs),
        out_shape=tuple(jax.ShapeDtypeStruct((size, panel.shape[1]), panel.dtype) for _, size in spans),
        in_specs=[pl.BlockSpec(memory_space=pltpu.HBM)],
        out_specs=tuple([HBM] * len(spans)),
        scratch_shapes=[
            pltpu.VMEM(panel.shape, panel.dtype),
            pltpu.SemaphoreType.DMA((count,)),
            pltpu.SemaphoreType.DMA((len(spans),)),
        ],
        compiler_params=pltpu.CompilerParams(vmem_limit_bytes=8 << 20),
        cost_estimate=SMALL,
        name="cut",
    )(pltpu.with_memory_space_constraint(panel, pltpu.HBM))


def pick_kernel(info, pivots, slab, send, keep, rows, sem, top_sem):
    copy = pltpu.make_async_copy(slab, rows, sem)
    copy.start()
    place = info[1]
    count = rows.shape[0]
    block = send.shape[0]
    first = place * count

    def fill(picked, top):
        load = pltpu.make_async_copy(slab.at[pl.ds(0, block), :], top, top_sem)

        @pl.when(place == 0)
        def _():
            load.start()

        @pl.when(place != 0)
        def _():
            top[...] = jnp.zeros_like(top)

        copy.wait()

        @pl.loop(0, block // 8)
        def _(group):
            base = pl.multiple_of(group * 8, 8)
            for j in range(8):
                row = pivots[base + j] - first
                owned = (row >= 0) & (row < count)
                value = rows[pl.ds(jnp.where(owned, row, 0), 1), :]
                picked[pl.ds(base + j, 1), :] = jnp.where(owned, value, 0.0)

        @pl.when(place == 0)
        def _():
            load.wait()

    @pl.when(place % 2 == 0)
    def _():
        fill(keep, send)

    @pl.when(place % 2 == 1)
    def _():
        fill(send, keep)


def pick(info, pivots, slab, block):
    columns = slab.shape[1]
    shape = jax.ShapeDtypeStruct((block, columns), slab.dtype)
    return pl.pallas_call(
        pick_kernel,
        out_shape=(shape, shape),
        grid_spec=pltpu.PrefetchScalarGridSpec(
            num_scalar_prefetch=2,
            grid=(),
            in_specs=[HBM],
            out_specs=(VMEM, VMEM),
            scratch_shapes=[
                pltpu.VMEM(slab.shape, slab.dtype),
                pltpu.SemaphoreType.DMA,
                pltpu.SemaphoreType.DMA,
            ],
        ),
        compiler_params=pltpu.CompilerParams(vmem_limit_bytes=16 << 20),
        cost_estimate=SMALL,
        name="pick",
    )(info, pivots, slab)


def upper_kernel(width, info, total, other, inverse, upper, terms, across_terms, last_terms):
    block = upper.shape[0]

    def fill(picked):
        upper[...] = dot(left_terms(inverse[...]), right_terms(picked[...]))

    @pl.when(info[1] % 2 == 0)
    def _():
        fill(total)

    @pl.when(info[1] % 2 == 1)
    def _():
        fill(other)

    for shard in range(4):
        value = right_terms(upper[aligned((info[0] ^ shard) * width, width), :])
        if shard == 2:
            across_terms[...] = value
        if shard < 3:
            terms[pl.ds(shard * 3 * width, 3 * width), :] = value
        else:
            last_terms[...] = value


def make_upper(info, total, other, inverse, width):
    block, columns = total.shape
    return pl.pallas_call(
        lambda *refs: upper_kernel(width, *refs),
        out_shape=(
            jax.ShapeDtypeStruct((block, columns), total.dtype),
            jax.ShapeDtypeStruct((9 * width, columns), jnp.bfloat16),
            jax.ShapeDtypeStruct((3 * width, columns), jnp.bfloat16),
            jax.ShapeDtypeStruct((3 * width, columns), jnp.bfloat16),
        ),
        grid_spec=pltpu.PrefetchScalarGridSpec(
            num_scalar_prefetch=1,
            grid=(),
            in_specs=[VMEM] * 3,
            out_specs=(VMEM, VMEM, VMEM, VMEM),
        ),
        compiler_params=pltpu.CompilerParams(vmem_limit_bytes=24 << 20),
        cost_estimate=SMALL,
        name="upper",
    )(info, total, other, inverse)


def main_kernel(tile, info, pivots, slab, total, other, own, near, *refs):
    *across, upper, terms, out, own_rows, near_rows, across_rows, sem, panel_sem = refs
    copy = pltpu.make_async_copy(slab, out, sem)
    copy.start()
    loads = [(own, own_rows), (near, near_rows)]
    at = 0
    for piece in across:
        loads.append((piece, across_rows.at[pl.ds(at, piece.shape[0]), :]))
        at += piece.shape[0]
    loads = [pltpu.make_async_copy(a, b, panel_sem.at[i]) for i, (a, b) in enumerate(loads)]
    for load in loads:
        load.start()
    place = info[1]
    count = own_rows.shape[0]
    block = upper.shape[0]
    first = place * count
    copy.wait()

    def fill(old_top):
        @pl.loop(0, block // 8)
        def _(group):
            base = pl.multiple_of(group * 8, 8)
            for j in range(8):
                row = pivots[base + j] - first
                owned = (row >= 0) & (row < count)
                place_at = pl.ds(jnp.where(owned, row, 0), 1)
                out[place_at, :] = jnp.where(owned, old_top[pl.ds(base + j, 1), :], out[place_at, :])

    @pl.when(place % 2 == 0)
    def _():
        fill(other)

    @pl.when(place % 2 == 1)
    def _():
        fill(total)

    for load in loads:
        load.wait()

    def subtract(part, panels):
        left = jnp.concatenate([left_terms(panel[part, :]) for panel in panels], axis=1)
        out[part, :] = out[part, :] - dot(left, terms[pl.ds(0, left.shape[1]), :])

    @pl.loop(0, at // tile)
    def _(t):
        part = aligned(t * tile, tile)
        subtract(part, (own_rows, near_rows, across_rows))

        @pl.when((place == 0) & (t < block // tile))
        def _():
            out[part, :] = upper[aligned(jnp.minimum(t * tile, block - tile), tile), :]

    if at % tile:
        subtract(pl.ds(at - at % tile, at % tile), (own_rows, near_rows, across_rows))
    subtract(pl.ds(at, count - at), (own_rows, near_rows))


def main_update(info, pivots, slab, total, other, own, near, across, upper, terms):
    block = upper.shape[0]
    return pl.pallas_call(
        lambda *refs: main_kernel(min(TILE, block), *refs),
        out_shape=jax.ShapeDtypeStruct(slab.shape, slab.dtype),
        grid_spec=pltpu.PrefetchScalarGridSpec(
            num_scalar_prefetch=2,
            grid=(),
            in_specs=[HBM, VMEM, VMEM, HBM, HBM] + [HBM] * len(across) + [VMEM, VMEM],
            out_specs=VMEM,
            scratch_shapes=[pltpu.VMEM(own.shape, own.dtype)] * 2
            + [pltpu.VMEM((sum(piece.shape[0] for piece in across), own.shape[1]), own.dtype)]
            + [pltpu.SemaphoreType.DMA, pltpu.SemaphoreType.DMA((2 + len(across),))],
        ),
        compiler_params=pltpu.CompilerParams(vmem_limit_bytes=32 << 20),
        cost_estimate=SMALL,
        name="main_update",
    )(info, pivots, slab, total, other, own, near, *across, upper, terms)


def last_kernel(first_row, block, tile, segments, base, *refs):
    out, result, sem = refs[-3:]
    at = 0
    for count, groups in segments:
        for inner in range(0, count, tile):
            size = min(tile, count - inner)
            part = pl.ds(at, size)
            row = first_row + at
            delta = None
            for terms, pieces in groups:
                left = sum(refs[piece][pl.ds(offset + inner, size), :] for piece, offset in pieces)
                change = dot(left_terms(left), refs[terms][...])
                delta = change if delta is None else delta + change
            if row < block:
                delta = jnp.where(lax.axis_index("prow") == 0, 0.0, delta)
            result[part, :] = base[pl.ds(row, size), :] - delta
            pltpu.make_async_copy(result.at[part, :], out.at[pl.ds(row, size), :], sem).start()
            at += size
    pltpu.make_async_copy(result, out.at[pl.ds(first_row, at), :], sem).wait()


def last_update(base, arrays, segments, block, first_row, done):
    count = sum(size for size, _ in segments)
    return pl.pallas_call(
        lambda *refs: last_kernel(first_row, block, min(LAST_TILE, block), segments, *refs),
        out_shape=jax.ShapeDtypeStruct(base.shape, base.dtype),
        in_specs=[VMEM] * (1 + len(arrays)) + [HBM] * len(done),
        out_specs=HBM,
        scratch_shapes=[pltpu.VMEM((count, base.shape[1]), base.dtype), pltpu.SemaphoreType.DMA],
        input_output_aliases={1 + len(arrays): 0} if done else {},
        compiler_params=pltpu.CompilerParams(vmem_limit_bytes=24 << 20),
        cost_estimate=SMALL,
        name="last_update",
    )(base, *arrays, *done)


def exchange(value, bit, count):
    return lax.ppermute(value, "prow", [(i, i ^ (1 << bit)) for i in range(count)])


def solution(mesh):
    row_parts, column_parts = mesh.shape["prow"], mesh.shape["pcol"]
    bits = row_parts.bit_length() - 1
    if column_parts != 4 or row_parts != 1 << bits or bits < 1:
        raise ValueError("unsupported mesh")

    def shards(panel, slab, pivots, diag_inverse):
        rows_here = slab.shape[0]
        width = panel.shape[1]
        block = diag_inverse.shape[0]
        place = lax.axis_index("prow")
        column = lax.axis_index("pcol")
        info = jnp.stack([column, place]).astype(jnp.int32)

        first, second, last = (rows_here * part // sum(PIECES) for part in PIECES)
        first_mid, second_mid, _ = (rows_here * part // sum(PIECES) for part in MIDDLE_PIECES)
        early = first + second
        near = lax.ppermute(panel, "pcol", SWAP)
        *pieces, tail = cut(panel, [(0, first), (first, second), (early, last)])
        across = [lax.ppermute(piece, "pcol", ACROSS) for piece in pieces]
        far = lax.ppermute(tail, "pcol", FAR)

        def gather_rows(slab, pivots):
            send, keep = pick(info, pivots, slab, block)
            total = keep + exchange(send, 0, row_parts)
            for bit in range(1, bits):
                total = total + exchange(total, bit, row_parts)
            return total, exchange(total, 0, row_parts)

        def no_rows(slab, pivots):
            return slab[:block], slab[:block]

        total, other = lax.cond(pivots[0] >= 0, gather_rows, no_rows, slab, pivots)
        upper, terms, across_terms, last_terms = make_upper(info, total, other, diag_inverse, width)
        later, upper = lax.optimization_barrier((panel, upper))
        head, upper = lax.optimization_barrier((across[0], upper))
        head_mid, rest_mid, tail_mid = load_pieces(
            later, [(0, first_mid), (first_mid, second_mid), (early, last)]
        )
        tail_mid = lax.ppermute(tail_mid, "pcol", MIDDLE)
        head_end = lax.ppermute(head, "pcol", ENDS)
        rest, head_mid, rest_mid, near, far = lax.optimization_barrier(
            (across[1], head_mid, rest_mid, near, far)
        )
        head_mid = lax.ppermute(head_mid, "pcol", MIDDLE)
        rest_mid = lax.ppermute(rest_mid, "pcol", MIDDLE)
        rest_end = lax.ppermute(rest, "pcol", ENDS)
        both, rest = lax.optimization_barrier((jnp.concatenate([far, tail_mid], axis=0), rest))
        both = lax.ppermute(both, "pcol", ENDS)

        base = main_update(info, pivots, slab, total, other, panel, near, [head, rest], upper, terms)
        segments = [(first_mid, [(0, [(1, 0), (2, 0)])])]
        result = last_update(base, [last_terms, head_end, head_mid], segments, block, 0, [])
        segments = [
            (first - first_mid, [(0, [(1, first_mid), (3, 0)])]),
            (second, [(0, [(2, 0), (3, first - first_mid)])]),
        ]
        arrays = [last_terms, head_end, rest_end, rest_mid]
        result = last_update(base, arrays, segments, block, first_mid, [result])
        segments = [(last, [(0, [(2, 0), (4, last)]), (1, [(3, 0), (4, 0)])])]
        arrays = [across_terms, last_terms, far, tail_mid, both]
        return last_update(base, arrays, segments, block, early, [result])

    in_specs = (P("prow", "pcol"), P("prow", "pcol"), P(), P())
    return jax.shard_map(
        shards, mesh=mesh, in_specs=in_specs, out_specs=P("prow", "pcol"), check_vma=False
    )
```

```python
import jax
import jax.numpy as jnp
from jax import lax
from jax.experimental import pallas as pl
from jax.experimental.pallas import tpu as pltpu
from jax.sharding import PartitionSpec as P

SWAP = [(0, 1), (1, 0), (2, 3), (3, 2)]
ACROSS = [(0, 2), (1, 3), (2, 0), (3, 1)]
MIDDLE = [(1, 2), (2, 1)]
ENDS = [(2, 3), (1, 0)]
FAR = [(0, 2), (3, 1)]
PIECES = (64, 46, 18)
MIDDLE_PIECES = (58, 52, 18)
TILE = 512
LAST_TILE = 256
SMALL = pl.CostEstimate(flops=0, bytes_accessed=0, transcendentals=0)
HBM = pl.BlockSpec(memory_space=pl.ANY)
VMEM = pl.BlockSpec(memory_space=pltpu.VMEM)


def split(x):
    high = x.astype(jnp.bfloat16)
    low = (x - high.astype(jnp.float32)).astype(jnp.bfloat16)
    return high, low


def left_terms(x):
    high, low = split(x)
    return jnp.concatenate([high, high, low], axis=1)


def right_terms(x):
    high, low = split(x)
    return jnp.concatenate([high, low, high], axis=0)


def dot(a, b):
    return jnp.dot(a, b, preferred_element_type=jnp.float32)


def aligned(start, size):
    return pl.ds(pl.multiple_of(start, size), size)


def load_kernel(spans, panel, *refs):
    outs, sem = refs[:-1], refs[-1]
    copies = [
        pltpu.make_async_copy(panel.at[pl.ds(start, size), :], out, sem.at[i])
        for i, ((start, size), out) in enumerate(zip(spans, outs))
    ]
    for copy in copies:
        copy.start()
    for copy in copies:
        copy.wait()


def load_pieces(panel, spans):
    return pl.pallas_call(
        lambda *refs: load_kernel(spans, *refs),
        out_shape=tuple(jax.ShapeDtypeStruct((size, panel.shape[1]), panel.dtype) for _, size in spans),
        in_specs=[pl.BlockSpec(memory_space=pltpu.HBM)],
        out_specs=tuple([VMEM] * len(spans)),
        scratch_shapes=[pltpu.SemaphoreType.DMA((len(spans),))],
        compiler_params=pltpu.CompilerParams(vmem_limit_bytes=8 << 20),
        cost_estimate=SMALL,
        name="load_pieces",
    )(pltpu.with_memory_space_constraint(panel, pltpu.HBM))


def cut_kernel(spans, panel, *refs):
    outs, (rows, sem, out_sem) = refs[:-3], refs[-3:]
    steps = []
    for i, (start, size) in enumerate(spans):
        for at in range(0, size, TILE):
            steps.append((i, start + at, at, min(TILE, size - at)))

    def load(number):
        _, row, _, size = steps[number]
        part = pl.ds(row, size)
        return pltpu.make_async_copy(panel.at[part, :], rows.at[part, :], sem.at[number])

    for number in range(len(steps)):
        load(number).start()
    for number, (i, row, at, size) in enumerate(steps):
        load(number).wait()
        pltpu.make_async_copy(rows.at[pl.ds(row, size), :], outs[i].at[pl.ds(at, size), :], out_sem.at[i]).start()
    for i, (start, size) in enumerate(spans):
        pltpu.make_async_copy(rows.at[pl.ds(start, size), :], outs[i], out_sem.at[i]).wait()


def cut(panel, spans):
    count = sum(-(-size // TILE) for _, size in spans)
    return pl.pallas_call(
        lambda *refs: cut_kernel(spans, *refs),
        out_shape=tuple(jax.ShapeDtypeStruct((size, panel.shape[1]), panel.dtype) for _, size in spans),
        in_specs=[pl.BlockSpec(memory_space=pltpu.HBM)],
        out_specs=tuple([HBM] * len(spans)),
        scratch_shapes=[
            pltpu.VMEM(panel.shape, panel.dtype),
            pltpu.SemaphoreType.DMA((count,)),
            pltpu.SemaphoreType.DMA((len(spans),)),
        ],
        compiler_params=pltpu.CompilerParams(vmem_limit_bytes=8 << 20),
        cost_estimate=SMALL,
        name="cut",
    )(pltpu.with_memory_space_constraint(panel, pltpu.HBM))


def pick_kernel(info, pivots, slab, send, keep, rows, sem, top_sem):
    copy = pltpu.make_async_copy(slab, rows, sem)
    copy.start()
    place = info[1]
    count = rows.shape[0]
    block = send.shape[0]
    first = place * count

    def fill(picked, top):
        load = pltpu.make_async_copy(slab.at[pl.ds(0, block), :], top, top_sem)

        @pl.when(place == 0)
        def _():
            load.start()

        @pl.when(place != 0)
        def _():
            top[...] = jnp.zeros_like(top)

        copy.wait()

        @pl.loop(0, block // 8)
        def _(group):
            base = pl.multiple_of(group * 8, 8)
            for j in range(8):
                row = pivots[base + j] - first
                owned = (row >= 0) & (row < count)
                value = rows[pl.ds(jnp.where(owned, row, 0), 1), :]
                picked[pl.ds(base + j, 1), :] = jnp.where(owned, value, 0.0)

        @pl.when(place == 0)
        def _():
            load.wait()

    @pl.when(place % 2 == 0)
    def _():
        fill(keep, send)

    @pl.when(place % 2 == 1)
    def _():
        fill(send, keep)


def pick(info, pivots, slab, block):
    columns = slab.shape[1]
    shape = jax.ShapeDtypeStruct((block, columns), slab.dtype)
    return pl.pallas_call(
        pick_kernel,
        out_shape=(shape, shape),
        grid_spec=pltpu.PrefetchScalarGridSpec(
            num_scalar_prefetch=2,
            grid=(),
            in_specs=[HBM],
            out_specs=(VMEM, VMEM),
            scratch_shapes=[
                pltpu.VMEM(slab.shape, slab.dtype),
                pltpu.SemaphoreType.DMA,
                pltpu.SemaphoreType.DMA,
            ],
        ),
        compiler_params=pltpu.CompilerParams(vmem_limit_bytes=16 << 20),
        cost_estimate=SMALL,
        name="pick",
    )(info, pivots, slab)


def upper_kernel(width, info, total, other, inverse, upper, terms, across_terms, last_terms):
    block = upper.shape[0]

    def fill(picked):
        upper[...] = dot(left_terms(inverse[...]), right_terms(picked[...]))

    @pl.when(info[1] % 2 == 0)
    def _():
        fill(total)

    @pl.when(info[1] % 2 == 1)
    def _():
        fill(other)

    for shard in range(4):
        value = right_terms(upper[aligned((info[0] ^ shard) * width, width), :])
        if shard == 2:
            across_terms[...] = value
        if shard < 3:
            terms[pl.ds(shard * 3 * width, 3 * width), :] = value
        else:
            last_terms[...] = value


def make_upper(info, total, other, inverse, width):
    block, columns = total.shape
    return pl.pallas_call(
        lambda *refs: upper_kernel(width, *refs),
        out_shape=(
            jax.ShapeDtypeStruct((block, columns), total.dtype),
            jax.ShapeDtypeStruct((9 * width, columns), jnp.bfloat16),
            jax.ShapeDtypeStruct((3 * width, columns), jnp.bfloat16),
            jax.ShapeDtypeStruct((3 * width, columns), jnp.bfloat16),
        ),
        grid_spec=pltpu.PrefetchScalarGridSpec(
            num_scalar_prefetch=1,
            grid=(),
            in_specs=[VMEM] * 3,
            out_specs=(VMEM, VMEM, VMEM, VMEM),
        ),
        compiler_params=pltpu.CompilerParams(vmem_limit_bytes=24 << 20),
        cost_estimate=SMALL,
        name="upper",
    )(info, total, other, inverse)


def main_kernel(tile, info, pivots, slab, total, other, own, near, *refs):
    *across, upper, terms, out, own_rows, near_rows, across_rows, sem, panel_sem = refs
    copy = pltpu.make_async_copy(slab, out, sem)
    copy.start()
    loads = [(own, own_rows), (near, near_rows)]
    at = 0
    for piece in across:
        loads.append((piece, across_rows.at[pl.ds(at, piece.shape[0]), :]))
        at += piece.shape[0]
    loads = [pltpu.make_async_copy(a, b, panel_sem.at[i]) for i, (a, b) in enumerate(loads)]
    for load in loads:
        load.start()
    place = info[1]
    count = own_rows.shape[0]
    block = upper.shape[0]
    first = place * count
    copy.wait()

    def fill(old_top):
        @pl.loop(0, block // 8)
        def _(group):
            base = pl.multiple_of(group * 8, 8)
            for j in range(8):
                row = pivots[base + j] - first
                owned = (row >= 0) & (row < count)
                place_at = pl.ds(jnp.where(owned, row, 0), 1)
                out[place_at, :] = jnp.where(owned, old_top[pl.ds(base + j, 1), :], out[place_at, :])

    @pl.when(place % 2 == 0)
    def _():
        fill(other)

    @pl.when(place % 2 == 1)
    def _():
        fill(total)

    for load in loads:
        load.wait()

    def subtract(part, panels):
        left = jnp.concatenate([left_terms(panel[part, :]) for panel in panels], axis=1)
        out[part, :] = out[part, :] - dot(left, terms[pl.ds(0, left.shape[1]), :])

    @pl.loop(0, at // tile)
    def _(t):
        part = aligned(t * tile, tile)
        subtract(part, (own_rows, near_rows, across_rows))

        @pl.when((place == 0) & (t < block // tile))
        def _():
            out[part, :] = upper[aligned(jnp.minimum(t * tile, block - tile), tile), :]

    if at % tile:
        subtract(pl.ds(at - at % tile, at % tile), (own_rows, near_rows, across_rows))
    subtract(pl.ds(at, count - at), (own_rows, near_rows))


def main_update(info, pivots, slab, total, other, own, near, across, upper, terms):
    block = upper.shape[0]
    return pl.pallas_call(
        lambda *refs: main_kernel(min(TILE, block), *refs),
        out_shape=jax.ShapeDtypeStruct(slab.shape, slab.dtype),
        grid_spec=pltpu.PrefetchScalarGridSpec(
            num_scalar_prefetch=2,
            grid=(),
            in_specs=[HBM, VMEM, VMEM, HBM, HBM] + [HBM] * len(across) + [VMEM, VMEM],
            out_specs=VMEM,
            scratch_shapes=[pltpu.VMEM(own.shape, own.dtype)] * 2
            + [pltpu.VMEM((sum(piece.shape[0] for piece in across), own.shape[1]), own.dtype)]
            + [pltpu.SemaphoreType.DMA, pltpu.SemaphoreType.DMA((2 + len(across),))],
        ),
        compiler_params=pltpu.CompilerParams(vmem_limit_bytes=32 << 20),
        cost_estimate=SMALL,
        name="main_update",
    )(info, pivots, slab, total, other, own, near, *across, upper, terms)


def last_kernel(first_row, block, tile, segments, base, *refs):
    out, result, sem = refs[-3:]
    at = 0
    for count, groups in segments:
        for inner in range(0, count, tile):
            size = min(tile, count - inner)
            part = pl.ds(at, size)
            row = first_row + at
            delta = None
            for terms, pieces in groups:
                left = sum(refs[piece][pl.ds(offset + inner, size), :] for piece, offset in pieces)
                change = dot(left_terms(left), refs[terms][...])
                delta = change if delta is None else delta + change
            if row < block:
                delta = jnp.where(lax.axis_index("prow") == 0, 0.0, delta)
            result[part, :] = base[pl.ds(row, size), :] - delta
            pltpu.make_async_copy(result.at[part, :], out.at[pl.ds(row, size), :], sem).start()
            at += size
    pltpu.make_async_copy(result, out.at[pl.ds(first_row, at), :], sem).wait()


def last_update(base, arrays, segments, block, first_row, done):
    count = sum(size for size, _ in segments)
    return pl.pallas_call(
        lambda *refs: last_kernel(first_row, block, min(LAST_TILE, block), segments, *refs),
        out_shape=jax.ShapeDtypeStruct(base.shape, base.dtype),
        in_specs=[VMEM] * (1 + len(arrays)) + [HBM] * len(done),
        out_specs=HBM,
        scratch_shapes=[pltpu.VMEM((count, base.shape[1]), base.dtype), pltpu.SemaphoreType.DMA],
        input_output_aliases={1 + len(arrays): 0} if done else {},
        compiler_params=pltpu.CompilerParams(vmem_limit_bytes=24 << 20),
        cost_estimate=SMALL,
        name="last_update",
    )(base, *arrays, *done)


def exchange(value, bit, count):
    return lax.ppermute(value, "prow", [(i, i ^ (1 << bit)) for i in range(count)])


def solution(mesh):
    row_parts, column_parts = mesh.shape["prow"], mesh.shape["pcol"]
    bits = row_parts.bit_length() - 1
    if column_parts != 4 or row_parts != 1 << bits or bits < 1:
        raise ValueError("unsupported mesh")

    def shards(panel, slab, pivots, diag_inverse):
        rows_here = slab.shape[0]
        width = panel.shape[1]
        block = diag_inverse.shape[0]
        place = lax.axis_index("prow")
        column = lax.axis_index("pcol")
        info = jnp.stack([column, place]).astype(jnp.int32)

        first, second, last = (rows_here * part // sum(PIECES) for part in PIECES)
        first_mid, second_mid, _ = (rows_here * part // sum(PIECES) for part in MIDDLE_PIECES)
        early = first + second
        near = lax.ppermute(panel, "pcol", SWAP)
        *pieces, tail = cut(panel, [(0, first), (first, second), (early, last)])
        across = [lax.ppermute(piece, "pcol", ACROSS) for piece in pieces]
        far = lax.ppermute(tail, "pcol", FAR)

        def gather_rows(slab, pivots):
            send, keep = pick(info, pivots, slab, block)
            total = keep + exchange(send, 0, row_parts)
            halves = [total[: block // 2], total[block // 2 :]]
            orders = [list(range(1, bits)), list(range(1, bits))[::-1]]
            for step in range(bits - 1):
                other = [exchange(half, order[step], row_parts) for half, order in zip(halves, orders)]
                halves = [half + part for half, part in zip(halves, other)]
            total = jnp.concatenate(halves, axis=0)
            return total, exchange(total, 0, row_parts)

        def no_rows(slab, pivots):
            return slab[:block], slab[:block]

        total, other = lax.cond(pivots[0] >= 0, gather_rows, no_rows, slab, pivots)
        upper, terms, across_terms, last_terms = make_upper(info, total, other, diag_inverse, width)
        later, upper = lax.optimization_barrier((panel, upper))
        head, upper = lax.optimization_barrier((across[0], upper))
        head_mid, rest_mid, tail_mid = load_pieces(
            later, [(0, first_mid), (first_mid, second_mid), (early, last)]
        )
        tail_mid = lax.ppermute(tail_mid, "pcol", MIDDLE)
        head_end = lax.ppermute(head, "pcol", ENDS)
        rest, head_mid, near = lax.optimization_barrier((across[1], head_mid, near))
        rest_mid, far, near = lax.optimization_barrier((rest_mid, far, near))
        head_mid = lax.ppermute(head_mid, "pcol", MIDDLE)
        rest_mid = lax.ppermute(rest_mid, "pcol", MIDDLE)
        rest_end = lax.ppermute(rest, "pcol", ENDS)
        both, rest = lax.optimization_barrier((jnp.concatenate([far, tail_mid], axis=0), rest))
        both = lax.ppermute(both, "pcol", ENDS)

        base = main_update(info, pivots, slab, total, other, panel, near, [head, rest], upper, terms)
        segments = [(first_mid, [(0, [(1, 0), (2, 0)])])]
        result = last_update(base, [last_terms, head_end, head_mid], segments, block, 0, [])
        segments = [
            (first - first_mid, [(0, [(1, first_mid), (3, 0)])]),
            (second, [(0, [(2, 0), (3, first - first_mid)])]),
        ]
        arrays = [last_terms, head_end, rest_end, rest_mid]
        result = last_update(base, arrays, segments, block, first_mid, [result])
        segments = [(last, [(0, [(2, 0), (4, last)]), (1, [(3, 0), (4, 0)])])]
        arrays = [across_terms, last_terms, far, tail_mid, both]
        return last_update(base, arrays, segments, block, early, [result])

    in_specs = (P("prow", "pcol"), P("prow", "pcol"), P(), P())
    return jax.shard_map(
        shards, mesh=mesh, in_specs=in_specs, out_specs=P("prow", "pcol"), check_vma=False
    )
```

```python
import jax
import jax.numpy as jnp
from jax import lax
from jax.experimental import pallas as pl
from jax.experimental.pallas import tpu as pltpu
from jax.sharding import PartitionSpec as P

SWAP = [(0, 1), (1, 0), (2, 3), (3, 2)]
ACROSS = [(0, 2), (1, 3), (2, 0), (3, 1)]
MIDDLE = [(1, 2), (2, 1)]
ENDS = [(2, 3), (1, 0)]
FAR = [(0, 2), (3, 1)]
PIECES = (88, 12, 28)
MIDDLE_PIECES = (84, 16, 28)
TILE = 512
LAST_TILE = 256
SMALL = pl.CostEstimate(flops=0, bytes_accessed=0, transcendentals=0)
HBM = pl.BlockSpec(memory_space=pl.ANY)
VMEM = pl.BlockSpec(memory_space=pltpu.VMEM)


def split(x):
    high = x.astype(jnp.bfloat16)
    low = (x - high.astype(jnp.float32)).astype(jnp.bfloat16)
    return high, low


def left_terms(x):
    high, low = split(x)
    return jnp.concatenate([high, high, low], axis=1)


def right_terms(x):
    high, low = split(x)
    return jnp.concatenate([high, low, high], axis=0)


def dot(a, b):
    return jnp.dot(a, b, preferred_element_type=jnp.float32)


def aligned(start, size):
    return pl.ds(pl.multiple_of(start, size), size)


def load_kernel(spans, panel, *refs):
    outs, sem = refs[:-1], refs[-1]
    copies = [
        pltpu.make_async_copy(panel.at[pl.ds(start, size), :], out, sem.at[i])
        for i, ((start, size), out) in enumerate(zip(spans, outs))
    ]
    for copy in copies:
        copy.start()
    for copy in copies:
        copy.wait()


def load_pieces(panel, spans):
    return pl.pallas_call(
        lambda *refs: load_kernel(spans, *refs),
        out_shape=tuple(jax.ShapeDtypeStruct((size, panel.shape[1]), panel.dtype) for _, size in spans),
        in_specs=[pl.BlockSpec(memory_space=pltpu.HBM)],
        out_specs=tuple([VMEM] * len(spans)),
        scratch_shapes=[pltpu.SemaphoreType.DMA((len(spans),))],
        compiler_params=pltpu.CompilerParams(vmem_limit_bytes=8 << 20),
        cost_estimate=SMALL,
        name="load_pieces",
    )(pltpu.with_memory_space_constraint(panel, pltpu.HBM))


def cut_kernel(spans, panel, *refs):
    outs, (rows, sem, out_sem) = refs[:-3], refs[-3:]
    steps = []
    for i, (start, size) in enumerate(spans):
        for at in range(0, size, TILE):
            steps.append((i, start + at, at, min(TILE, size - at)))

    def load(number):
        _, row, _, size = steps[number]
        part = pl.ds(row, size)
        return pltpu.make_async_copy(panel.at[part, :], rows.at[part, :], sem.at[number])

    for number in range(len(steps)):
        load(number).start()
    for number, (i, row, at, size) in enumerate(steps):
        load(number).wait()
        pltpu.make_async_copy(rows.at[pl.ds(row, size), :], outs[i].at[pl.ds(at, size), :], out_sem.at[i]).start()
    for i, (start, size) in enumerate(spans):
        pltpu.make_async_copy(rows.at[pl.ds(start, size), :], outs[i], out_sem.at[i]).wait()


def cut(panel, spans):
    count = sum(-(-size // TILE) for _, size in spans)
    return pl.pallas_call(
        lambda *refs: cut_kernel(spans, *refs),
        out_shape=tuple(jax.ShapeDtypeStruct((size, panel.shape[1]), panel.dtype) for _, size in spans),
        in_specs=[pl.BlockSpec(memory_space=pltpu.HBM)],
        out_specs=tuple([HBM] * len(spans)),
        scratch_shapes=[
            pltpu.VMEM(panel.shape, panel.dtype),
            pltpu.SemaphoreType.DMA((count,)),
            pltpu.SemaphoreType.DMA((len(spans),)),
        ],
        compiler_params=pltpu.CompilerParams(vmem_limit_bytes=8 << 20),
        cost_estimate=SMALL,
        name="cut",
    )(pltpu.with_memory_space_constraint(panel, pltpu.HBM))


def pick_kernel(info, pivots, slab, send, keep, rows, sem, top_sem):
    copy = pltpu.make_async_copy(slab, rows, sem)
    copy.start()
    place = info[1]
    count = rows.shape[0]
    block = send.shape[0]
    first = place * count

    def fill(picked, top):
        load = pltpu.make_async_copy(slab.at[pl.ds(0, block), :], top, top_sem)

        @pl.when(place == 0)
        def _():
            load.start()

        @pl.when(place != 0)
        def _():
            top[...] = jnp.zeros_like(top)

        copy.wait()

        @pl.loop(0, block // 8)
        def _(group):
            base = pl.multiple_of(group * 8, 8)
            for j in range(8):
                row = pivots[base + j] - first
                owned = (row >= 0) & (row < count)
                value = rows[pl.ds(jnp.where(owned, row, 0), 1), :]
                picked[pl.ds(base + j, 1), :] = jnp.where(owned, value, 0.0)

        @pl.when(place == 0)
        def _():
            load.wait()

    @pl.when(place % 2 == 0)
    def _():
        fill(keep, send)

    @pl.when(place % 2 == 1)
    def _():
        fill(send, keep)


def pick(info, pivots, slab, block):
    columns = slab.shape[1]
    shape = jax.ShapeDtypeStruct((block, columns), slab.dtype)
    return pl.pallas_call(
        pick_kernel,
        out_shape=(shape, shape),
        grid_spec=pltpu.PrefetchScalarGridSpec(
            num_scalar_prefetch=2,
            grid=(),
            in_specs=[HBM],
            out_specs=(VMEM, VMEM),
            scratch_shapes=[
                pltpu.VMEM(slab.shape, slab.dtype),
                pltpu.SemaphoreType.DMA,
                pltpu.SemaphoreType.DMA,
            ],
        ),
        compiler_params=pltpu.CompilerParams(vmem_limit_bytes=16 << 20),
        cost_estimate=SMALL,
        name="pick",
    )(info, pivots, slab)


def upper_kernel(width, info, total, other, inverse, upper, terms, across_terms, last_terms):
    block = upper.shape[0]

    def fill(picked):
        upper[...] = dot(left_terms(inverse[...]), right_terms(picked[...]))

    @pl.when(info[1] % 2 == 0)
    def _():
        fill(total)

    @pl.when(info[1] % 2 == 1)
    def _():
        fill(other)

    for shard in range(4):
        value = right_terms(upper[aligned((info[0] ^ shard) * width, width), :])
        if shard == 2:
            across_terms[...] = value
        if shard < 3:
            terms[pl.ds(shard * 3 * width, 3 * width), :] = value
        else:
            last_terms[...] = value


def make_upper(info, total, other, inverse, width):
    block, columns = total.shape
    return pl.pallas_call(
        lambda *refs: upper_kernel(width, *refs),
        out_shape=(
            jax.ShapeDtypeStruct((block, columns), total.dtype),
            jax.ShapeDtypeStruct((9 * width, columns), jnp.bfloat16),
            jax.ShapeDtypeStruct((3 * width, columns), jnp.bfloat16),
            jax.ShapeDtypeStruct((3 * width, columns), jnp.bfloat16),
        ),
        grid_spec=pltpu.PrefetchScalarGridSpec(
            num_scalar_prefetch=1,
            grid=(),
            in_specs=[VMEM] * 3,
            out_specs=(VMEM, VMEM, VMEM, VMEM),
        ),
        compiler_params=pltpu.CompilerParams(vmem_limit_bytes=24 << 20),
        cost_estimate=SMALL,
        name="upper",
    )(info, total, other, inverse)


def main_kernel(tile, info, pivots, slab, total, other, own, near, *refs):
    *across, upper, terms, out, own_rows, near_rows, across_rows, sem, panel_sem = refs
    copy = pltpu.make_async_copy(slab, out, sem)
    copy.start()
    loads = [(own, own_rows), (near, near_rows)]
    at = 0
    for piece in across:
        loads.append((piece, across_rows.at[pl.ds(at, piece.shape[0]), :]))
        at += piece.shape[0]
    loads = [pltpu.make_async_copy(a, b, panel_sem.at[i]) for i, (a, b) in enumerate(loads)]
    for load in loads:
        load.start()
    place = info[1]
    count = own_rows.shape[0]
    block = upper.shape[0]
    first = place * count
    copy.wait()

    def fill(old_top):
        @pl.loop(0, block // 8)
        def _(group):
            base = pl.multiple_of(group * 8, 8)
            for j in range(8):
                row = pivots[base + j] - first
                owned = (row >= 0) & (row < count)
                place_at = pl.ds(jnp.where(owned, row, 0), 1)
                out[place_at, :] = jnp.where(owned, old_top[pl.ds(base + j, 1), :], out[place_at, :])

    @pl.when(place % 2 == 0)
    def _():
        fill(other)

    @pl.when(place % 2 == 1)
    def _():
        fill(total)

    for load in loads:
        load.wait()

    def subtract(part, panels):
        left = jnp.concatenate([left_terms(panel[part, :]) for panel in panels], axis=1)
        out[part, :] = out[part, :] - dot(left, terms[pl.ds(0, left.shape[1]), :])

    @pl.loop(0, at // tile)
    def _(t):
        part = aligned(t * tile, tile)
        subtract(part, (own_rows, near_rows, across_rows))

        @pl.when((place == 0) & (t < block // tile))
        def _():
            out[part, :] = upper[aligned(jnp.minimum(t * tile, block - tile), tile), :]

    if at % tile:
        subtract(pl.ds(at - at % tile, at % tile), (own_rows, near_rows, across_rows))
    subtract(pl.ds(at, count - at), (own_rows, near_rows))


def main_update(info, pivots, slab, total, other, own, near, across, upper, terms):
    block = upper.shape[0]
    return pl.pallas_call(
        lambda *refs: main_kernel(min(TILE, block), *refs),
        out_shape=jax.ShapeDtypeStruct(slab.shape, slab.dtype),
        grid_spec=pltpu.PrefetchScalarGridSpec(
            num_scalar_prefetch=2,
            grid=(),
            in_specs=[HBM, VMEM, VMEM, HBM, HBM] + [HBM] * len(across) + [VMEM, VMEM],
            out_specs=VMEM,
            scratch_shapes=[pltpu.VMEM(own.shape, own.dtype)] * 2
            + [pltpu.VMEM((sum(piece.shape[0] for piece in across), own.shape[1]), own.dtype)]
            + [pltpu.SemaphoreType.DMA, pltpu.SemaphoreType.DMA((2 + len(across),))],
        ),
        compiler_params=pltpu.CompilerParams(vmem_limit_bytes=32 << 20),
        cost_estimate=SMALL,
        name="main_update",
    )(info, pivots, slab, total, other, own, near, *across, upper, terms)


def last_kernel(first_row, block, tile, segments, base, *refs):
    out, result, sem = refs[-3:]
    at = 0
    for count, groups in segments:
        for inner in range(0, count, tile):
            size = min(tile, count - inner)
            part = pl.ds(at, size)
            row = first_row + at
            delta = None
            for terms, pieces in groups:
                left = sum(refs[piece][pl.ds(offset + inner, size), :] for piece, offset in pieces)
                change = dot(left_terms(left), refs[terms][...])
                delta = change if delta is None else delta + change
            if row < block:
                delta = jnp.where(lax.axis_index("prow") == 0, 0.0, delta)
            result[part, :] = base[pl.ds(row, size), :] - delta
            pltpu.make_async_copy(result.at[part, :], out.at[pl.ds(row, size), :], sem).start()
            at += size
    pltpu.make_async_copy(result, out.at[pl.ds(first_row, at), :], sem).wait()


def last_update(base, arrays, segments, block, first_row, done):
    count = sum(size for size, _ in segments)
    return pl.pallas_call(
        lambda *refs: last_kernel(first_row, block, min(LAST_TILE, block), segments, *refs),
        out_shape=jax.ShapeDtypeStruct(base.shape, base.dtype),
        in_specs=[VMEM] * (1 + len(arrays)) + [HBM] * len(done),
        out_specs=HBM,
        scratch_shapes=[pltpu.VMEM((count, base.shape[1]), base.dtype), pltpu.SemaphoreType.DMA],
        input_output_aliases={1 + len(arrays): 0} if done else {},
        compiler_params=pltpu.CompilerParams(vmem_limit_bytes=24 << 20),
        cost_estimate=SMALL,
        name="last_update",
    )(base, *arrays, *done)


def exchange(value, bit, count):
    return lax.ppermute(value, "prow", [(i, i ^ (1 << bit)) for i in range(count)])


def solution(mesh):
    row_parts, column_parts = mesh.shape["prow"], mesh.shape["pcol"]
    bits = row_parts.bit_length() - 1
    if column_parts != 4 or row_parts != 1 << bits or bits < 1:
        raise ValueError("unsupported mesh")

    def shards(panel, slab, pivots, diag_inverse):
        rows_here = slab.shape[0]
        width = panel.shape[1]
        block = diag_inverse.shape[0]
        place = lax.axis_index("prow")
        column = lax.axis_index("pcol")
        info = jnp.stack([column, place]).astype(jnp.int32)

        first, second, last = (rows_here * part // sum(PIECES) for part in PIECES)
        first_mid, second_mid, _ = (rows_here * part // sum(PIECES) for part in MIDDLE_PIECES)
        early = first + second
        near = lax.ppermute(panel, "pcol", SWAP)
        *pieces, tail = cut(panel, [(0, first), (first, second), (early, last)])
        across = [lax.ppermute(piece, "pcol", ACROSS) for piece in pieces]
        far = lax.ppermute(tail, "pcol", FAR)

        def gather_rows(slab, pivots):
            send, keep = pick(info, pivots, slab, block)
            total = keep + exchange(send, 0, row_parts)
            halves = [total[: block // 2], total[block // 2 :]]
            orders = [list(range(1, bits)), list(range(1, bits))[::-1]]
            for step in range(bits - 1):
                other = [exchange(half, order[step], row_parts) for half, order in zip(halves, orders)]
                halves = [half + part for half, part in zip(halves, other)]
            total = jnp.concatenate(halves, axis=0)
            return total, exchange(total, 0, row_parts)

        def no_rows(slab, pivots):
            return slab[:block], slab[:block]

        total, other = lax.cond(pivots[0] >= 0, gather_rows, no_rows, slab, pivots)
        upper, terms, across_terms, last_terms = make_upper(info, total, other, diag_inverse, width)
        later, upper = lax.optimization_barrier((panel, upper))
        head, upper = lax.optimization_barrier((across[0], upper))
        head_mid, rest_mid, tail_mid = load_pieces(
            later, [(0, first_mid), (first_mid, second_mid), (early, last)]
        )
        tail_mid = lax.ppermute(tail_mid, "pcol", MIDDLE)
        head_end = lax.ppermute(head, "pcol", ENDS)
        rest, head_mid, near = lax.optimization_barrier((across[1], head_mid, near))
        rest_mid, far, near = lax.optimization_barrier((rest_mid, far, near))
        head_mid = lax.ppermute(head_mid, "pcol", MIDDLE)
        rest_mid = lax.ppermute(rest_mid, "pcol", MIDDLE)
        rest_end = lax.ppermute(rest, "pcol", ENDS)
        both, rest = lax.optimization_barrier((jnp.concatenate([far, tail_mid], axis=0), rest))
        both = lax.ppermute(both, "pcol", ENDS)

        base = main_update(info, pivots, slab, total, other, panel, near, [head, rest], upper, terms)
        segments = [(first_mid, [(0, [(1, 0), (2, 0)])])]
        result = last_update(base, [last_terms, head_end, head_mid], segments, block, 0, [])
        segments = [(last, [(0, [(2, 0), (4, last)]), (1, [(3, 0), (4, 0)])])]
        arrays = [across_terms, last_terms, far, tail_mid, both]
        result = last_update(base, arrays, segments, block, early, [result])
        segments = [
            (first - first_mid, [(0, [(1, first_mid), (3, 0)])]),
            (second, [(0, [(2, 0), (3, first - first_mid)])]),
        ]
        arrays = [last_terms, head_end, rest_end, rest_mid]
        return last_update(base, arrays, segments, block, first_mid, [result])

    in_specs = (P("prow", "pcol"), P("prow", "pcol"), P(), P())
    return jax.shard_map(
        shards, mesh=mesh, in_specs=in_specs, out_specs=P("prow", "pcol"), check_vma=False
    )
```

```python
import jax
import jax.numpy as jnp
from jax import lax
from jax.experimental import pallas as pl
from jax.experimental.pallas import tpu as pltpu
from jax.sharding import PartitionSpec as P

SWAP = [(0, 1), (1, 0), (2, 3), (3, 2)]
ACROSS = [(0, 2), (1, 3), (2, 0), (3, 1)]
MIDDLE = [(1, 2), (2, 1)]
ENDS = [(2, 3), (1, 0)]
FAR = [(0, 2), (3, 1)]
PIECES = (76, 28, 24)
MIDDLE_PIECES = (72, 32, 24)
TILE = 512
LAST_TILE = 256
SMALL = pl.CostEstimate(flops=0, bytes_accessed=0, transcendentals=0)
HBM = pl.BlockSpec(memory_space=pl.ANY)
VMEM = pl.BlockSpec(memory_space=pltpu.VMEM)


def split(x):
    high = x.astype(jnp.bfloat16)
    low = (x - high.astype(jnp.float32)).astype(jnp.bfloat16)
    return high, low


def left_terms(x):
    high, low = split(x)
    return jnp.concatenate([high, high, low], axis=1)


def right_terms(x):
    high, low = split(x)
    return jnp.concatenate([high, low, high], axis=0)


def dot(a, b):
    return jnp.dot(a, b, preferred_element_type=jnp.float32)


def aligned(start, size):
    return pl.ds(pl.multiple_of(start, size), size)


def load_kernel(spans, panel, *refs):
    outs, sem = refs[:-1], refs[-1]
    copies = [
        pltpu.make_async_copy(panel.at[pl.ds(start, size), :], out, sem.at[i])
        for i, ((start, size), out) in enumerate(zip(spans, outs))
    ]
    for copy in copies:
        copy.start()
    for copy in copies:
        copy.wait()


def load_pieces(panel, spans):
    return pl.pallas_call(
        lambda *refs: load_kernel(spans, *refs),
        out_shape=tuple(jax.ShapeDtypeStruct((size, panel.shape[1]), panel.dtype) for _, size in spans),
        in_specs=[pl.BlockSpec(memory_space=pltpu.HBM)],
        out_specs=tuple([VMEM] * len(spans)),
        scratch_shapes=[pltpu.SemaphoreType.DMA((len(spans),))],
        compiler_params=pltpu.CompilerParams(vmem_limit_bytes=8 << 20),
        cost_estimate=SMALL,
        name="load_pieces",
    )(pltpu.with_memory_space_constraint(panel, pltpu.HBM))


def cut_kernel(spans, panel, *refs):
    outs, (rows, sem, out_sem) = refs[:-3], refs[-3:]
    steps = []
    for i, (start, size) in enumerate(spans):
        for at in range(0, size, TILE):
            steps.append((i, start + at, at, min(TILE, size - at)))

    def load(number):
        _, row, _, size = steps[number]
        part = pl.ds(row, size)
        return pltpu.make_async_copy(panel.at[part, :], rows.at[part, :], sem.at[number])

    for number in range(len(steps)):
        load(number).start()
    for number, (i, row, at, size) in enumerate(steps):
        load(number).wait()
        pltpu.make_async_copy(rows.at[pl.ds(row, size), :], outs[i].at[pl.ds(at, size), :], out_sem.at[i]).start()
    for i, (start, size) in enumerate(spans):
        pltpu.make_async_copy(rows.at[pl.ds(start, size), :], outs[i], out_sem.at[i]).wait()


def cut(panel, spans):
    count = sum(-(-size // TILE) for _, size in spans)
    return pl.pallas_call(
        lambda *refs: cut_kernel(spans, *refs),
        out_shape=tuple(jax.ShapeDtypeStruct((size, panel.shape[1]), panel.dtype) for _, size in spans),
        in_specs=[pl.BlockSpec(memory_space=pltpu.HBM)],
        out_specs=tuple([HBM] * len(spans)),
        scratch_shapes=[
            pltpu.VMEM(panel.shape, panel.dtype),
            pltpu.SemaphoreType.DMA((count,)),
            pltpu.SemaphoreType.DMA((len(spans),)),
        ],
        compiler_params=pltpu.CompilerParams(vmem_limit_bytes=8 << 20),
        cost_estimate=SMALL,
        name="cut",
    )(pltpu.with_memory_space_constraint(panel, pltpu.HBM))


def pick_kernel(info, pivots, slab, send, keep, rows, sem, top_sem):
    copy = pltpu.make_async_copy(slab, rows, sem)
    copy.start()
    place = info[1]
    count = rows.shape[0]
    block = send.shape[0]
    first = place * count

    def fill(picked, top):
        load = pltpu.make_async_copy(slab.at[pl.ds(0, block), :], top, top_sem)

        @pl.when(place == 0)
        def _():
            load.start()

        @pl.when(place != 0)
        def _():
            top[...] = jnp.zeros_like(top)

        copy.wait()

        @pl.loop(0, block // 8)
        def _(group):
            base = pl.multiple_of(group * 8, 8)
            for j in range(8):
                row = pivots[base + j] - first
                owned = (row >= 0) & (row < count)
                value = rows[pl.ds(jnp.where(owned, row, 0), 1), :]
                picked[pl.ds(base + j, 1), :] = jnp.where(owned, value, 0.0)

        @pl.when(place == 0)
        def _():
            load.wait()

    @pl.when(place % 2 == 0)
    def _():
        fill(keep, send)

    @pl.when(place % 2 == 1)
    def _():
        fill(send, keep)


def pick(info, pivots, slab, block):
    columns = slab.shape[1]
    shape = jax.ShapeDtypeStruct((block, columns), slab.dtype)
    return pl.pallas_call(
        pick_kernel,
        out_shape=(shape, shape),
        grid_spec=pltpu.PrefetchScalarGridSpec(
            num_scalar_prefetch=2,
            grid=(),
            in_specs=[HBM],
            out_specs=(VMEM, VMEM),
            scratch_shapes=[
                pltpu.VMEM(slab.shape, slab.dtype),
                pltpu.SemaphoreType.DMA,
                pltpu.SemaphoreType.DMA,
            ],
        ),
        compiler_params=pltpu.CompilerParams(vmem_limit_bytes=16 << 20),
        cost_estimate=SMALL,
        name="pick",
    )(info, pivots, slab)


def upper_kernel(width, info, total, other, inverse, upper, terms, across_terms, last_terms):
    block = upper.shape[0]

    def fill(picked):
        upper[...] = dot(left_terms(inverse[...]), right_terms(picked[...]))

    @pl.when(info[1] % 2 == 0)
    def _():
        fill(total)

    @pl.when(info[1] % 2 == 1)
    def _():
        fill(other)

    for shard in range(4):
        value = right_terms(upper[aligned((info[0] ^ shard) * width, width), :])
        if shard == 2:
            across_terms[...] = value
        if shard < 3:
            terms[pl.ds(shard * 3 * width, 3 * width), :] = value
        else:
            last_terms[...] = value


def make_upper(info, total, other, inverse, width):
    block, columns = total.shape
    return pl.pallas_call(
        lambda *refs: upper_kernel(width, *refs),
        out_shape=(
            jax.ShapeDtypeStruct((block, columns), total.dtype),
            jax.ShapeDtypeStruct((9 * width, columns), jnp.bfloat16),
            jax.ShapeDtypeStruct((3 * width, columns), jnp.bfloat16),
            jax.ShapeDtypeStruct((3 * width, columns), jnp.bfloat16),
        ),
        grid_spec=pltpu.PrefetchScalarGridSpec(
            num_scalar_prefetch=1,
            grid=(),
            in_specs=[VMEM] * 3,
            out_specs=(VMEM, VMEM, VMEM, VMEM),
        ),
        compiler_params=pltpu.CompilerParams(vmem_limit_bytes=24 << 20),
        cost_estimate=SMALL,
        name="upper",
    )(info, total, other, inverse)


def main_kernel(tile, info, pivots, slab, total, other, own, near, *refs):
    *across, upper, terms, out, own_rows, near_rows, across_rows, sem, panel_sem = refs
    copy = pltpu.make_async_copy(slab, out, sem)
    copy.start()
    loads = [(own, own_rows), (near, near_rows)]
    at = 0
    for piece in across:
        loads.append((piece, across_rows.at[pl.ds(at, piece.shape[0]), :]))
        at += piece.shape[0]
    loads = [pltpu.make_async_copy(a, b, panel_sem.at[i]) for i, (a, b) in enumerate(loads)]
    for load in loads:
        load.start()
    place = info[1]
    count = own_rows.shape[0]
    block = upper.shape[0]
    first = place * count
    copy.wait()

    def fill(old_top):
        @pl.loop(0, block // 8)
        def _(group):
            base = pl.multiple_of(group * 8, 8)
            for j in range(8):
                row = pivots[base + j] - first
                owned = (row >= 0) & (row < count)
                place_at = pl.ds(jnp.where(owned, row, 0), 1)
                out[place_at, :] = jnp.where(owned, old_top[pl.ds(base + j, 1), :], out[place_at, :])

    @pl.when(place % 2 == 0)
    def _():
        fill(other)

    @pl.when(place % 2 == 1)
    def _():
        fill(total)

    for load in loads:
        load.wait()

    def subtract(part, panels):
        left = jnp.concatenate([left_terms(panel[part, :]) for panel in panels], axis=1)
        out[part, :] = out[part, :] - dot(left, terms[pl.ds(0, left.shape[1]), :])

    @pl.loop(0, at // tile)
    def _(t):
        part = aligned(t * tile, tile)
        subtract(part, (own_rows, near_rows, across_rows))

        @pl.when((place == 0) & (t < block // tile))
        def _():
            out[part, :] = upper[aligned(jnp.minimum(t * tile, block - tile), tile), :]

    if at % tile:
        subtract(pl.ds(at - at % tile, at % tile), (own_rows, near_rows, across_rows))
    subtract(pl.ds(at, count - at), (own_rows, near_rows))


def main_update(info, pivots, slab, total, other, own, near, across, upper, terms):
    block = upper.shape[0]
    return pl.pallas_call(
        lambda *refs: main_kernel(min(TILE, block), *refs),
        out_shape=jax.ShapeDtypeStruct(slab.shape, slab.dtype),
        grid_spec=pltpu.PrefetchScalarGridSpec(
            num_scalar_prefetch=2,
            grid=(),
            in_specs=[HBM, VMEM, VMEM, HBM, HBM] + [HBM] * len(across) + [VMEM, VMEM],
            out_specs=VMEM,
            scratch_shapes=[pltpu.VMEM(own.shape, own.dtype)] * 2
            + [pltpu.VMEM((sum(piece.shape[0] for piece in across), own.shape[1]), own.dtype)]
            + [pltpu.SemaphoreType.DMA, pltpu.SemaphoreType.DMA((2 + len(across),))],
        ),
        compiler_params=pltpu.CompilerParams(vmem_limit_bytes=32 << 20),
        cost_estimate=SMALL,
        name="main_update",
    )(info, pivots, slab, total, other, own, near, *across, upper, terms)


def last_kernel(first_row, block, tile, segments, base, *refs):
    out, result, sem = refs[-3:]
    at = 0
    for count, groups in segments:
        for inner in range(0, count, tile):
            size = min(tile, count - inner)
            part = pl.ds(at, size)
            row = first_row + at
            delta = None
            for terms, pieces in groups:
                left = sum(refs[piece][pl.ds(offset + inner, size), :] for piece, offset in pieces)
                change = dot(left_terms(left), refs[terms][...])
                delta = change if delta is None else delta + change
            if row < block:
                delta = jnp.where(lax.axis_index("prow") == 0, 0.0, delta)
            result[part, :] = base[pl.ds(row, size), :] - delta
            pltpu.make_async_copy(result.at[part, :], out.at[pl.ds(row, size), :], sem).start()
            at += size
    pltpu.make_async_copy(result, out.at[pl.ds(first_row, at), :], sem).wait()


def last_update(base, arrays, segments, block, first_row, done):
    count = sum(size for size, _ in segments)
    return pl.pallas_call(
        lambda *refs: last_kernel(first_row, block, min(LAST_TILE, block), segments, *refs),
        out_shape=jax.ShapeDtypeStruct(base.shape, base.dtype),
        in_specs=[VMEM] * (1 + len(arrays)) + [HBM] * len(done),
        out_specs=HBM,
        scratch_shapes=[pltpu.VMEM((count, base.shape[1]), base.dtype), pltpu.SemaphoreType.DMA],
        input_output_aliases={1 + len(arrays): 0} if done else {},
        compiler_params=pltpu.CompilerParams(vmem_limit_bytes=24 << 20),
        cost_estimate=SMALL,
        name="last_update",
    )(base, *arrays, *done)


def exchange(value, bit, count):
    return lax.ppermute(value, "prow", [(i, i ^ (1 << bit)) for i in range(count)])


def solution(mesh):
    row_parts, column_parts = mesh.shape["prow"], mesh.shape["pcol"]
    bits = row_parts.bit_length() - 1
    if column_parts != 4 or row_parts != 1 << bits or bits < 1:
        raise ValueError("unsupported mesh")

    def shards(panel, slab, pivots, diag_inverse):
        rows_here = slab.shape[0]
        width = panel.shape[1]
        block = diag_inverse.shape[0]
        place = lax.axis_index("prow")
        column = lax.axis_index("pcol")
        info = jnp.stack([column, place]).astype(jnp.int32)

        first, second, last = (rows_here * part // sum(PIECES) for part in PIECES)
        first_mid, second_mid, _ = (rows_here * part // sum(PIECES) for part in MIDDLE_PIECES)
        early = first + second
        near = lax.ppermute(panel, "pcol", SWAP)
        *pieces, tail = cut(panel, [(0, first), (first, second), (early, last)])
        across = [lax.ppermute(piece, "pcol", ACROSS) for piece in pieces]
        far = lax.ppermute(tail, "pcol", FAR)

        def gather_rows(slab, pivots):
            send, keep = pick(info, pivots, slab, block)
            total = keep + exchange(send, 0, row_parts)
            halves = [total[: block // 2], total[block // 2 :]]
            orders = [list(range(1, bits)), list(range(1, bits))[::-1]]
            for step in range(bits - 1):
                other = [exchange(half, order[step], row_parts) for half, order in zip(halves, orders)]
                halves = [half + part for half, part in zip(halves, other)]
            total = jnp.concatenate(halves, axis=0)
            return total, exchange(total, 0, row_parts)

        def no_rows(slab, pivots):
            return slab[:block], slab[:block]

        total, other = lax.cond(pivots[0] >= 0, gather_rows, no_rows, slab, pivots)
        upper, terms, across_terms, last_terms = make_upper(info, total, other, diag_inverse, width)
        later, upper = lax.optimization_barrier((panel, upper))
        head, upper = lax.optimization_barrier((across[0], upper))
        head_mid, rest_mid, tail_mid = load_pieces(
            later, [(0, first_mid), (first_mid, second_mid), (early, last)]
        )
        tail_mid = lax.ppermute(tail_mid, "pcol", MIDDLE)
        head_end = lax.ppermute(head, "pcol", ENDS)
        rest, head_mid, near = lax.optimization_barrier((across[1], head_mid, near))
        rest_mid, far, near = lax.optimization_barrier((rest_mid, far, near))
        head_mid = lax.ppermute(head_mid, "pcol", MIDDLE)
        rest_mid = lax.ppermute(rest_mid, "pcol", MIDDLE)
        rest_end = lax.ppermute(rest, "pcol", ENDS)
        both, rest = lax.optimization_barrier((jnp.concatenate([far, tail_mid], axis=0), rest))
        both = lax.ppermute(both, "pcol", ENDS)

        base = main_update(info, pivots, slab, total, other, panel, near, [head, rest], upper, terms)
        segments = [(first_mid, [(0, [(1, 0), (2, 0)])])]
        result = last_update(base, [last_terms, head_end, head_mid], segments, block, 0, [])
        segments = [(last, [(0, [(2, 0), (4, last)]), (1, [(3, 0), (4, 0)])])]
        arrays = [across_terms, last_terms, far, tail_mid, both]
        result = last_update(base, arrays, segments, block, early, [result])
        segments = [
            (first - first_mid, [(0, [(1, first_mid), (3, 0)])]),
            (second, [(0, [(2, 0), (3, first - first_mid)])]),
        ]
        arrays = [last_terms, head_end, rest_end, rest_mid]
        return last_update(base, arrays, segments, block, first_mid, [result])

    in_specs = (P("prow", "pcol"), P("prow", "pcol"), P(), P())
    return jax.shard_map(
        shards, mesh=mesh, in_specs=in_specs, out_specs=P("prow", "pcol"), check_vma=False
    )
```

```python
import jax
import jax.numpy as jnp
from jax import lax
from jax.experimental import pallas as pl
from jax.experimental.pallas import tpu as pltpu
from jax.sharding import PartitionSpec as P

SWAP = [(0, 1), (1, 0), (2, 3), (3, 2)]
ACROSS = [(0, 2), (1, 3), (2, 0), (3, 1)]
MIDDLE = [(1, 2), (2, 1)]
ENDS = [(2, 3), (1, 0)]
FAR = [(0, 2), (3, 1)]
PIECES = (86, 16, 26)
MIDDLE_PIECES = (80, 22, 26)
TILE = 512
LAST_TILE = 256
SMALL = pl.CostEstimate(flops=0, bytes_accessed=0, transcendentals=0)
HBM = pl.BlockSpec(memory_space=pl.ANY)
VMEM = pl.BlockSpec(memory_space=pltpu.VMEM)


def split(x):
    high = x.astype(jnp.bfloat16)
    low = (x - high.astype(jnp.float32)).astype(jnp.bfloat16)
    return high, low


def left_terms(x):
    high, low = split(x)
    return jnp.concatenate([high, high, low], axis=1)


def right_terms(x):
    high, low = split(x)
    return jnp.concatenate([high, low, high], axis=0)


def dot(a, b):
    return jnp.dot(a, b, preferred_element_type=jnp.float32)


def aligned(start, size):
    return pl.ds(pl.multiple_of(start, size), size)


def load_kernel(spans, panel, *refs):
    outs, sem = refs[:-1], refs[-1]
    copies = [
        pltpu.make_async_copy(panel.at[pl.ds(start, size), :], out, sem.at[i])
        for i, ((start, size), out) in enumerate(zip(spans, outs))
    ]
    for copy in copies:
        copy.start()
    for copy in copies:
        copy.wait()


def load_pieces(panel, spans):
    return pl.pallas_call(
        lambda *refs: load_kernel(spans, *refs),
        out_shape=tuple(jax.ShapeDtypeStruct((size, panel.shape[1]), panel.dtype) for _, size in spans),
        in_specs=[pl.BlockSpec(memory_space=pltpu.HBM)],
        out_specs=tuple([VMEM] * len(spans)),
        scratch_shapes=[pltpu.SemaphoreType.DMA((len(spans),))],
        compiler_params=pltpu.CompilerParams(vmem_limit_bytes=8 << 20),
        cost_estimate=SMALL,
        name="load_pieces",
    )(pltpu.with_memory_space_constraint(panel, pltpu.HBM))


def cut_kernel(spans, panel, *refs):
    outs, (rows, sem, out_sem) = refs[:-3], refs[-3:]
    steps = []
    for i, (start, size) in enumerate(spans):
        for at in range(0, size, TILE):
            steps.append((i, start + at, at, min(TILE, size - at)))

    def load(number):
        _, row, _, size = steps[number]
        part = pl.ds(row, size)
        return pltpu.make_async_copy(panel.at[part, :], rows.at[part, :], sem.at[number])

    for number in range(len(steps)):
        load(number).start()
    for number, (i, row, at, size) in enumerate(steps):
        load(number).wait()
        pltpu.make_async_copy(rows.at[pl.ds(row, size), :], outs[i].at[pl.ds(at, size), :], out_sem.at[i]).start()
    for i, (start, size) in enumerate(spans):
        pltpu.make_async_copy(rows.at[pl.ds(start, size), :], outs[i], out_sem.at[i]).wait()


def cut(panel, spans):
    count = sum(-(-size // TILE) for _, size in spans)
    return pl.pallas_call(
        lambda *refs: cut_kernel(spans, *refs),
        out_shape=tuple(jax.ShapeDtypeStruct((size, panel.shape[1]), panel.dtype) for _, size in spans),
        in_specs=[pl.BlockSpec(memory_space=pltpu.HBM)],
        out_specs=tuple([HBM] * len(spans)),
        scratch_shapes=[
            pltpu.VMEM(panel.shape, panel.dtype),
            pltpu.SemaphoreType.DMA((count,)),
            pltpu.SemaphoreType.DMA((len(spans),)),
        ],
        compiler_params=pltpu.CompilerParams(vmem_limit_bytes=8 << 20),
        cost_estimate=SMALL,
        name="cut",
    )(pltpu.with_memory_space_constraint(panel, pltpu.HBM))


def pick_kernel(info, pivots, slab, send, keep, rows, sem, top_sem):
    copy = pltpu.make_async_copy(slab, rows, sem)
    copy.start()
    place = info[1]
    count = rows.shape[0]
    block = send.shape[0]
    first = place * count

    def fill(picked, top):
        load = pltpu.make_async_copy(slab.at[pl.ds(0, block), :], top, top_sem)

        @pl.when(place == 0)
        def _():
            load.start()

        @pl.when(place != 0)
        def _():
            top[...] = jnp.zeros_like(top)

        copy.wait()

        @pl.loop(0, block // 8)
        def _(group):
            base = pl.multiple_of(group * 8, 8)
            for j in range(8):
                row = pivots[base + j] - first
                owned = (row >= 0) & (row < count)
                value = rows[pl.ds(jnp.where(owned, row, 0), 1), :]
                picked[pl.ds(base + j, 1), :] = jnp.where(owned, value, 0.0)

        @pl.when(place == 0)
        def _():
            load.wait()

    @pl.when(place % 2 == 0)
    def _():
        fill(keep, send)

    @pl.when(place % 2 == 1)
    def _():
        fill(send, keep)


def pick(info, pivots, slab, block):
    columns = slab.shape[1]
    shape = jax.ShapeDtypeStruct((block, columns), slab.dtype)
    return pl.pallas_call(
        pick_kernel,
        out_shape=(shape, shape),
        grid_spec=pltpu.PrefetchScalarGridSpec(
            num_scalar_prefetch=2,
            grid=(),
            in_specs=[HBM],
            out_specs=(VMEM, VMEM),
            scratch_shapes=[
                pltpu.VMEM(slab.shape, slab.dtype),
                pltpu.SemaphoreType.DMA,
                pltpu.SemaphoreType.DMA,
            ],
        ),
        compiler_params=pltpu.CompilerParams(vmem_limit_bytes=16 << 20),
        cost_estimate=SMALL,
        name="pick",
    )(info, pivots, slab)


def upper_kernel(width, info, total, other, inverse, upper, terms, across_terms, last_terms):
    block = upper.shape[0]

    def fill(picked):
        upper[...] = dot(left_terms(inverse[...]), right_terms(picked[...]))

    @pl.when(info[1] % 2 == 0)
    def _():
        fill(total)

    @pl.when(info[1] % 2 == 1)
    def _():
        fill(other)

    for shard in range(4):
        value = right_terms(upper[aligned((info[0] ^ shard) * width, width), :])
        if shard == 2:
            across_terms[...] = value
        if shard < 3:
            terms[pl.ds(shard * 3 * width, 3 * width), :] = value
        else:
            last_terms[...] = value


def make_upper(info, total, other, inverse, width):
    block, columns = total.shape
    return pl.pallas_call(
        lambda *refs: upper_kernel(width, *refs),
        out_shape=(
            jax.ShapeDtypeStruct((block, columns), total.dtype),
            jax.ShapeDtypeStruct((9 * width, columns), jnp.bfloat16),
            jax.ShapeDtypeStruct((3 * width, columns), jnp.bfloat16),
            jax.ShapeDtypeStruct((3 * width, columns), jnp.bfloat16),
        ),
        grid_spec=pltpu.PrefetchScalarGridSpec(
            num_scalar_prefetch=1,
            grid=(),
            in_specs=[VMEM] * 3,
            out_specs=(VMEM, VMEM, VMEM, VMEM),
        ),
        compiler_params=pltpu.CompilerParams(vmem_limit_bytes=24 << 20),
        cost_estimate=SMALL,
        name="upper",
    )(info, total, other, inverse)


def main_kernel(tile, info, pivots, slab, total, other, own, near, *refs):
    *across, upper, terms, out, own_rows, near_rows, across_rows, sem, panel_sem = refs
    copy = pltpu.make_async_copy(slab, out, sem)
    copy.start()
    loads = [(own, own_rows), (near, near_rows)]
    at = 0
    for piece in across:
        loads.append((piece, across_rows.at[pl.ds(at, piece.shape[0]), :]))
        at += piece.shape[0]
    loads = [pltpu.make_async_copy(a, b, panel_sem.at[i]) for i, (a, b) in enumerate(loads)]
    for load in loads:
        load.start()
    place = info[1]
    count = own_rows.shape[0]
    block = upper.shape[0]
    first = place * count
    copy.wait()

    def fill(old_top):
        @pl.loop(0, block // 8)
        def _(group):
            base = pl.multiple_of(group * 8, 8)
            for j in range(8):
                row = pivots[base + j] - first
                owned = (row >= 0) & (row < count)
                place_at = pl.ds(jnp.where(owned, row, 0), 1)
                out[place_at, :] = jnp.where(owned, old_top[pl.ds(base + j, 1), :], out[place_at, :])

    @pl.when(place % 2 == 0)
    def _():
        fill(other)

    @pl.when(place % 2 == 1)
    def _():
        fill(total)

    for load in loads:
        load.wait()

    def subtract(part, panels):
        left = jnp.concatenate([left_terms(panel[part, :]) for panel in panels], axis=1)
        out[part, :] = out[part, :] - dot(left, terms[pl.ds(0, left.shape[1]), :])

    @pl.loop(0, at // tile)
    def _(t):
        part = aligned(t * tile, tile)
        subtract(part, (own_rows, near_rows, across_rows))

        @pl.when((place == 0) & (t < block // tile))
        def _():
            out[part, :] = upper[aligned(jnp.minimum(t * tile, block - tile), tile), :]

    if at % tile:
        subtract(pl.ds(at - at % tile, at % tile), (own_rows, near_rows, across_rows))
    subtract(pl.ds(at, count - at), (own_rows, near_rows))


def main_update(info, pivots, slab, total, other, own, near, across, upper, terms):
    block = upper.shape[0]
    return pl.pallas_call(
        lambda *refs: main_kernel(min(TILE, block), *refs),
        out_shape=jax.ShapeDtypeStruct(slab.shape, slab.dtype),
        grid_spec=pltpu.PrefetchScalarGridSpec(
            num_scalar_prefetch=2,
            grid=(),
            in_specs=[HBM, VMEM, VMEM, HBM, HBM] + [HBM] * len(across) + [VMEM, VMEM],
            out_specs=VMEM,
            scratch_shapes=[pltpu.VMEM(own.shape, own.dtype)] * 2
            + [pltpu.VMEM((sum(piece.shape[0] for piece in across), own.shape[1]), own.dtype)]
            + [pltpu.SemaphoreType.DMA, pltpu.SemaphoreType.DMA((2 + len(across),))],
        ),
        compiler_params=pltpu.CompilerParams(vmem_limit_bytes=32 << 20),
        cost_estimate=SMALL,
        name="main_update",
    )(info, pivots, slab, total, other, own, near, *across, upper, terms)


def last_kernel(first_row, block, tile, segments, base, *refs):
    out, result, sem = refs[-3:]
    at = 0
    for count, groups in segments:
        for inner in range(0, count, tile):
            size = min(tile, count - inner)
            part = pl.ds(at, size)
            row = first_row + at
            delta = None
            for terms, pieces in groups:
                left = sum(refs[piece][pl.ds(offset + inner, size), :] for piece, offset in pieces)
                change = dot(left_terms(left), refs[terms][...])
                delta = change if delta is None else delta + change
            if row < block:
                delta = jnp.where(lax.axis_index("prow") == 0, 0.0, delta)
            result[part, :] = base[pl.ds(row, size), :] - delta
            pltpu.make_async_copy(result.at[part, :], out.at[pl.ds(row, size), :], sem).start()
            at += size
    pltpu.make_async_copy(result, out.at[pl.ds(first_row, at), :], sem).wait()


def last_update(base, arrays, segments, block, first_row, done):
    count = sum(size for size, _ in segments)
    return pl.pallas_call(
        lambda *refs: last_kernel(first_row, block, min(LAST_TILE, block), segments, *refs),
        out_shape=jax.ShapeDtypeStruct(base.shape, base.dtype),
        in_specs=[VMEM] * (1 + len(arrays)) + [HBM] * len(done),
        out_specs=HBM,
        scratch_shapes=[pltpu.VMEM((count, base.shape[1]), base.dtype), pltpu.SemaphoreType.DMA],
        input_output_aliases={1 + len(arrays): 0} if done else {},
        compiler_params=pltpu.CompilerParams(vmem_limit_bytes=24 << 20),
        cost_estimate=SMALL,
        name="last_update",
    )(base, *arrays, *done)


def exchange(value, bit, count):
    return lax.ppermute(value, "prow", [(i, i ^ (1 << bit)) for i in range(count)])


def on_rows(value, rows, pairs):
    return lax.ppermute(
        value, ("prow", "pcol"), [(4 * row + a, 4 * row + b) for row in rows for a, b in pairs]
    )


def solution(mesh):
    row_parts, column_parts = mesh.shape["prow"], mesh.shape["pcol"]
    bits = row_parts.bit_length() - 1
    if column_parts != 4 or row_parts != 1 << bits or bits < 1:
        raise ValueError("unsupported mesh")

    def shards(panel, slab, pivots, diag_inverse):
        rows_here = slab.shape[0]
        width = panel.shape[1]
        block = diag_inverse.shape[0]
        place = lax.axis_index("prow")
        column = lax.axis_index("pcol")
        info = jnp.stack([column, place]).astype(jnp.int32)

        first, second, last = (rows_here * part // sum(PIECES) for part in PIECES)
        first_mid, second_mid, _ = (rows_here * part // sum(PIECES) for part in MIDDLE_PIECES)
        early = first + second
        if second > block or second % min(LAST_TILE, block):
            raise ValueError("unsupported sizes")
        below = [row for row in range(row_parts) if row]
        near = lax.ppermute(panel, "pcol", SWAP)
        pieces = cut(panel, [(second, first), (0, second)])
        across = [lax.ppermute(pieces[0], "pcol", ACROSS), on_rows(pieces[1], below, ACROSS)]

        def gather_rows(slab, pivots):
            send, keep = pick(info, pivots, slab, block)
            total = keep + exchange(send, 0, row_parts)
            halves = [total[: block // 2], total[block // 2 :]]
            orders = [list(range(1, bits)), list(range(1, bits))[::-1]]
            for step in range(bits - 1):
                other = [exchange(half, order[step], row_parts) for half, order in zip(halves, orders)]
                halves = [half + part for half, part in zip(halves, other)]
            total = jnp.concatenate(halves, axis=0)
            return total, exchange(total, 0, row_parts)

        def no_rows(slab, pivots):
            return slab[:block], slab[:block]

        total, other = lax.cond(pivots[0] >= 0, gather_rows, no_rows, slab, pivots)
        upper, terms, across_terms, last_terms = make_upper(info, total, other, diag_inverse, width)
        later, upper = lax.optimization_barrier((panel, upper))
        head, upper = lax.optimization_barrier((across[0], upper))
        head_mid, rest_mid, tail = load_pieces(
            later, [(second_mid, first_mid), (0, second_mid), (early, last)]
        )
        tail_mid = lax.ppermute(tail, "pcol", MIDDLE)
        far = lax.ppermute(tail, "pcol", FAR)
        head_end = lax.ppermute(head, "pcol", ENDS)
        rest, head_mid, near = lax.optimization_barrier((across[1], head_mid, near))
        rest_mid, far, near = lax.optimization_barrier((rest_mid, far, near))
        head_mid = lax.ppermute(head_mid, "pcol", MIDDLE)
        rest_mid = lax.ppermute(rest_mid, "pcol", MIDDLE)
        rest_end = on_rows(rest, below, ENDS)
        both, rest = lax.optimization_barrier((jnp.concatenate([far, tail_mid], axis=0), rest))
        both = lax.ppermute(both, "pcol", ENDS)

        base = main_update(info, pivots, slab, total, other, panel, near, [rest, head], upper, terms)
        segments = [(first_mid, [(0, [(1, second_mid - second), (2, 0)])])]
        arrays = [last_terms, head_end, head_mid]
        result = last_update(base, arrays, segments, block, second_mid, [])
        segments = [(last, [(0, [(2, 0), (4, last)]), (1, [(3, 0), (4, 0)])])]
        arrays = [across_terms, last_terms, far, tail_mid, both]
        result = last_update(base, arrays, segments, block, early, [result])
        segments = [
            (second_mid - second, [(0, [(1, 0), (3, second)])]),
            (second, [(0, [(2, 0), (3, 0)])]),
        ]
        arrays = [last_terms, head_end, rest_end, rest_mid]
        return last_update(base, arrays, segments[::-1], block, 0, [result])

    in_specs = (P("prow", "pcol"), P("prow", "pcol"), P(), P())
    return jax.shard_map(
        shards, mesh=mesh, in_specs=in_specs, out_specs=P("prow", "pcol"), check_vma=False
    )
```

```python
import jax
import jax.numpy as jnp
from jax import lax
from jax.experimental import pallas as pl
from jax.experimental.pallas import tpu as pltpu
from jax.sharding import PartitionSpec as P

SWAP = [(0, 1), (1, 0), (2, 3), (3, 2)]
ACROSS = [(0, 2), (1, 3), (2, 0), (3, 1)]
MIDDLE = [(1, 2), (2, 1)]
ENDS = [(2, 3), (1, 0)]
FAR = [(0, 2), (3, 1)]
PIECES = (86, 16, 26)
MIDDLE_PIECES = (80, 22, 26)
TILE = 512
LAST_TILE = 256
SMALL = pl.CostEstimate(flops=0, bytes_accessed=0, transcendentals=0)
HBM = pl.BlockSpec(memory_space=pl.ANY)
VMEM = pl.BlockSpec(memory_space=pltpu.VMEM)


def split(x):
    high = x.astype(jnp.bfloat16)
    low = (x - high.astype(jnp.float32)).astype(jnp.bfloat16)
    return high, low


def left_terms(x):
    high, low = split(x)
    return jnp.concatenate([high, high, low], axis=1)


def right_terms(x):
    high, low = split(x)
    return jnp.concatenate([high, low, high], axis=0)


def dot(a, b):
    return jnp.dot(a, b, preferred_element_type=jnp.float32)


def aligned(start, size):
    return pl.ds(pl.multiple_of(start, size), size)


def load_kernel(spans, panel, *refs):
    outs, sem = refs[:-1], refs[-1]
    copies = [
        pltpu.make_async_copy(panel.at[pl.ds(start, size), :], out, sem.at[i])
        for i, ((start, size), out) in enumerate(zip(spans, outs))
    ]
    for copy in copies:
        copy.start()
    for copy in copies:
        copy.wait()


def load_pieces(panel, spans):
    return pl.pallas_call(
        lambda *refs: load_kernel(spans, *refs),
        out_shape=tuple(jax.ShapeDtypeStruct((size, panel.shape[1]), panel.dtype) for _, size in spans),
        in_specs=[pl.BlockSpec(memory_space=pltpu.HBM)],
        out_specs=tuple([VMEM] * len(spans)),
        scratch_shapes=[pltpu.SemaphoreType.DMA((len(spans),))],
        compiler_params=pltpu.CompilerParams(vmem_limit_bytes=8 << 20),
        cost_estimate=SMALL,
        name="load_pieces",
    )(pltpu.with_memory_space_constraint(panel, pltpu.HBM))


def cut_kernel(spans, panel, *refs):
    outs, (rows, sem, out_sem) = refs[:-3], refs[-3:]
    steps = []
    for i, (start, size) in enumerate(spans):
        for at in range(0, size, TILE):
            steps.append((i, start + at, at, min(TILE, size - at)))

    def load(number):
        _, row, _, size = steps[number]
        part = pl.ds(row, size)
        return pltpu.make_async_copy(panel.at[part, :], rows.at[part, :], sem.at[number])

    for number in range(len(steps)):
        load(number).start()
    for number, (i, row, at, size) in enumerate(steps):
        load(number).wait()
        pltpu.make_async_copy(rows.at[pl.ds(row, size), :], outs[i].at[pl.ds(at, size), :], out_sem.at[i]).start()
    for i, (start, size) in enumerate(spans):
        pltpu.make_async_copy(rows.at[pl.ds(start, size), :], outs[i], out_sem.at[i]).wait()


def cut(panel, spans):
    count = sum(-(-size // TILE) for _, size in spans)
    return pl.pallas_call(
        lambda *refs: cut_kernel(spans, *refs),
        out_shape=tuple(jax.ShapeDtypeStruct((size, panel.shape[1]), panel.dtype) for _, size in spans),
        in_specs=[pl.BlockSpec(memory_space=pltpu.HBM)],
        out_specs=tuple([HBM] * len(spans)),
        scratch_shapes=[
            pltpu.VMEM(panel.shape, panel.dtype),
            pltpu.SemaphoreType.DMA((count,)),
            pltpu.SemaphoreType.DMA((len(spans),)),
        ],
        compiler_params=pltpu.CompilerParams(vmem_limit_bytes=8 << 20),
        cost_estimate=SMALL,
        name="cut",
    )(pltpu.with_memory_space_constraint(panel, pltpu.HBM))


def pick_kernel(info, pivots, slab, send, keep, rows, sem, top_sem):
    copy = pltpu.make_async_copy(slab, rows, sem)
    copy.start()
    place = info[1]
    count = rows.shape[0]
    block = send.shape[0]
    first = place * count

    def fill(picked, top):
        load = pltpu.make_async_copy(slab.at[pl.ds(0, block), :], top, top_sem)

        @pl.when(place == 0)
        def _():
            load.start()

        @pl.when(place != 0)
        def _():
            top[...] = jnp.zeros_like(top)

        copy.wait()

        @pl.loop(0, block // 8)
        def _(group):
            base = pl.multiple_of(group * 8, 8)
            for j in range(8):
                row = pivots[base + j] - first
                owned = (row >= 0) & (row < count)
                value = rows[pl.ds(jnp.where(owned, row, 0), 1), :]
                picked[pl.ds(base + j, 1), :] = jnp.where(owned, value, 0.0)

        @pl.when(place == 0)
        def _():
            load.wait()

    @pl.when(place % 2 == 0)
    def _():
        fill(keep, send)

    @pl.when(place % 2 == 1)
    def _():
        fill(send, keep)


def pick(info, pivots, slab, block):
    columns = slab.shape[1]
    shape = jax.ShapeDtypeStruct((block, columns), slab.dtype)
    return pl.pallas_call(
        pick_kernel,
        out_shape=(shape, shape),
        grid_spec=pltpu.PrefetchScalarGridSpec(
            num_scalar_prefetch=2,
            grid=(),
            in_specs=[HBM],
            out_specs=(VMEM, VMEM),
            scratch_shapes=[
                pltpu.VMEM(slab.shape, slab.dtype),
                pltpu.SemaphoreType.DMA,
                pltpu.SemaphoreType.DMA,
            ],
        ),
        compiler_params=pltpu.CompilerParams(vmem_limit_bytes=16 << 20),
        cost_estimate=SMALL,
        name="pick",
    )(info, pivots, slab)


def upper_kernel(width, info, total, other, inverse, upper, terms, across_terms, last_terms):
    block = upper.shape[0]

    def fill(picked):
        upper[...] = dot(left_terms(inverse[...]), right_terms(picked[...]))

    @pl.when(info[1] % 2 == 0)
    def _():
        fill(total)

    @pl.when(info[1] % 2 == 1)
    def _():
        fill(other)

    for shard in range(4):
        value = right_terms(upper[aligned((info[0] ^ shard) * width, width), :])
        if shard == 2:
            across_terms[...] = value
        if shard < 3:
            terms[pl.ds(shard * 3 * width, 3 * width), :] = value
        else:
            last_terms[...] = value


def make_upper(info, total, other, inverse, width):
    block, columns = total.shape
    return pl.pallas_call(
        lambda *refs: upper_kernel(width, *refs),
        out_shape=(
            jax.ShapeDtypeStruct((block, columns), total.dtype),
            jax.ShapeDtypeStruct((9 * width, columns), jnp.bfloat16),
            jax.ShapeDtypeStruct((3 * width, columns), jnp.bfloat16),
            jax.ShapeDtypeStruct((3 * width, columns), jnp.bfloat16),
        ),
        grid_spec=pltpu.PrefetchScalarGridSpec(
            num_scalar_prefetch=1,
            grid=(),
            in_specs=[VMEM] * 3,
            out_specs=(VMEM, VMEM, VMEM, VMEM),
        ),
        compiler_params=pltpu.CompilerParams(vmem_limit_bytes=24 << 20),
        cost_estimate=SMALL,
        name="upper",
    )(info, total, other, inverse)


def main_kernel(tile, info, pivots, slab, total, other, own, near, *refs):
    *across, upper, terms, out, own_rows, near_rows, across_rows, sem, panel_sem = refs
    copy = pltpu.make_async_copy(slab, out, sem)
    copy.start()
    loads = [(own, own_rows), (near, near_rows)]
    at = 0
    for piece in across:
        loads.append((piece, across_rows.at[pl.ds(at, piece.shape[0]), :]))
        at += piece.shape[0]
    loads = [pltpu.make_async_copy(a, b, panel_sem.at[i]) for i, (a, b) in enumerate(loads)]
    for load in loads:
        load.start()
    place = info[1]
    count = own_rows.shape[0]
    block = upper.shape[0]
    first = place * count
    copy.wait()

    def fill(old_top):
        @pl.loop(0, block // 8)
        def _(group):
            base = pl.multiple_of(group * 8, 8)
            for j in range(8):
                row = pivots[base + j] - first
                owned = (row >= 0) & (row < count)
                place_at = pl.ds(jnp.where(owned, row, 0), 1)
                out[place_at, :] = jnp.where(owned, old_top[pl.ds(base + j, 1), :], out[place_at, :])

    @pl.when(place % 2 == 0)
    def _():
        fill(other)

    @pl.when(place % 2 == 1)
    def _():
        fill(total)

    for load in loads:
        load.wait()

    def subtract(part, panels):
        left = jnp.concatenate([left_terms(panel[part, :]) for panel in panels], axis=1)
        out[part, :] = out[part, :] - dot(left, terms[pl.ds(0, left.shape[1]), :])

    @pl.loop(0, at // tile)
    def _(t):
        part = aligned(t * tile, tile)
        subtract(part, (own_rows, near_rows, across_rows))

        @pl.when((place == 0) & (t < block // tile))
        def _():
            out[part, :] = upper[aligned(jnp.minimum(t * tile, block - tile), tile), :]

    if at % tile:
        subtract(pl.ds(at - at % tile, at % tile), (own_rows, near_rows, across_rows))
    subtract(pl.ds(at, count - at), (own_rows, near_rows))


def main_update(info, pivots, slab, total, other, own, near, across, upper, terms):
    block = upper.shape[0]
    return pl.pallas_call(
        lambda *refs: main_kernel(min(TILE, block), *refs),
        out_shape=jax.ShapeDtypeStruct(slab.shape, slab.dtype),
        grid_spec=pltpu.PrefetchScalarGridSpec(
            num_scalar_prefetch=2,
            grid=(),
            in_specs=[HBM, VMEM, VMEM, HBM, HBM] + [HBM] * len(across) + [VMEM, VMEM],
            out_specs=VMEM,
            scratch_shapes=[pltpu.VMEM(own.shape, own.dtype)] * 2
            + [pltpu.VMEM((sum(piece.shape[0] for piece in across), own.shape[1]), own.dtype)]
            + [pltpu.SemaphoreType.DMA, pltpu.SemaphoreType.DMA((2 + len(across),))],
        ),
        compiler_params=pltpu.CompilerParams(vmem_limit_bytes=32 << 20),
        cost_estimate=SMALL,
        name="main_update",
    )(info, pivots, slab, total, other, own, near, *across, upper, terms)


def last_kernel(first_row, block, tile, segments, base, *refs):
    out, result, sem = refs[-3:]
    at = 0
    for count, groups in segments:
        for inner in range(0, count, tile):
            size = min(tile, count - inner)
            part = pl.ds(at, size)
            row = first_row + at
            delta = None
            for terms, pieces in groups:
                left = sum(refs[piece][pl.ds(offset + inner, size), :] for piece, offset in pieces)
                change = dot(left_terms(left), refs[terms][...])
                delta = change if delta is None else delta + change
            if row < block:
                delta = jnp.where(lax.axis_index("prow") == 0, 0.0, delta)
            result[part, :] = base[pl.ds(row, size), :] - delta
            pltpu.make_async_copy(result.at[part, :], out.at[pl.ds(row, size), :], sem).start()
            at += size
    pltpu.make_async_copy(result, out.at[pl.ds(first_row, at), :], sem).wait()


def last_update(base, arrays, segments, block, first_row, done):
    count = sum(size for size, _ in segments)
    return pl.pallas_call(
        lambda *refs: last_kernel(first_row, block, min(LAST_TILE, block), segments, *refs),
        out_shape=jax.ShapeDtypeStruct(base.shape, base.dtype),
        in_specs=[VMEM] * (1 + len(arrays)) + [HBM] * len(done),
        out_specs=HBM,
        scratch_shapes=[pltpu.VMEM((count, base.shape[1]), base.dtype), pltpu.SemaphoreType.DMA],
        input_output_aliases={1 + len(arrays): 0} if done else {},
        compiler_params=pltpu.CompilerParams(vmem_limit_bytes=24 << 20),
        cost_estimate=SMALL,
        name="last_update",
    )(base, *arrays, *done)


def exchange(value, bit, count):
    return lax.ppermute(value, "prow", [(i, i ^ (1 << bit)) for i in range(count)])


def on_rows(value, rows, pairs):
    return lax.ppermute(
        value, ("prow", "pcol"), [(4 * row + a, 4 * row + b) for row in rows for a, b in pairs]
    )


def solution(mesh):
    row_parts, column_parts = mesh.shape["prow"], mesh.shape["pcol"]
    bits = row_parts.bit_length() - 1
    if column_parts != 4 or row_parts != 1 << bits or bits < 1:
        raise ValueError("unsupported mesh")

    def shards(panel, slab, pivots, diag_inverse):
        rows_here = slab.shape[0]
        width = panel.shape[1]
        block = diag_inverse.shape[0]
        place = lax.axis_index("prow")
        column = lax.axis_index("pcol")
        info = jnp.stack([column, place]).astype(jnp.int32)

        first, second, last = (rows_here * part // sum(PIECES) for part in PIECES)
        first_mid, second_mid, _ = (rows_here * part // sum(PIECES) for part in MIDDLE_PIECES)
        early = first + second
        if second > block or second % min(LAST_TILE, block):
            raise ValueError("unsupported sizes")
        below = [row for row in range(row_parts) if row]
        near = lax.ppermute(panel, "pcol", SWAP)
        pieces = cut(panel, [(second, first), (0, second)])
        across = [lax.ppermute(pieces[0], "pcol", ACROSS), on_rows(pieces[1], below, ACROSS)]
        tail_mid = lax.ppermute(panel[early:], "pcol", MIDDLE)

        def gather_rows(slab, pivots):
            send, keep = pick(info, pivots, slab, block)
            total = keep + exchange(send, 0, row_parts)
            halves = [total[: block // 2], total[block // 2 :]]
            orders = [list(range(1, bits)), list(range(1, bits))[::-1]]
            for step in range(bits - 1):
                other = [exchange(half, order[step], row_parts) for half, order in zip(halves, orders)]
                halves = [half + part for half, part in zip(halves, other)]
            total = jnp.concatenate(halves, axis=0)
            return total, exchange(total, 0, row_parts)

        def no_rows(slab, pivots):
            return slab[:block], slab[:block]

        total, other = lax.cond(pivots[0] >= 0, gather_rows, no_rows, slab, pivots)
        upper, terms, across_terms, last_terms = make_upper(info, total, other, diag_inverse, width)
        later, upper = lax.optimization_barrier((panel, upper))
        head, tail_mid, upper = lax.optimization_barrier((across[0], tail_mid, upper))
        head_mid, rest_mid, tail = load_pieces(
            later, [(second_mid, first_mid), (0, second_mid), (early, last)]
        )
        far = lax.ppermute(tail, "pcol", FAR)
        head_end = lax.ppermute(head, "pcol", ENDS)
        rest, head_mid, near = lax.optimization_barrier((across[1], head_mid, near))
        rest_mid, far, near = lax.optimization_barrier((rest_mid, far, near))
        head_mid = lax.ppermute(head_mid, "pcol", MIDDLE)
        rest_mid = lax.ppermute(rest_mid, "pcol", MIDDLE)
        rest_end = on_rows(rest, below, ENDS)
        both, rest = lax.optimization_barrier((jnp.concatenate([far, tail_mid], axis=0), rest))
        both = lax.ppermute(both, "pcol", ENDS)

        base = main_update(info, pivots, slab, total, other, panel, near, [rest, head], upper, terms)
        segments = [(first_mid, [(0, [(1, second_mid - second), (2, 0)])])]
        arrays = [last_terms, head_end, head_mid]
        result = last_update(base, arrays, segments, block, second_mid, [])
        segments = [(last, [(0, [(2, 0), (4, last)]), (1, [(3, 0), (4, 0)])])]
        arrays = [across_terms, last_terms, far, tail_mid, both]
        result = last_update(base, arrays, segments, block, early, [result])
        segments = [
            (second_mid - second, [(0, [(1, 0), (3, second)])]),
            (second, [(0, [(2, 0), (3, 0)])]),
        ]
        arrays = [last_terms, head_end, rest_end, rest_mid]
        return last_update(base, arrays, segments[::-1], block, 0, [result])

    in_specs = (P("prow", "pcol"), P("prow", "pcol"), P(), P())
    return jax.shard_map(
        shards, mesh=mesh, in_specs=in_specs, out_specs=P("prow", "pcol"), check_vma=False
    )
```

```python
import jax
import jax.numpy as jnp
from jax import lax
from jax.experimental import pallas as pl
from jax.experimental.pallas import tpu as pltpu
from jax.sharding import PartitionSpec as P

SWAP = [(0, 1), (1, 0), (2, 3), (3, 2)]
ACROSS = [(0, 2), (1, 3), (2, 0), (3, 1)]
MIDDLE = [(1, 2), (2, 1)]
ENDS = [(2, 3), (1, 0)]
FAR = [(0, 2), (3, 1)]
PIECES = (85, 16, 27)
MIDDLE_PIECES = (83, 18, 27)
TILE = 512
LAST_TILE = 256
SMALL = pl.CostEstimate(flops=0, bytes_accessed=0, transcendentals=0)
HBM = pl.BlockSpec(memory_space=pl.ANY)
VMEM = pl.BlockSpec(memory_space=pltpu.VMEM)


def split(x):
    high = x.astype(jnp.bfloat16)
    low = (x - high.astype(jnp.float32)).astype(jnp.bfloat16)
    return high, low


def left_terms(x):
    high, low = split(x)
    return jnp.concatenate([high, high, low], axis=1)


def right_terms(x):
    high, low = split(x)
    return jnp.concatenate([high, low, high], axis=0)


def dot(a, b):
    return jnp.dot(a, b, preferred_element_type=jnp.float32)


def aligned(start, size):
    return pl.ds(pl.multiple_of(start, size), size)


def load_kernel(spans, panel, *refs):
    outs, sem = refs[:-1], refs[-1]
    copies = [
        pltpu.make_async_copy(panel.at[pl.ds(start, size), :], out, sem.at[i])
        for i, ((start, size), out) in enumerate(zip(spans, outs))
    ]
    for copy in copies:
        copy.start()
    for copy in copies:
        copy.wait()


def load_pieces(panel, spans):
    return pl.pallas_call(
        lambda *refs: load_kernel(spans, *refs),
        out_shape=tuple(jax.ShapeDtypeStruct((size, panel.shape[1]), panel.dtype) for _, size in spans),
        in_specs=[pl.BlockSpec(memory_space=pltpu.HBM)],
        out_specs=tuple([VMEM] * len(spans)),
        scratch_shapes=[pltpu.SemaphoreType.DMA((len(spans),))],
        compiler_params=pltpu.CompilerParams(vmem_limit_bytes=8 << 20),
        cost_estimate=SMALL,
        name="load_pieces",
    )(pltpu.with_memory_space_constraint(panel, pltpu.HBM))


def cut_kernel(spans, panel, *refs):
    outs, (rows, sem, out_sem) = refs[:-3], refs[-3:]
    steps = []
    for i, (start, size) in enumerate(spans):
        for at in range(0, size, TILE):
            steps.append((i, start + at, at, min(TILE, size - at)))

    def load(number):
        _, row, _, size = steps[number]
        part = pl.ds(row, size)
        return pltpu.make_async_copy(panel.at[part, :], rows.at[part, :], sem.at[number])

    for number in range(len(steps)):
        load(number).start()
    for number, (i, row, at, size) in enumerate(steps):
        load(number).wait()
        pltpu.make_async_copy(rows.at[pl.ds(row, size), :], outs[i].at[pl.ds(at, size), :], out_sem.at[i]).start()
    for i, (start, size) in enumerate(spans):
        pltpu.make_async_copy(rows.at[pl.ds(start, size), :], outs[i], out_sem.at[i]).wait()


def cut(panel, spans):
    count = sum(-(-size // TILE) for _, size in spans)
    return pl.pallas_call(
        lambda *refs: cut_kernel(spans, *refs),
        out_shape=tuple(jax.ShapeDtypeStruct((size, panel.shape[1]), panel.dtype) for _, size in spans),
        in_specs=[pl.BlockSpec(memory_space=pltpu.HBM)],
        out_specs=tuple([HBM] * len(spans)),
        scratch_shapes=[
            pltpu.VMEM(panel.shape, panel.dtype),
            pltpu.SemaphoreType.DMA((count,)),
            pltpu.SemaphoreType.DMA((len(spans),)),
        ],
        compiler_params=pltpu.CompilerParams(vmem_limit_bytes=8 << 20),
        cost_estimate=SMALL,
        name="cut",
    )(pltpu.with_memory_space_constraint(panel, pltpu.HBM))


def pick_kernel(info, pivots, slab, send, keep, rows, sem, top_sem):
    copy = pltpu.make_async_copy(slab, rows, sem)
    copy.start()
    place = info[1]
    count = rows.shape[0]
    block = send.shape[0]
    first = place * count

    def fill(picked, top):
        load = pltpu.make_async_copy(slab.at[pl.ds(0, block), :], top, top_sem)

        @pl.when(place == 0)
        def _():
            load.start()

        @pl.when(place != 0)
        def _():
            top[...] = jnp.zeros_like(top)

        copy.wait()

        @pl.loop(0, block // 8)
        def _(group):
            base = pl.multiple_of(group * 8, 8)
            for j in range(8):
                row = pivots[base + j] - first
                owned = (row >= 0) & (row < count)
                value = rows[pl.ds(jnp.where(owned, row, 0), 1), :]
                picked[pl.ds(base + j, 1), :] = jnp.where(owned, value, 0.0)

        @pl.when(place == 0)
        def _():
            load.wait()

    @pl.when(place % 2 == 0)
    def _():
        fill(keep, send)

    @pl.when(place % 2 == 1)
    def _():
        fill(send, keep)


def pick(info, pivots, slab, block):
    columns = slab.shape[1]
    shape = jax.ShapeDtypeStruct((block, columns), slab.dtype)
    return pl.pallas_call(
        pick_kernel,
        out_shape=(shape, shape),
        grid_spec=pltpu.PrefetchScalarGridSpec(
            num_scalar_prefetch=2,
            grid=(),
            in_specs=[HBM],
            out_specs=(VMEM, VMEM),
            scratch_shapes=[
                pltpu.VMEM(slab.shape, slab.dtype),
                pltpu.SemaphoreType.DMA,
                pltpu.SemaphoreType.DMA,
            ],
        ),
        compiler_params=pltpu.CompilerParams(vmem_limit_bytes=16 << 20),
        cost_estimate=SMALL,
        name="pick",
    )(info, pivots, slab)


def upper_kernel(width, info, total, other, inverse, upper, terms, across_terms, last_terms):
    block = upper.shape[0]

    def fill(picked):
        upper[...] = dot(left_terms(inverse[...]), right_terms(picked[...]))

    @pl.when(info[1] % 2 == 0)
    def _():
        fill(total)

    @pl.when(info[1] % 2 == 1)
    def _():
        fill(other)

    for shard in range(4):
        value = right_terms(upper[aligned((info[0] ^ shard) * width, width), :])
        if shard == 2:
            across_terms[...] = value
        if shard < 3:
            terms[pl.ds(shard * 3 * width, 3 * width), :] = value
        else:
            last_terms[...] = value


def make_upper(info, total, other, inverse, width):
    block, columns = total.shape
    return pl.pallas_call(
        lambda *refs: upper_kernel(width, *refs),
        out_shape=(
            jax.ShapeDtypeStruct((block, columns), total.dtype),
            jax.ShapeDtypeStruct((9 * width, columns), jnp.bfloat16),
            jax.ShapeDtypeStruct((3 * width, columns), jnp.bfloat16),
            jax.ShapeDtypeStruct((3 * width, columns), jnp.bfloat16),
        ),
        grid_spec=pltpu.PrefetchScalarGridSpec(
            num_scalar_prefetch=1,
            grid=(),
            in_specs=[VMEM] * 3,
            out_specs=(VMEM, VMEM, VMEM, VMEM),
        ),
        compiler_params=pltpu.CompilerParams(vmem_limit_bytes=24 << 20),
        cost_estimate=SMALL,
        name="upper",
    )(info, total, other, inverse)


def main_kernel(tile, info, pivots, slab, total, other, own, near, *refs):
    *across, upper, terms, out, own_rows, near_rows, across_rows, sem, panel_sem = refs
    copy = pltpu.make_async_copy(slab, out, sem)
    copy.start()
    loads = [(own, own_rows), (near, near_rows)]
    at = 0
    for piece in across:
        loads.append((piece, across_rows.at[pl.ds(at, piece.shape[0]), :]))
        at += piece.shape[0]
    loads = [pltpu.make_async_copy(a, b, panel_sem.at[i]) for i, (a, b) in enumerate(loads)]
    for load in loads:
        load.start()
    place = info[1]
    count = own_rows.shape[0]
    block = upper.shape[0]
    first = place * count
    copy.wait()

    def fill(old_top):
        @pl.loop(0, block // 8)
        def _(group):
            base = pl.multiple_of(group * 8, 8)
            for j in range(8):
                row = pivots[base + j] - first
                owned = (row >= 0) & (row < count)
                place_at = pl.ds(jnp.where(owned, row, 0), 1)
                out[place_at, :] = jnp.where(owned, old_top[pl.ds(base + j, 1), :], out[place_at, :])

    @pl.when(place % 2 == 0)
    def _():
        fill(other)

    @pl.when(place % 2 == 1)
    def _():
        fill(total)

    for load in loads:
        load.wait()

    def subtract(part, panels):
        left = jnp.concatenate([left_terms(panel[part, :]) for panel in panels], axis=1)
        out[part, :] = out[part, :] - dot(left, terms[pl.ds(0, left.shape[1]), :])

    @pl.loop(0, at // tile)
    def _(t):
        part = aligned(t * tile, tile)
        subtract(part, (own_rows, near_rows, across_rows))

        @pl.when((place == 0) & (t < block // tile))
        def _():
            out[part, :] = upper[aligned(jnp.minimum(t * tile, block - tile), tile), :]

    if at % tile:
        subtract(pl.ds(at - at % tile, at % tile), (own_rows, near_rows, across_rows))
    subtract(pl.ds(at, count - at), (own_rows, near_rows))


def main_update(info, pivots, slab, total, other, own, near, across, upper, terms):
    block = upper.shape[0]
    return pl.pallas_call(
        lambda *refs: main_kernel(min(TILE, block), *refs),
        out_shape=jax.ShapeDtypeStruct(slab.shape, slab.dtype),
        grid_spec=pltpu.PrefetchScalarGridSpec(
            num_scalar_prefetch=2,
            grid=(),
            in_specs=[HBM, VMEM, VMEM, HBM, HBM] + [HBM] * len(across) + [VMEM, VMEM],
            out_specs=VMEM,
            scratch_shapes=[pltpu.VMEM(own.shape, own.dtype)] * 2
            + [pltpu.VMEM((sum(piece.shape[0] for piece in across), own.shape[1]), own.dtype)]
            + [pltpu.SemaphoreType.DMA, pltpu.SemaphoreType.DMA((2 + len(across),))],
        ),
        compiler_params=pltpu.CompilerParams(vmem_limit_bytes=32 << 20),
        cost_estimate=SMALL,
        name="main_update",
    )(info, pivots, slab, total, other, own, near, *across, upper, terms)


def last_kernel(first_row, block, tile, segments, base, *refs):
    out, result, sem = refs[-3:]
    at = 0
    for count, groups in segments:
        for inner in range(0, count, tile):
            size = min(tile, count - inner)
            part = pl.ds(at, size)
            row = first_row + at
            delta = None
            for terms, pieces in groups:
                left = sum(refs[piece][pl.ds(offset + inner, size), :] for piece, offset in pieces)
                change = dot(left_terms(left), refs[terms][...])
                delta = change if delta is None else delta + change
            if row < block:
                delta = jnp.where(lax.axis_index("prow") == 0, 0.0, delta)
            result[part, :] = base[pl.ds(row, size), :] - delta
            pltpu.make_async_copy(result.at[part, :], out.at[pl.ds(row, size), :], sem).start()
            at += size
    pltpu.make_async_copy(result, out.at[pl.ds(first_row, at), :], sem).wait()


def last_update(base, arrays, segments, block, first_row, done):
    count = sum(size for size, _ in segments)
    return pl.pallas_call(
        lambda *refs: last_kernel(first_row, block, min(LAST_TILE, block), segments, *refs),
        out_shape=jax.ShapeDtypeStruct(base.shape, base.dtype),
        in_specs=[VMEM] * (1 + len(arrays)) + [HBM] * len(done),
        out_specs=HBM,
        scratch_shapes=[pltpu.VMEM((count, base.shape[1]), base.dtype), pltpu.SemaphoreType.DMA],
        input_output_aliases={1 + len(arrays): 0} if done else {},
        compiler_params=pltpu.CompilerParams(vmem_limit_bytes=24 << 20),
        cost_estimate=SMALL,
        name="last_update",
    )(base, *arrays, *done)


def exchange(value, bit, count):
    return lax.ppermute(value, "prow", [(i, i ^ (1 << bit)) for i in range(count)])


def on_rows(value, rows, pairs):
    return lax.ppermute(
        value, ("prow", "pcol"), [(4 * row + a, 4 * row + b) for row in rows for a, b in pairs]
    )


def solution(mesh):
    row_parts, column_parts = mesh.shape["prow"], mesh.shape["pcol"]
    bits = row_parts.bit_length() - 1
    if column_parts != 4 or row_parts != 1 << bits or bits < 1:
        raise ValueError("unsupported mesh")

    def shards(panel, slab, pivots, diag_inverse):
        rows_here = slab.shape[0]
        width = panel.shape[1]
        block = diag_inverse.shape[0]
        place = lax.axis_index("prow")
        column = lax.axis_index("pcol")
        info = jnp.stack([column, place]).astype(jnp.int32)

        first, second, last = (rows_here * part // sum(PIECES) for part in PIECES)
        first_mid, second_mid, _ = (rows_here * part // sum(PIECES) for part in MIDDLE_PIECES)
        early = first + second
        if second > block or second % min(LAST_TILE, block):
            raise ValueError("unsupported sizes")
        below = [row for row in range(row_parts) if row]
        near = lax.ppermute(panel, "pcol", SWAP)
        pieces = cut(panel, [(second, first), (0, second)])
        across = [lax.ppermute(pieces[0], "pcol", ACROSS), on_rows(pieces[1], below, ACROSS)]

        def gather_rows(slab, pivots):
            send, keep = pick(info, pivots, slab, block)
            total = keep + exchange(send, 0, row_parts)
            halves = [total[: block // 2], total[block // 2 :]]
            orders = [list(range(1, bits)), list(range(1, bits))[::-1]]
            for step in range(bits - 1):
                other = [exchange(half, order[step], row_parts) for half, order in zip(halves, orders)]
                halves = [half + part for half, part in zip(halves, other)]
            total = jnp.concatenate(halves, axis=0)
            return total, exchange(total, 0, row_parts)

        def no_rows(slab, pivots):
            return slab[:block], slab[:block]

        total, other = lax.cond(pivots[0] >= 0, gather_rows, no_rows, slab, pivots)
        upper, terms, across_terms, last_terms = make_upper(info, total, other, diag_inverse, width)
        later, upper = lax.optimization_barrier((panel, upper))
        head, upper = lax.optimization_barrier((across[0], upper))
        head_mid, rest_mid, tail = load_pieces(
            later, [(second_mid, first_mid), (0, second_mid), (early, last)]
        )
        tail_mid = lax.ppermute(tail, "pcol", MIDDLE)
        far = lax.ppermute(tail, "pcol", FAR)
        head_end = lax.ppermute(head, "pcol", ENDS)
        rest, head_mid, near = lax.optimization_barrier((across[1], head_mid, near))
        rest_mid, far, near = lax.optimization_barrier((rest_mid, far, near))
        head_mid = lax.ppermute(head_mid, "pcol", MIDDLE)
        rest_mid = lax.ppermute(rest_mid, "pcol", MIDDLE)
        rest_end = on_rows(rest, below, ENDS)
        both, rest = lax.optimization_barrier((jnp.concatenate([far, tail_mid], axis=0), rest))
        both = lax.ppermute(both, "pcol", ENDS)

        base = main_update(info, pivots, slab, total, other, panel, near, [rest, head], upper, terms)
        segments = [(first_mid, [(0, [(1, second_mid - second), (2, 0)])])]
        arrays = [last_terms, head_end, head_mid]
        result = last_update(base, arrays, segments, block, second_mid, [])
        segments = [(last, [(0, [(2, 0), (4, last)]), (1, [(3, 0), (4, 0)])])]
        arrays = [across_terms, last_terms, far, tail_mid, both]
        result = last_update(base, arrays, segments, block, early, [result])
        segments = [
            (second_mid - second, [(0, [(1, 0), (3, second)])]),
            (second, [(0, [(2, 0), (3, 0)])]),
        ]
        arrays = [last_terms, head_end, rest_end, rest_mid]
        return last_update(base, arrays, segments[::-1], block, 0, [result])

    in_specs = (P("prow", "pcol"), P("prow", "pcol"), P(), P())
    return jax.shard_map(
        shards, mesh=mesh, in_specs=in_specs, out_specs=P("prow", "pcol"), check_vma=False
    )
```

```python
import jax
import jax.numpy as jnp
from jax import lax
from jax.experimental import pallas as pl
from jax.experimental.pallas import tpu as pltpu
from jax.sharding import PartitionSpec as P

SWAP = [(0, 1), (1, 0), (2, 3), (3, 2)]
ACROSS = [(0, 2), (1, 3), (2, 0), (3, 1)]
MIDDLE = [(1, 2), (2, 1)]
ENDS = [(2, 3), (1, 0)]
FAR = [(0, 2), (3, 1)]
PIECES = (85, 16, 27)
MIDDLE_PIECES = (83, 18, 27)
TILE = 512
LAST_TILE = 256
SMALL = pl.CostEstimate(flops=0, bytes_accessed=0, transcendentals=0)
HBM = pl.BlockSpec(memory_space=pl.ANY)
VMEM = pl.BlockSpec(memory_space=pltpu.VMEM)


def split(x):
    high = x.astype(jnp.bfloat16)
    low = (x - high.astype(jnp.float32)).astype(jnp.bfloat16)
    return high, low


def left_terms(x):
    high, low = split(x)
    return jnp.concatenate([high, high, low], axis=1)


def right_terms(x):
    high, low = split(x)
    return jnp.concatenate([high, low, high], axis=0)


def dot(a, b):
    return jnp.dot(a, b, preferred_element_type=jnp.float32)


def aligned(start, size):
    return pl.ds(pl.multiple_of(start, size), size)


def load_kernel(spans, panel, *refs):
    outs, sem = refs[:-1], refs[-1]
    copies = [
        pltpu.make_async_copy(panel.at[pl.ds(start, size), :], out, sem.at[i])
        for i, ((start, size), out) in enumerate(zip(spans, outs))
    ]
    for copy in copies:
        copy.start()
    for copy in copies:
        copy.wait()


def load_pieces(panel, spans):
    return pl.pallas_call(
        lambda *refs: load_kernel(spans, *refs),
        out_shape=tuple(jax.ShapeDtypeStruct((size, panel.shape[1]), panel.dtype) for _, size in spans),
        in_specs=[pl.BlockSpec(memory_space=pltpu.HBM)],
        out_specs=tuple([VMEM] * len(spans)),
        scratch_shapes=[pltpu.SemaphoreType.DMA((len(spans),))],
        compiler_params=pltpu.CompilerParams(vmem_limit_bytes=8 << 20),
        cost_estimate=SMALL,
        name="load_pieces",
    )(pltpu.with_memory_space_constraint(panel, pltpu.HBM))


def cut_kernel(spans, panel, *refs):
    outs, (rows, sem, out_sem) = refs[:-3], refs[-3:]
    steps = []
    for i, (start, size) in enumerate(spans):
        for at in range(0, size, TILE):
            steps.append((i, start + at, at, min(TILE, size - at)))

    def load(number):
        _, row, _, size = steps[number]
        part = pl.ds(row, size)
        return pltpu.make_async_copy(panel.at[part, :], rows.at[part, :], sem.at[number])

    for number in range(len(steps)):
        load(number).start()
    for number, (i, row, at, size) in enumerate(steps):
        load(number).wait()
        pltpu.make_async_copy(rows.at[pl.ds(row, size), :], outs[i].at[pl.ds(at, size), :], out_sem.at[i]).start()
    for i, (start, size) in enumerate(spans):
        pltpu.make_async_copy(rows.at[pl.ds(start, size), :], outs[i], out_sem.at[i]).wait()


def cut(panel, spans):
    count = sum(-(-size // TILE) for _, size in spans)
    return pl.pallas_call(
        lambda *refs: cut_kernel(spans, *refs),
        out_shape=tuple(jax.ShapeDtypeStruct((size, panel.shape[1]), panel.dtype) for _, size in spans),
        in_specs=[pl.BlockSpec(memory_space=pltpu.HBM)],
        out_specs=tuple([HBM] * len(spans)),
        scratch_shapes=[
            pltpu.VMEM(panel.shape, panel.dtype),
            pltpu.SemaphoreType.DMA((count,)),
            pltpu.SemaphoreType.DMA((len(spans),)),
        ],
        compiler_params=pltpu.CompilerParams(vmem_limit_bytes=8 << 20),
        cost_estimate=SMALL,
        name="cut",
    )(pltpu.with_memory_space_constraint(panel, pltpu.HBM))


def pick_kernel(info, pivots, slab, send, keep, rows, sem, top_sem):
    copy = pltpu.make_async_copy(slab, rows, sem)
    copy.start()
    place = info[1]
    count = rows.shape[0]
    block = send.shape[0]
    first = place * count

    def fill(picked, top):
        load = pltpu.make_async_copy(slab.at[pl.ds(0, block), :], top, top_sem)

        @pl.when(place == 0)
        def _():
            load.start()

        @pl.when(place != 0)
        def _():
            top[...] = jnp.zeros_like(top)

        copy.wait()

        @pl.loop(0, block // 8)
        def _(group):
            base = pl.multiple_of(group * 8, 8)
            for j in range(8):
                row = pivots[base + j] - first
                owned = (row >= 0) & (row < count)
                value = rows[pl.ds(jnp.where(owned, row, 0), 1), :]
                picked[pl.ds(base + j, 1), :] = jnp.where(owned, value, 0.0)

        @pl.when(place == 0)
        def _():
            load.wait()

    @pl.when(place % 2 == 0)
    def _():
        fill(keep, send)

    @pl.when(place % 2 == 1)
    def _():
        fill(send, keep)


def pick(info, pivots, slab, block):
    columns = slab.shape[1]
    shape = jax.ShapeDtypeStruct((block, columns), slab.dtype)
    return pl.pallas_call(
        pick_kernel,
        out_shape=(shape, shape),
        grid_spec=pltpu.PrefetchScalarGridSpec(
            num_scalar_prefetch=2,
            grid=(),
            in_specs=[HBM],
            out_specs=(VMEM, VMEM),
            scratch_shapes=[
                pltpu.VMEM(slab.shape, slab.dtype),
                pltpu.SemaphoreType.DMA,
                pltpu.SemaphoreType.DMA,
            ],
        ),
        compiler_params=pltpu.CompilerParams(vmem_limit_bytes=16 << 20),
        cost_estimate=SMALL,
        name="pick",
    )(info, pivots, slab)


def upper_kernel(width, info, total, other, inverse, upper, terms, across_terms, last_terms):
    block = upper.shape[0]

    def fill(picked):
        upper[...] = dot(left_terms(inverse[...]), right_terms(picked[...]))

    @pl.when(info[1] % 2 == 0)
    def _():
        fill(total)

    @pl.when(info[1] % 2 == 1)
    def _():
        fill(other)

    for shard in range(4):
        value = right_terms(upper[aligned((info[0] ^ shard) * width, width), :])
        if shard == 2:
            across_terms[...] = value
        if shard < 3:
            terms[pl.ds(shard * 3 * width, 3 * width), :] = value
        else:
            last_terms[...] = value


def make_upper(info, total, other, inverse, width):
    block, columns = total.shape
    return pl.pallas_call(
        lambda *refs: upper_kernel(width, *refs),
        out_shape=(
            jax.ShapeDtypeStruct((block, columns), total.dtype),
            jax.ShapeDtypeStruct((9 * width, columns), jnp.bfloat16),
            jax.ShapeDtypeStruct((3 * width, columns), jnp.bfloat16),
            jax.ShapeDtypeStruct((3 * width, columns), jnp.bfloat16),
        ),
        grid_spec=pltpu.PrefetchScalarGridSpec(
            num_scalar_prefetch=1,
            grid=(),
            in_specs=[VMEM] * 3,
            out_specs=(VMEM, VMEM, VMEM, VMEM),
        ),
        compiler_params=pltpu.CompilerParams(vmem_limit_bytes=24 << 20),
        cost_estimate=SMALL,
        name="upper",
    )(info, total, other, inverse)


def main_kernel(tile, info, pivots, slab, total, other, own, near, *refs):
    *across, upper, terms, out, own_rows, near_rows, across_rows, sem, panel_sem = refs
    copy = pltpu.make_async_copy(slab, out, sem)
    copy.start()
    loads = [(own, own_rows), (near, near_rows)]
    at = 0
    for piece in across:
        loads.append((piece, across_rows.at[pl.ds(at, piece.shape[0]), :]))
        at += piece.shape[0]
    loads = [pltpu.make_async_copy(a, b, panel_sem.at[i]) for i, (a, b) in enumerate(loads)]
    for load in loads:
        load.start()
    place = info[1]
    count = own_rows.shape[0]
    block = upper.shape[0]
    first = place * count
    copy.wait()

    def fill(old_top):
        @pl.loop(0, block // 8)
        def _(group):
            base = pl.multiple_of(group * 8, 8)
            for j in range(8):
                row = pivots[base + j] - first
                owned = (row >= 0) & (row < count)
                place_at = pl.ds(jnp.where(owned, row, 0), 1)
                out[place_at, :] = jnp.where(owned, old_top[pl.ds(base + j, 1), :], out[place_at, :])

    @pl.when(place % 2 == 0)
    def _():
        fill(other)

    @pl.when(place % 2 == 1)
    def _():
        fill(total)

    for load in loads:
        load.wait()

    def subtract(part, panels):
        left = jnp.concatenate([left_terms(panel[part, :]) for panel in panels], axis=1)
        out[part, :] = out[part, :] - dot(left, terms[pl.ds(0, left.shape[1]), :])

    @pl.loop(0, at // tile)
    def _(t):
        part = aligned(t * tile, tile)
        subtract(part, (own_rows, near_rows, across_rows))

        @pl.when((place == 0) & (t < block // tile))
        def _():
            out[part, :] = upper[aligned(jnp.minimum(t * tile, block - tile), tile), :]

    if at % tile:
        subtract(pl.ds(at - at % tile, at % tile), (own_rows, near_rows, across_rows))
    subtract(pl.ds(at, count - at), (own_rows, near_rows))


def main_update(info, pivots, slab, total, other, own, near, across, upper, terms):
    block = upper.shape[0]
    return pl.pallas_call(
        lambda *refs: main_kernel(min(TILE, block), *refs),
        out_shape=jax.ShapeDtypeStruct(slab.shape, slab.dtype),
        grid_spec=pltpu.PrefetchScalarGridSpec(
            num_scalar_prefetch=2,
            grid=(),
            in_specs=[HBM, VMEM, VMEM, HBM, HBM] + [HBM] * len(across) + [VMEM, VMEM],
            out_specs=VMEM,
            scratch_shapes=[pltpu.VMEM(own.shape, own.dtype)] * 2
            + [pltpu.VMEM((sum(piece.shape[0] for piece in across), own.shape[1]), own.dtype)]
            + [pltpu.SemaphoreType.DMA, pltpu.SemaphoreType.DMA((2 + len(across),))],
        ),
        compiler_params=pltpu.CompilerParams(vmem_limit_bytes=32 << 20),
        cost_estimate=SMALL,
        name="main_update",
    )(info, pivots, slab, total, other, own, near, *across, upper, terms)


def last_kernel(first_row, block, tile, segments, base, *refs):
    out, result, sem = refs[-3:]
    at = 0
    for count, groups in segments:
        for inner in range(0, count, tile):
            size = min(tile, count - inner)
            part = pl.ds(at, size)
            row = first_row + at
            delta = None
            for terms, pieces in groups:
                left = sum(refs[piece][pl.ds(offset + inner, size), :] for piece, offset in pieces)
                change = dot(left_terms(left), refs[terms][...])
                delta = change if delta is None else delta + change
            if row < block:
                delta = jnp.where(lax.axis_index("prow") == 0, 0.0, delta)
            result[part, :] = base[pl.ds(row, size), :] - delta
            pltpu.make_async_copy(result.at[part, :], out.at[pl.ds(row, size), :], sem).start()
            at += size
    pltpu.make_async_copy(result, out.at[pl.ds(first_row, at), :], sem).wait()


def last_update(base, arrays, segments, block, first_row, done):
    count = sum(size for size, _ in segments)
    return pl.pallas_call(
        lambda *refs: last_kernel(first_row, block, min(LAST_TILE, block), segments, *refs),
        out_shape=jax.ShapeDtypeStruct(base.shape, base.dtype),
        in_specs=[VMEM] * (1 + len(arrays)) + [HBM] * len(done),
        out_specs=HBM,
        scratch_shapes=[pltpu.VMEM((count, base.shape[1]), base.dtype), pltpu.SemaphoreType.DMA],
        input_output_aliases={1 + len(arrays): 0} if done else {},
        compiler_params=pltpu.CompilerParams(vmem_limit_bytes=24 << 20),
        cost_estimate=SMALL,
        name="last_update",
    )(base, *arrays, *done)


def exchange(value, bit, count):
    return lax.ppermute(value, "prow", [(i, i ^ (1 << bit)) for i in range(count)])


def on_rows(value, rows, pairs):
    return lax.ppermute(
        value, ("prow", "pcol"), [(4 * row + a, 4 * row + b) for row in rows for a, b in pairs]
    )


def solution(mesh):
    row_parts, column_parts = mesh.shape["prow"], mesh.shape["pcol"]
    bits = row_parts.bit_length() - 1
    if column_parts != 4 or row_parts != 1 << bits or bits < 1:
        raise ValueError("unsupported mesh")

    def shards(panel, slab, pivots, diag_inverse):
        rows_here = slab.shape[0]
        width = panel.shape[1]
        block = diag_inverse.shape[0]
        place = lax.axis_index("prow")
        column = lax.axis_index("pcol")
        info = jnp.stack([column, place]).astype(jnp.int32)

        first, second, last = (rows_here * part // sum(PIECES) for part in PIECES)
        first_mid, second_mid, _ = (rows_here * part // sum(PIECES) for part in MIDDLE_PIECES)
        early = first + second
        if second > block or second % min(LAST_TILE, block):
            raise ValueError("unsupported sizes")
        below = [row for row in range(row_parts) if row]
        near = lax.ppermute(panel, "pcol", SWAP)
        pieces = cut(panel, [(second, first), (0, second)])
        across = [lax.ppermute(pieces[0], "pcol", ACROSS), on_rows(pieces[1], below, ACROSS)]
        tail = panel[early:]
        tail_mid = lax.ppermute(tail, "pcol", MIDDLE)

        def gather_rows(slab, pivots):
            send, keep = pick(info, pivots, slab, block)
            total = keep + exchange(send, 0, row_parts)
            for bit in range(1, bits):
                total = total + exchange(total, bit, row_parts)
            return total, exchange(total, 0, row_parts)

        def no_rows(slab, pivots):
            return slab[:block], slab[:block]

        total, other = lax.cond(pivots[0] >= 0, gather_rows, no_rows, slab, pivots)
        tail, total = lax.optimization_barrier((tail, total))
        far = lax.ppermute(tail, "pcol", FAR)
        head, tail_mid, total = lax.optimization_barrier((across[0], tail_mid, total))
        upper, terms, across_terms, last_terms = make_upper(info, total, other, diag_inverse, width)
        later, upper = lax.optimization_barrier((panel, upper))
        head_mid, rest_mid = load_pieces(later, [(second_mid, first_mid), (0, second_mid)])
        head_end = lax.ppermute(head, "pcol", ENDS)
        rest, head_mid, near = lax.optimization_barrier((across[1], head_mid, near))
        rest_mid, far, near = lax.optimization_barrier((rest_mid, far, near))
        head_mid = lax.ppermute(head_mid, "pcol", MIDDLE)
        rest_mid = lax.ppermute(rest_mid, "pcol", MIDDLE)
        rest_end = on_rows(rest, below, ENDS)
        both, rest = lax.optimization_barrier((jnp.concatenate([far, tail_mid], axis=0), rest))
        both = lax.ppermute(both, "pcol", ENDS)

        base = main_update(info, pivots, slab, total, other, panel, near, [rest, head], upper, terms)
        segments = [(first_mid, [(0, [(1, second_mid - second), (2, 0)])])]
        arrays = [last_terms, head_end, head_mid]
        result = last_update(base, arrays, segments, block, second_mid, [])
        segments = [(last, [(0, [(2, 0), (4, last)]), (1, [(3, 0), (4, 0)])])]
        arrays = [across_terms, last_terms, far, tail_mid, both]
        result = last_update(base, arrays, segments, block, early, [result])
        segments = [
            (second_mid - second, [(0, [(1, 0), (3, second)])]),
            (second, [(0, [(2, 0), (3, 0)])]),
        ]
        arrays = [last_terms, head_end, rest_end, rest_mid]
        return last_update(base, arrays, segments[::-1], block, 0, [result])

    in_specs = (P("prow", "pcol"), P("prow", "pcol"), P(), P())
    return jax.shard_map(
        shards, mesh=mesh, in_specs=in_specs, out_specs=P("prow", "pcol"), check_vma=False
    )
```

```python
import jax
import jax.numpy as jnp
from jax import lax
from jax.experimental import pallas as pl
from jax.experimental.pallas import tpu as pltpu
from jax.sharding import PartitionSpec as P

SWAP = [(0, 1), (1, 0), (2, 3), (3, 2)]
ACROSS = [(0, 2), (1, 3), (2, 0), (3, 1)]
MIDDLE = [(1, 2), (2, 1)]
ENDS = [(2, 3), (1, 0)]
FAR = [(0, 2), (3, 1)]
PIECES = (85, 16, 27)
MIDDLE_PIECES = (83, 18, 27)
TILE = 512
LAST_TILE = 256
SMALL = pl.CostEstimate(flops=0, bytes_accessed=0, transcendentals=0)
HBM = pl.BlockSpec(memory_space=pl.ANY)
VMEM = pl.BlockSpec(memory_space=pltpu.VMEM)


def split(x):
    high = x.astype(jnp.bfloat16)
    low = (x - high.astype(jnp.float32)).astype(jnp.bfloat16)
    return high, low


def left_terms(x):
    high, low = split(x)
    return jnp.concatenate([high, high, low], axis=1)


def right_terms(x):
    high, low = split(x)
    return jnp.concatenate([high, low, high], axis=0)


def dot(a, b):
    return jnp.dot(a, b, preferred_element_type=jnp.float32)


def aligned(start, size):
    return pl.ds(pl.multiple_of(start, size), size)


def load_kernel(spans, panel, *refs):
    outs, sem = refs[:-1], refs[-1]
    copies = [
        pltpu.make_async_copy(panel.at[pl.ds(start, size), :], out, sem.at[i])
        for i, ((start, size), out) in enumerate(zip(spans, outs))
    ]
    for copy in copies:
        copy.start()
    for copy in copies:
        copy.wait()


def load_pieces(panel, spans):
    return pl.pallas_call(
        lambda *refs: load_kernel(spans, *refs),
        out_shape=tuple(jax.ShapeDtypeStruct((size, panel.shape[1]), panel.dtype) for _, size in spans),
        in_specs=[pl.BlockSpec(memory_space=pltpu.HBM)],
        out_specs=tuple([VMEM] * len(spans)),
        scratch_shapes=[pltpu.SemaphoreType.DMA((len(spans),))],
        compiler_params=pltpu.CompilerParams(vmem_limit_bytes=8 << 20),
        cost_estimate=SMALL,
        name="load_pieces",
    )(pltpu.with_memory_space_constraint(panel, pltpu.HBM))


def cut_kernel(spans, panel, *refs):
    outs, (rows, sem, out_sem) = refs[:-3], refs[-3:]
    steps = []
    for i, (start, size) in enumerate(spans):
        for at in range(0, size, TILE):
            steps.append((i, start + at, at, min(TILE, size - at)))

    def load(number):
        _, row, _, size = steps[number]
        part = pl.ds(row, size)
        return pltpu.make_async_copy(panel.at[part, :], rows.at[part, :], sem.at[number])

    for number in range(len(steps)):
        load(number).start()
    for number, (i, row, at, size) in enumerate(steps):
        load(number).wait()
        pltpu.make_async_copy(rows.at[pl.ds(row, size), :], outs[i].at[pl.ds(at, size), :], out_sem.at[i]).start()
    for i, (start, size) in enumerate(spans):
        pltpu.make_async_copy(rows.at[pl.ds(start, size), :], outs[i], out_sem.at[i]).wait()


def cut(panel, spans):
    count = sum(-(-size // TILE) for _, size in spans)
    return pl.pallas_call(
        lambda *refs: cut_kernel(spans, *refs),
        out_shape=tuple(jax.ShapeDtypeStruct((size, panel.shape[1]), panel.dtype) for _, size in spans),
        in_specs=[pl.BlockSpec(memory_space=pltpu.HBM)],
        out_specs=tuple([HBM] * len(spans)),
        scratch_shapes=[
            pltpu.VMEM(panel.shape, panel.dtype),
            pltpu.SemaphoreType.DMA((count,)),
            pltpu.SemaphoreType.DMA((len(spans),)),
        ],
        compiler_params=pltpu.CompilerParams(vmem_limit_bytes=8 << 20),
        cost_estimate=SMALL,
        name="cut",
    )(pltpu.with_memory_space_constraint(panel, pltpu.HBM))


def pick_kernel(info, pivots, slab, send, keep, rows, sem, top_sem):
    copy = pltpu.make_async_copy(slab, rows, sem)
    copy.start()
    place = info[1]
    count = rows.shape[0]
    block = send.shape[0]
    first = place * count

    def fill(picked, top):
        load = pltpu.make_async_copy(slab.at[pl.ds(0, block), :], top, top_sem)

        @pl.when(place == 0)
        def _():
            load.start()

        @pl.when(place != 0)
        def _():
            top[...] = jnp.zeros_like(top)

        copy.wait()

        @pl.loop(0, block // 8)
        def _(group):
            base = pl.multiple_of(group * 8, 8)
            for j in range(8):
                row = pivots[base + j] - first
                owned = (row >= 0) & (row < count)
                value = rows[pl.ds(jnp.where(owned, row, 0), 1), :]
                picked[pl.ds(base + j, 1), :] = jnp.where(owned, value, 0.0)

        @pl.when(place == 0)
        def _():
            load.wait()

    @pl.when(place % 2 == 0)
    def _():
        fill(keep, send)

    @pl.when(place % 2 == 1)
    def _():
        fill(send, keep)


def pick(info, pivots, slab, block):
    columns = slab.shape[1]
    shape = jax.ShapeDtypeStruct((block, columns), slab.dtype)
    return pl.pallas_call(
        pick_kernel,
        out_shape=(shape, shape),
        grid_spec=pltpu.PrefetchScalarGridSpec(
            num_scalar_prefetch=2,
            grid=(),
            in_specs=[HBM],
            out_specs=(VMEM, VMEM),
            scratch_shapes=[
                pltpu.VMEM(slab.shape, slab.dtype),
                pltpu.SemaphoreType.DMA,
                pltpu.SemaphoreType.DMA,
            ],
        ),
        compiler_params=pltpu.CompilerParams(vmem_limit_bytes=16 << 20),
        cost_estimate=SMALL,
        name="pick",
    )(info, pivots, slab)


def upper_kernel(width, info, total, other, inverse, upper, terms, across_terms, last_terms):
    block = upper.shape[0]

    def fill(picked):
        upper[...] = dot(left_terms(inverse[...]), right_terms(picked[...]))

    @pl.when(info[1] % 2 == 0)
    def _():
        fill(total)

    @pl.when(info[1] % 2 == 1)
    def _():
        fill(other)

    for shard in range(4):
        value = right_terms(upper[aligned((info[0] ^ shard) * width, width), :])
        if shard == 2:
            across_terms[...] = value
        if shard < 3:
            terms[pl.ds(shard * 3 * width, 3 * width), :] = value
        else:
            last_terms[...] = value


def make_upper(info, total, other, inverse, width):
    block, columns = total.shape
    return pl.pallas_call(
        lambda *refs: upper_kernel(width, *refs),
        out_shape=(
            jax.ShapeDtypeStruct((block, columns), total.dtype),
            jax.ShapeDtypeStruct((9 * width, columns), jnp.bfloat16),
            jax.ShapeDtypeStruct((3 * width, columns), jnp.bfloat16),
            jax.ShapeDtypeStruct((3 * width, columns), jnp.bfloat16),
        ),
        grid_spec=pltpu.PrefetchScalarGridSpec(
            num_scalar_prefetch=1,
            grid=(),
            in_specs=[VMEM] * 3,
            out_specs=(VMEM, VMEM, VMEM, VMEM),
        ),
        compiler_params=pltpu.CompilerParams(vmem_limit_bytes=24 << 20),
        cost_estimate=SMALL,
        name="upper",
    )(info, total, other, inverse)


def main_kernel(tile, info, pivots, slab, total, other, own, near, *refs):
    *across, upper, terms, out, own_rows, near_rows, across_rows, sem, panel_sem = refs
    copy = pltpu.make_async_copy(slab, out, sem)
    copy.start()
    loads = [(own, own_rows), (near, near_rows)]
    at = 0
    for piece in across:
        loads.append((piece, across_rows.at[pl.ds(at, piece.shape[0]), :]))
        at += piece.shape[0]
    loads = [pltpu.make_async_copy(a, b, panel_sem.at[i]) for i, (a, b) in enumerate(loads)]
    for load in loads:
        load.start()
    place = info[1]
    count = own_rows.shape[0]
    block = upper.shape[0]
    first = place * count
    copy.wait()

    def fill(old_top):
        @pl.loop(0, block // 8)
        def _(group):
            base = pl.multiple_of(group * 8, 8)
            for j in range(8):
                row = pivots[base + j] - first
                owned = (row >= 0) & (row < count)
                place_at = pl.ds(jnp.where(owned, row, 0), 1)
                out[place_at, :] = jnp.where(owned, old_top[pl.ds(base + j, 1), :], out[place_at, :])

    @pl.when(place % 2 == 0)
    def _():
        fill(other)

    @pl.when(place % 2 == 1)
    def _():
        fill(total)

    for load in loads:
        load.wait()

    def subtract(part, panels):
        left = jnp.concatenate([left_terms(panel[part, :]) for panel in panels], axis=1)
        out[part, :] = out[part, :] - dot(left, terms[pl.ds(0, left.shape[1]), :])

    @pl.loop(0, at // tile)
    def _(t):
        part = aligned(t * tile, tile)
        subtract(part, (own_rows, near_rows, across_rows))

        @pl.when((place == 0) & (t < block // tile))
        def _():
            out[part, :] = upper[aligned(jnp.minimum(t * tile, block - tile), tile), :]

    if at % tile:
        subtract(pl.ds(at - at % tile, at % tile), (own_rows, near_rows, across_rows))
    subtract(pl.ds(at, count - at), (own_rows, near_rows))


def main_update(info, pivots, slab, total, other, own, near, across, upper, terms):
    block = upper.shape[0]
    return pl.pallas_call(
        lambda *refs: main_kernel(min(TILE, block), *refs),
        out_shape=jax.ShapeDtypeStruct(slab.shape, slab.dtype),
        grid_spec=pltpu.PrefetchScalarGridSpec(
            num_scalar_prefetch=2,
            grid=(),
            in_specs=[HBM, VMEM, VMEM, HBM, HBM] + [HBM] * len(across) + [VMEM, VMEM],
            out_specs=VMEM,
            scratch_shapes=[pltpu.VMEM(own.shape, own.dtype)] * 2
            + [pltpu.VMEM((sum(piece.shape[0] for piece in across), own.shape[1]), own.dtype)]
            + [pltpu.SemaphoreType.DMA, pltpu.SemaphoreType.DMA((2 + len(across),))],
        ),
        compiler_params=pltpu.CompilerParams(vmem_limit_bytes=32 << 20),
        cost_estimate=SMALL,
        name="main_update",
    )(info, pivots, slab, total, other, own, near, *across, upper, terms)


def last_kernel(first_row, block, tile, segments, base, *refs):
    out, result, sem = refs[-3:]
    at = 0
    for count, groups in segments:
        for inner in range(0, count, tile):
            size = min(tile, count - inner)
            part = pl.ds(at, size)
            row = first_row + at
            delta = None
            for terms, pieces in groups:
                left = sum(refs[piece][pl.ds(offset + inner, size), :] for piece, offset in pieces)
                change = dot(left_terms(left), refs[terms][...])
                delta = change if delta is None else delta + change
            if row < block:
                delta = jnp.where(lax.axis_index("prow") == 0, 0.0, delta)
            result[part, :] = base[pl.ds(row, size), :] - delta
            pltpu.make_async_copy(result.at[part, :], out.at[pl.ds(row, size), :], sem).start()
            at += size
    pltpu.make_async_copy(result, out.at[pl.ds(first_row, at), :], sem).wait()


def last_update(base, arrays, segments, block, first_row, done):
    count = sum(size for size, _ in segments)
    return pl.pallas_call(
        lambda *refs: last_kernel(first_row, block, min(LAST_TILE, block), segments, *refs),
        out_shape=jax.ShapeDtypeStruct(base.shape, base.dtype),
        in_specs=[VMEM] * (1 + len(arrays)) + [HBM] * len(done),
        out_specs=HBM,
        scratch_shapes=[pltpu.VMEM((count, base.shape[1]), base.dtype), pltpu.SemaphoreType.DMA],
        input_output_aliases={1 + len(arrays): 0} if done else {},
        compiler_params=pltpu.CompilerParams(vmem_limit_bytes=24 << 20),
        cost_estimate=SMALL,
        name="last_update",
    )(base, *arrays, *done)


def exchange(value, bit, count):
    return lax.ppermute(value, "prow", [(i, i ^ (1 << bit)) for i in range(count)])


def on_rows(value, rows, pairs):
    return lax.ppermute(
        value, ("prow", "pcol"), [(4 * row + a, 4 * row + b) for row in rows for a, b in pairs]
    )


def solution(mesh):
    row_parts, column_parts = mesh.shape["prow"], mesh.shape["pcol"]
    bits = row_parts.bit_length() - 1
    if column_parts != 4 or row_parts != 1 << bits or bits < 1:
        raise ValueError("unsupported mesh")

    def shards(panel, slab, pivots, diag_inverse):
        rows_here = slab.shape[0]
        width = panel.shape[1]
        block = diag_inverse.shape[0]
        place = lax.axis_index("prow")
        column = lax.axis_index("pcol")
        info = jnp.stack([column, place]).astype(jnp.int32)

        first, second, last = (rows_here * part // sum(PIECES) for part in PIECES)
        first_mid, second_mid, _ = (rows_here * part // sum(PIECES) for part in MIDDLE_PIECES)
        early = first + second
        if second > block or second % min(LAST_TILE, block):
            raise ValueError("unsupported sizes")
        below = [row for row in range(row_parts) if row]
        near = lax.ppermute(panel, "pcol", SWAP)
        pieces = cut(panel, [(second, first), (0, second)])
        across = [lax.ppermute(pieces[0], "pcol", ACROSS), on_rows(pieces[1], below, ACROSS)]
        tail = panel[early:]
        tail_mid = lax.ppermute(tail, "pcol", MIDDLE)

        def gather_rows(slab, pivots):
            send, keep = pick(info, pivots, slab, block)
            total = keep + exchange(send, 0, row_parts)
            halves = [total[: block // 2], total[block // 2 :]]
            orders = [list(range(1, bits)), list(range(1, bits))[::-1]]
            for step in range(bits - 1):
                other = [exchange(half, order[step], row_parts) for half, order in zip(halves, orders)]
                halves = [half + part for half, part in zip(halves, other)]
            total = jnp.concatenate(halves, axis=0)
            return total, exchange(total, 0, row_parts)

        def no_rows(slab, pivots):
            return slab[:block], slab[:block]

        total, other = lax.cond(pivots[0] >= 0, gather_rows, no_rows, slab, pivots)
        tail, total = lax.optimization_barrier((tail, total))
        far = lax.ppermute(tail, "pcol", FAR)
        head, total = lax.optimization_barrier((across[0], total))
        upper, terms, across_terms, last_terms = make_upper(info, total, other, diag_inverse, width)
        later, upper = lax.optimization_barrier((panel, upper))
        head_mid, rest_mid = load_pieces(later, [(second_mid, first_mid), (0, second_mid)])
        head_end = lax.ppermute(head, "pcol", ENDS)
        rest, head_mid, near = lax.optimization_barrier((across[1], head_mid, near))
        rest_mid, far, near = lax.optimization_barrier((rest_mid, far, near))
        head_mid = lax.ppermute(head_mid, "pcol", MIDDLE)
        rest_mid = lax.ppermute(rest_mid, "pcol", MIDDLE)
        rest_end = on_rows(rest, below, ENDS)
        both, rest = lax.optimization_barrier((jnp.concatenate([far, tail_mid], axis=0), rest))
        both = lax.ppermute(both, "pcol", ENDS)

        base = main_update(info, pivots, slab, total, other, panel, near, [rest, head], upper, terms)
        segments = [(first_mid, [(0, [(1, second_mid - second), (2, 0)])])]
        arrays = [last_terms, head_end, head_mid]
        result = last_update(base, arrays, segments, block, second_mid, [])
        segments = [(last, [(0, [(2, 0), (4, last)]), (1, [(3, 0), (4, 0)])])]
        arrays = [across_terms, last_terms, far, tail_mid, both]
        result = last_update(base, arrays, segments, block, early, [result])
        segments = [
            (second_mid - second, [(0, [(1, 0), (3, second)])]),
            (second, [(0, [(2, 0), (3, 0)])]),
        ]
        arrays = [last_terms, head_end, rest_end, rest_mid]
        return last_update(base, arrays, segments[::-1], block, 0, [result])

    in_specs = (P("prow", "pcol"), P("prow", "pcol"), P(), P())
    return jax.shard_map(
        shards, mesh=mesh, in_specs=in_specs, out_specs=P("prow", "pcol"), check_vma=False
    )
```

```python
import jax
import jax.numpy as jnp
from jax import lax
from jax.experimental import pallas as pl
from jax.experimental.pallas import tpu as pltpu
from jax.sharding import PartitionSpec as P

SWAP = [(0, 1), (1, 0), (2, 3), (3, 2)]
ACROSS = [(0, 2), (1, 3), (2, 0), (3, 1)]
MIDDLE = [(1, 2), (2, 1)]
ENDS = [(2, 3), (1, 0)]
FAR = [(0, 2), (3, 1)]
PIECES = (169, 32, 55)
MIDDLE_PIECES = (165, 36, 55)
TILE = 512
LAST_TILE = 256
SMALL = pl.CostEstimate(flops=0, bytes_accessed=0, transcendentals=0)
HBM = pl.BlockSpec(memory_space=pl.ANY)
VMEM = pl.BlockSpec(memory_space=pltpu.VMEM)


def split(x):
    high = x.astype(jnp.bfloat16)
    low = (x - high.astype(jnp.float32)).astype(jnp.bfloat16)
    return high, low


def left_terms(x):
    high, low = split(x)
    return jnp.concatenate([high, high, low], axis=1)


def right_terms(x):
    high, low = split(x)
    return jnp.concatenate([high, low, high], axis=0)


def dot(a, b):
    return jnp.dot(a, b, preferred_element_type=jnp.float32)


def aligned(start, size):
    return pl.ds(pl.multiple_of(start, size), size)


def load_kernel(spans, panel, *refs):
    outs, sem = refs[:-1], refs[-1]
    copies = [
        pltpu.make_async_copy(panel.at[pl.ds(start, size), :], out, sem.at[i])
        for i, ((start, size), out) in enumerate(zip(spans, outs))
    ]
    for copy in copies:
        copy.start()
    for copy in copies:
        copy.wait()


def load_pieces(panel, spans):
    return pl.pallas_call(
        lambda *refs: load_kernel(spans, *refs),
        out_shape=tuple(jax.ShapeDtypeStruct((size, panel.shape[1]), panel.dtype) for _, size in spans),
        in_specs=[pl.BlockSpec(memory_space=pltpu.HBM)],
        out_specs=tuple([VMEM] * len(spans)),
        scratch_shapes=[pltpu.SemaphoreType.DMA((len(spans),))],
        compiler_params=pltpu.CompilerParams(vmem_limit_bytes=8 << 20),
        cost_estimate=SMALL,
        name="load_pieces",
    )(pltpu.with_memory_space_constraint(panel, pltpu.HBM))


def cut_kernel(spans, panel, *refs):
    outs, (rows, sem, out_sem) = refs[:-3], refs[-3:]
    steps = []
    for i, (start, size) in enumerate(spans):
        for at in range(0, size, TILE):
            steps.append((i, start + at, at, min(TILE, size - at)))

    def load(number):
        _, row, _, size = steps[number]
        part = pl.ds(row, size)
        return pltpu.make_async_copy(panel.at[part, :], rows.at[part, :], sem.at[number])

    for number in range(len(steps)):
        load(number).start()
    for number, (i, row, at, size) in enumerate(steps):
        load(number).wait()
        pltpu.make_async_copy(rows.at[pl.ds(row, size), :], outs[i].at[pl.ds(at, size), :], out_sem.at[i]).start()
    for i, (start, size) in enumerate(spans):
        pltpu.make_async_copy(rows.at[pl.ds(start, size), :], outs[i], out_sem.at[i]).wait()


def cut(panel, spans):
    count = sum(-(-size // TILE) for _, size in spans)
    return pl.pallas_call(
        lambda *refs: cut_kernel(spans, *refs),
        out_shape=tuple(jax.ShapeDtypeStruct((size, panel.shape[1]), panel.dtype) for _, size in spans),
        in_specs=[pl.BlockSpec(memory_space=pltpu.HBM)],
        out_specs=tuple([HBM] * len(spans)),
        scratch_shapes=[
            pltpu.VMEM(panel.shape, panel.dtype),
            pltpu.SemaphoreType.DMA((count,)),
            pltpu.SemaphoreType.DMA((len(spans),)),
        ],
        compiler_params=pltpu.CompilerParams(vmem_limit_bytes=8 << 20),
        cost_estimate=SMALL,
        name="cut",
    )(pltpu.with_memory_space_constraint(panel, pltpu.HBM))


def pick_kernel(info, pivots, slab, send, keep, rows, sem, top_sem):
    copy = pltpu.make_async_copy(slab, rows, sem)
    copy.start()
    place = info[1]
    count = rows.shape[0]
    block = send.shape[0]
    first = place * count

    def fill(picked, top):
        load = pltpu.make_async_copy(slab.at[pl.ds(0, block), :], top, top_sem)

        @pl.when(place == 0)
        def _():
            load.start()

        @pl.when(place != 0)
        def _():
            top[...] = jnp.zeros_like(top)

        copy.wait()

        @pl.loop(0, block // 8)
        def _(group):
            base = pl.multiple_of(group * 8, 8)
            for j in range(8):
                row = pivots[base + j] - first
                owned = (row >= 0) & (row < count)
                value = rows[pl.ds(jnp.where(owned, row, 0), 1), :]
                picked[pl.ds(base + j, 1), :] = jnp.where(owned, value, 0.0)

        @pl.when(place == 0)
        def _():
            load.wait()

    @pl.when(place % 2 == 0)
    def _():
        fill(keep, send)

    @pl.when(place % 2 == 1)
    def _():
        fill(send, keep)


def pick(info, pivots, slab, block):
    columns = slab.shape[1]
    shape = jax.ShapeDtypeStruct((block, columns), slab.dtype)
    return pl.pallas_call(
        pick_kernel,
        out_shape=(shape, shape),
        grid_spec=pltpu.PrefetchScalarGridSpec(
            num_scalar_prefetch=2,
            grid=(),
            in_specs=[HBM],
            out_specs=(VMEM, VMEM),
            scratch_shapes=[
                pltpu.VMEM(slab.shape, slab.dtype),
                pltpu.SemaphoreType.DMA,
                pltpu.SemaphoreType.DMA,
            ],
        ),
        compiler_params=pltpu.CompilerParams(vmem_limit_bytes=16 << 20),
        cost_estimate=SMALL,
        name="pick",
    )(info, pivots, slab)


def upper_kernel(width, info, total, other, inverse, upper, terms, across_terms, last_terms):
    block = upper.shape[0]

    def fill(picked):
        upper[...] = dot(left_terms(inverse[...]), right_terms(picked[...]))

    @pl.when(info[1] % 2 == 0)
    def _():
        fill(total)

    @pl.when(info[1] % 2 == 1)
    def _():
        fill(other)

    for shard in range(4):
        value = right_terms(upper[aligned((info[0] ^ shard) * width, width), :])
        if shard == 2:
            across_terms[...] = value
        if shard < 3:
            terms[pl.ds(shard * 3 * width, 3 * width), :] = value
        else:
            last_terms[...] = value


def make_upper(info, total, other, inverse, width):
    block, columns = total.shape
    return pl.pallas_call(
        lambda *refs: upper_kernel(width, *refs),
        out_shape=(
            jax.ShapeDtypeStruct((block, columns), total.dtype),
            jax.ShapeDtypeStruct((9 * width, columns), jnp.bfloat16),
            jax.ShapeDtypeStruct((3 * width, columns), jnp.bfloat16),
            jax.ShapeDtypeStruct((3 * width, columns), jnp.bfloat16),
        ),
        grid_spec=pltpu.PrefetchScalarGridSpec(
            num_scalar_prefetch=1,
            grid=(),
            in_specs=[VMEM] * 3,
            out_specs=(VMEM, VMEM, VMEM, VMEM),
        ),
        compiler_params=pltpu.CompilerParams(vmem_limit_bytes=24 << 20),
        cost_estimate=SMALL,
        name="upper",
    )(info, total, other, inverse)


def main_kernel(tile, info, pivots, slab, total, other, own, near, *refs):
    *across, upper, terms, out, own_rows, near_rows, across_rows, sem, panel_sem = refs
    copy = pltpu.make_async_copy(slab, out, sem)
    copy.start()
    loads = [(own, own_rows), (near, near_rows)]
    at = 0
    for piece in across:
        loads.append((piece, across_rows.at[pl.ds(at, piece.shape[0]), :]))
        at += piece.shape[0]
    loads = [pltpu.make_async_copy(a, b, panel_sem.at[i]) for i, (a, b) in enumerate(loads)]
    for load in loads:
        load.start()
    place = info[1]
    count = own_rows.shape[0]
    block = upper.shape[0]
    first = place * count
    copy.wait()

    def fill(old_top):
        @pl.loop(0, block // 8)
        def _(group):
            base = pl.multiple_of(group * 8, 8)
            for j in range(8):
                row = pivots[base + j] - first
                owned = (row >= 0) & (row < count)
                place_at = pl.ds(jnp.where(owned, row, 0), 1)
                out[place_at, :] = jnp.where(owned, old_top[pl.ds(base + j, 1), :], out[place_at, :])

    @pl.when(place % 2 == 0)
    def _():
        fill(other)

    @pl.when(place % 2 == 1)
    def _():
        fill(total)

    for load in loads:
        load.wait()

    def subtract(part, panels):
        left = jnp.concatenate([left_terms(panel[part, :]) for panel in panels], axis=1)
        out[part, :] = out[part, :] - dot(left, terms[pl.ds(0, left.shape[1]), :])

    @pl.loop(0, at // tile)
    def _(t):
        part = aligned(t * tile, tile)
        subtract(part, (own_rows, near_rows, across_rows))

        @pl.when((place == 0) & (t < block // tile))
        def _():
            out[part, :] = upper[aligned(jnp.minimum(t * tile, block - tile), tile), :]

    if at % tile:
        subtract(pl.ds(at - at % tile, at % tile), (own_rows, near_rows, across_rows))
    subtract(pl.ds(at, count - at), (own_rows, near_rows))


def main_update(info, pivots, slab, total, other, own, near, across, upper, terms):
    block = upper.shape[0]
    return pl.pallas_call(
        lambda *refs: main_kernel(min(TILE, block), *refs),
        out_shape=jax.ShapeDtypeStruct(slab.shape, slab.dtype),
        grid_spec=pltpu.PrefetchScalarGridSpec(
            num_scalar_prefetch=2,
            grid=(),
            in_specs=[HBM, VMEM, VMEM, HBM, HBM] + [HBM] * len(across) + [VMEM, VMEM],
            out_specs=VMEM,
            scratch_shapes=[pltpu.VMEM(own.shape, own.dtype)] * 2
            + [pltpu.VMEM((sum(piece.shape[0] for piece in across), own.shape[1]), own.dtype)]
            + [pltpu.SemaphoreType.DMA, pltpu.SemaphoreType.DMA((2 + len(across),))],
        ),
        compiler_params=pltpu.CompilerParams(vmem_limit_bytes=32 << 20),
        cost_estimate=SMALL,
        name="main_update",
    )(info, pivots, slab, total, other, own, near, *across, upper, terms)


def last_kernel(first_row, block, tile, segments, base, *refs):
    out, result, sem = refs[-3:]
    at = 0
    for count, groups in segments:
        for inner in range(0, count, tile):
            size = min(tile, count - inner)
            part = pl.ds(at, size)
            row = first_row + at
            delta = None
            for terms, pieces in groups:
                left = sum(refs[piece][pl.ds(offset + inner, size), :] for piece, offset in pieces)
                change = dot(left_terms(left), refs[terms][...])
                delta = change if delta is None else delta + change
            if row < block:
                delta = jnp.where(lax.axis_index("prow") == 0, 0.0, delta)
            result[part, :] = base[pl.ds(row, size), :] - delta
            pltpu.make_async_copy(result.at[part, :], out.at[pl.ds(row, size), :], sem).start()
            at += size
    pltpu.make_async_copy(result, out.at[pl.ds(first_row, at), :], sem).wait()


def last_update(base, arrays, segments, block, first_row, done):
    count = sum(size for size, _ in segments)
    return pl.pallas_call(
        lambda *refs: last_kernel(first_row, block, min(LAST_TILE, block), segments, *refs),
        out_shape=jax.ShapeDtypeStruct(base.shape, base.dtype),
        in_specs=[VMEM] * (1 + len(arrays)) + [HBM] * len(done),
        out_specs=HBM,
        scratch_shapes=[pltpu.VMEM((count, base.shape[1]), base.dtype), pltpu.SemaphoreType.DMA],
        input_output_aliases={1 + len(arrays): 0} if done else {},
        compiler_params=pltpu.CompilerParams(vmem_limit_bytes=24 << 20),
        cost_estimate=SMALL,
        name="last_update",
    )(base, *arrays, *done)


def exchange(value, bit, count):
    return lax.ppermute(value, "prow", [(i, i ^ (1 << bit)) for i in range(count)])


def on_rows(value, rows, pairs):
    return lax.ppermute(
        value, ("prow", "pcol"), [(4 * row + a, 4 * row + b) for row in rows for a, b in pairs]
    )


def solution(mesh):
    row_parts, column_parts = mesh.shape["prow"], mesh.shape["pcol"]
    bits = row_parts.bit_length() - 1
    if column_parts != 4 or row_parts != 1 << bits or bits < 1:
        raise ValueError("unsupported mesh")

    def shards(panel, slab, pivots, diag_inverse):
        rows_here = slab.shape[0]
        width = panel.shape[1]
        block = diag_inverse.shape[0]
        place = lax.axis_index("prow")
        column = lax.axis_index("pcol")
        info = jnp.stack([column, place]).astype(jnp.int32)

        first, second, last = (rows_here * part // sum(PIECES) for part in PIECES)
        first_mid, second_mid, _ = (rows_here * part // sum(PIECES) for part in MIDDLE_PIECES)
        early = first + second
        if second > block or second % min(LAST_TILE, block):
            raise ValueError("unsupported sizes")
        below = [row for row in range(row_parts) if row]
        near = lax.ppermute(panel, "pcol", SWAP)
        pieces = cut(panel, [(second, first), (0, second)])
        across = [lax.ppermute(pieces[0], "pcol", ACROSS), on_rows(pieces[1], below, ACROSS)]
        tail = panel[early:]
        tail_mid = lax.ppermute(tail, "pcol", MIDDLE)

        def gather_rows(slab, pivots):
            send, keep = pick(info, pivots, slab, block)
            total = keep + exchange(send, 0, row_parts)
            halves = [total[: block // 2], total[block // 2 :]]
            orders = [list(range(1, bits)), list(range(1, bits))[::-1]]
            for step in range(bits - 1):
                other = [exchange(half, order[step], row_parts) for half, order in zip(halves, orders)]
                halves = [half + part for half, part in zip(halves, other)]
            total = jnp.concatenate(halves, axis=0)
            return total, exchange(total, 0, row_parts)

        def no_rows(slab, pivots):
            return slab[:block], slab[:block]

        total, other = lax.cond(pivots[0] >= 0, gather_rows, no_rows, slab, pivots)
        tail, total = lax.optimization_barrier((tail, total))
        far = lax.ppermute(tail, "pcol", FAR)
        head, total = lax.optimization_barrier((across[0], total))
        upper, terms, across_terms, last_terms = make_upper(info, total, other, diag_inverse, width)
        later, upper = lax.optimization_barrier((panel, upper))
        head_mid, rest_mid = load_pieces(later, [(second_mid, first_mid), (0, second_mid)])
        head_end = lax.ppermute(head, "pcol", ENDS)
        rest, head_mid, near = lax.optimization_barrier((across[1], head_mid, near))
        rest_mid, far, near = lax.optimization_barrier((rest_mid, far, near))
        head_mid = lax.ppermute(head_mid, "pcol", MIDDLE)
        rest_mid = lax.ppermute(rest_mid, "pcol", MIDDLE)
        rest_end = on_rows(rest, below, ENDS)
        both, rest = lax.optimization_barrier((jnp.concatenate([far, tail_mid], axis=0), rest))
        both = lax.ppermute(both, "pcol", ENDS)

        base = main_update(info, pivots, slab, total, other, panel, near, [rest, head], upper, terms)
        segments = [(first_mid, [(0, [(1, second_mid - second), (2, 0)])])]
        arrays = [last_terms, head_end, head_mid]
        result = last_update(base, arrays, segments, block, second_mid, [])
        segments = [(last, [(0, [(2, 0), (4, last)]), (1, [(3, 0), (4, 0)])])]
        arrays = [across_terms, last_terms, far, tail_mid, both]
        result = last_update(base, arrays, segments, block, early, [result])
        segments = [
            (second_mid - second, [(0, [(1, 0), (3, second)])]),
            (second, [(0, [(2, 0), (3, 0)])]),
        ]
        arrays = [last_terms, head_end, rest_end, rest_mid]
        return last_update(base, arrays, segments[::-1], block, 0, [result])

    in_specs = (P("prow", "pcol"), P("prow", "pcol"), P(), P())
    return jax.shard_map(
        shards, mesh=mesh, in_specs=in_specs, out_specs=P("prow", "pcol"), check_vma=False
    )
```
